32 devices in a mesh: rows: 16 (over z, x, core), mlp: 2 (over y).
Axes of the slice: x: 2, y: 2, z: 4, core: 2. Of those that a mesh axis runs over, the one named last changes fastest.
Arguments:
- node_rows: bfloat16 [16384, 512], P(('rows', 'mlp')), may hold values from -6 to 6
- noise_cond: bfloat16 [8, 128], replicated, may hold values from -6 to 6
- sample_id: int32 [16384], P(('rows', 'mlp')), may hold values from 0 to 7, as said below
- neighbours: int32 [16384, 16], P(('rows', 'mlp')), may hold values from 0 to 16383, as said below
- ada_weight: bfloat16 [128, 2048], replicated, may hold values from -0.25 to 0.25
- ada_bias: bfloat16 [2048], replicated, may hold values from -3 to 3
- query_weight: bfloat16 [512, 512], replicated, may hold values from -0.25 to 0.25
- keyval_weight: bfloat16 [512, 1024], replicated, may hold values from -0.25 to 0.25
- out_weight: bfloat16 [512, 512], replicated, may hold values from -0.5 to 0.5
- up_weight: bfloat16 [512, 2048], P(None, 'mlp'), may hold values from -0.25 to 0.25
- up_bias: bfloat16 [2048], P('mlp'), may hold values from -3 to 3
- down_weight: bfloat16 [2048, 512], P('mlp'), may hold values from -0.125 to 0.125
- down_bias: bfloat16 [512], replicated, may hold values from -3 to 3
- cotangent: bfloat16 [16384, 512], P(('rows', 'mlp')), may hold values from -6 to 6
Outputs:
- layer_out: bfloat16 [16384, 512], P(('rows', 'mlp'))
- grad_rows: float32 [16384, 512], P(('rows', 'mlp'))
- grad_cond: float32 [8, 128], replicated
- grad_ada_weight: float32 [128, 2048], replicated
- grad_ada_bias: float32 [2048], replicated
- grad_query_weight: float32 [512, 512], replicated
- grad_keyval_weight: float32 [512, 1024], replicated
- grad_out_weight: float32 [512, 512], replicated
- grad_up_weight: float32 [512, 2048], P(None, 'mlp')
- grad_up_bias: float32 [2048], P('mlp')
- grad_down_weight: float32 [2048, 512], P('mlp')
- grad_down_bias: float32 [512], replicated
The draws below stay inside these ranges and needn't reach their ends.
Inputs may be any that keep to these rules, and one draw needn't show every extreme that they name: Row n stands for mesh node n // 8 of sample sample_id[n]. Each of its 16 neighbours is a row of the same sample whose node differs by at most 64, counted cyclically over the 2048 nodes; so it lies within 512 positions of n, counted cyclically over 16384. The first two are the rows of nodes one below and one above, cyclically. sample_id[n] depends only on n mod 8, and each sample is carried by 2048 rows.
All inputs are finite; a program needn't handle non-finite values.
Results may differ from the reference program's by a relative error of at most 0.012.
The reference program's roundings to bfloat16 on the way count: a program that leaves them out, or rounds other values in their place, can miss the bound.
Values may be sent and summed in bfloat16 or wider, within the bound.
A program may use at most 192 MiB of HBM per device.

```python
import math
import jax
import jax.numpy as jnp
from jax import lax

D = 512
FF = 2048
HEADS = 4
HEAD_DIM = 128
NEIGH = 16
COND = 128
SAMPLES = 8
ROWS_DEV = 512
NODES = 16384
SAMPLE_ROWS = 2048


def draw_sample_id(key, part):
    order = jax.random.permutation(jax.random.fold_in(key, 2), jnp.arange(SAMPLES, dtype=jnp.int32))
    return order[jnp.arange(NODES, dtype=jnp.int32) % SAMPLES].astype(jnp.int32)


def draw_neighbours(key, part):
    reach = ROWS_DEV // SAMPLES
    row_index = jnp.arange(NODES, dtype=jnp.int32)[:, None]
    node_index = row_index // SAMPLES
    sample_slot = row_index % SAMPLES
    offsets = jax.random.randint(jax.random.fold_in(key, 1), (NODES, NEIGH - 2), -reach, reach + 1, dtype=jnp.int32)
    steps_all = jnp.concatenate([jnp.full((NODES, 1), -1, jnp.int32), jnp.full((NODES, 1), 1, jnp.int32), offsets], axis=1)
    target_node = jnp.mod(node_index + steps_all, SAMPLE_ROWS)
    return (target_node * SAMPLES + sample_slot).astype(jnp.int32)


def shard_levels(stream_key, extent, pieces, low, top_value):
    loudness, own = 1.0, jax.random.fold_in(stream_key, 6)
    for axis_at, shards_of in pieces:
        draws = jnp.exp(jax.random.uniform(jax.random.fold_in(own, axis_at), (shards_of,), jnp.float32, low / len(pieces), top_value / len(pieces)))
        loudness = loudness * jnp.repeat(draws, extent[axis_at] // shards_of).reshape([-1 if axis == axis_at else 1 for axis in range(len(extent))])
    return loudness


def bell_draw(own_key, dims, width, most, cuts=(), held_as=jnp.bfloat16):
    values = width * jax.random.normal(own_key, dims, jnp.float32)
    if cuts:
        values = values * shard_levels(own_key, dims, cuts, -0.22, 0.18)
    return jnp.clip(values, -most, most).astype(held_as)


def setup_inputs(seed: int = 0) -> dict:
    streams_of = jax.random.split(jax.random.key(seed), 15)
    return {
        "node_rows": bell_draw(streams_of[0], (NODES, D), 1.0, 6.0, ((0, 32),)),
        "noise_cond": bell_draw(streams_of[1], (SAMPLES, COND), 1.0, 6.0),
        "sample_id": draw_sample_id(jax.random.fold_in(streams_of[14], 71), 0),
        "neighbours": draw_neighbours(jax.random.fold_in(streams_of[14], 71), 0),
        "ada_weight": bell_draw(streams_of[4], (COND, 4 * D), (4 * COND) ** -0.5, 0.25),
        "ada_bias": bell_draw(streams_of[5], (4 * D,), 0.5, 3.0),
        "query_weight": bell_draw(streams_of[6], (D, D), D ** -0.5, 0.25),
        "keyval_weight": bell_draw(streams_of[7], (D, 2 * D), D ** -0.5, 0.25),
        "out_weight": bell_draw(streams_of[8], (D, D), (D // 4) ** -0.5, 0.5),
        "up_weight": bell_draw(streams_of[9], (D, FF), D ** -0.5, 0.25, ((1, 2),)),
        "up_bias": bell_draw(streams_of[10], (FF,), 0.5, 3.0, ((0, 2),)),
        "down_weight": bell_draw(streams_of[11], (FF, D), FF ** -0.5, 0.125, ((0, 2),)),
        "down_bias": bell_draw(streams_of[12], (D,), 0.5, 3.0),
        "cotangent": bell_draw(streams_of[13], (NODES, D), 1.0, 6.0, ((0, 32),)),
    }


EPSILON = 1e-05
PRECISE = lax.Precision.HIGHEST

@jax.custom_vjp
def low(v):
    return lax.optimization_barrier(v.astype(jnp.bfloat16)).astype(jnp.float32)

@jax.custom_vjp
def low_back(v):
    return v

def low_keep(v):
    return (low(v), None)

def low_pass(kept, grad):
    return (grad,)

def back_keep(v):
    return (v, None)

def back_low(kept, grad):
    return (low(grad),)
low.defvjp(low_keep, low_pass)
low_back.defvjp(back_keep, back_low)

def matmul(left_operand, right_operand):
    return jnp.dot(left_operand, right_operand, precision=PRECISE, preferred_element_type=jnp.float32)

def ada_norm(values, modrows, offset):
    centred = values - lax.optimization_barrier(jnp.mean(values, axis=-1, keepdims=True))
    spread = lax.optimization_barrier(jnp.mean(centred * centred, axis=-1, keepdims=True))
    normed = centred * lax.rsqrt(spread + EPSILON)
    return normed * (1.0 + modrows[:, offset:offset + D]) + modrows[:, offset + D:offset + 2 * D]

def reference(node_rows, noise_cond, sample_id, neighbours, ada_weight, ada_bias, query_weight, keyval_weight, out_weight, up_weight, up_bias, down_weight, down_bias, cotangent):
    block_rows = min(4096, NODES)
    blocks = NODES // block_rows
    factor = 1.0 / math.sqrt(HEAD_DIM)
    sample_blocks = sample_id.reshape(blocks, block_rows)
    neighbour_blocks = neighbours.reshape(blocks, block_rows, NEIGH)

    def forward(inputs, cond_vec, ada_mat, ada_vec, query_mat, keyval_mat, out_mat, up_mat, up_vec, down_mat, down_vec):
        modulation = matmul(cond_vec, ada_mat) + ada_vec

        def first_norm(norm_items):
            return low(ada_norm(norm_items[0], modulation[norm_items[1]], 0))
        normed_one = lax.map(jax.checkpoint(first_norm), (inputs.reshape(blocks, block_rows, D), sample_blocks)).reshape(NODES, D)
        keyval_all = low_back(low(matmul(normed_one, keyval_mat)))

        def layer_block(block_items):
            rows_in, sample_rows, neighbour_rows, normed_rows = block_items
            modrows = modulation[sample_rows]
            queries = low_back(low(matmul(normed_rows, query_mat))).reshape(block_rows, HEADS, HEAD_DIM)
            picked = keyval_all[neighbour_rows]
            keys_near = picked[:, :, :D].reshape(block_rows, NEIGH, HEADS, HEAD_DIM)
            values_near = picked[:, :, D:].reshape(block_rows, NEIGH, HEADS, HEAD_DIM)
            scores = low_back(jnp.einsum('bhe,bjhe->bhj', queries, keys_near, precision=PRECISE) * factor)
            highest = lax.optimization_barrier(jnp.max(scores, axis=-1, keepdims=True))
            exponent = jnp.exp(scores - highest)
            attn_probs = exponent / lax.optimization_barrier(jnp.sum(exponent, axis=-1, keepdims=True))
            mixture = jnp.einsum('bhj,bjhe->bhe', low(attn_probs), values_near, precision=PRECISE).reshape(block_rows, D)
            attended = low_back(matmul(low_back(low(mixture)), out_mat))
            middle = rows_in + attended
            normed_two = low(ada_norm(middle, modrows, 2 * D))
            hidden = low_back(matmul(normed_two, up_mat) + up_vec)
            active = low(jax.nn.silu(hidden))
            return middle + matmul(active, down_mat) + down_vec
        result = lax.map(jax.checkpoint(layer_block), (inputs.reshape(blocks, block_rows, D), sample_blocks, neighbour_blocks, normed_one.reshape(blocks, block_rows, D)))
        return result.reshape(NODES, D)
    floats = (node_rows.astype(jnp.float32), noise_cond.astype(jnp.float32), ada_weight.astype(jnp.float32), ada_bias.astype(jnp.float32), query_weight.astype(jnp.float32), keyval_weight.astype(jnp.float32), out_weight.astype(jnp.float32), up_weight.astype(jnp.float32), up_bias.astype(jnp.float32), down_weight.astype(jnp.float32), down_bias.astype(jnp.float32))
    layer_out, pullback = jax.vjp(forward, *floats)
    gradients = pullback(cotangent.astype(jnp.float32))
    return (layer_out.astype(jnp.bfloat16), gradients[0], gradients[1], gradients[2], gradients[3], gradients[4], gradients[5], gradients[6], gradients[7], gradients[8], gradients[9], gradients[10])
```

```python
import functools
import math
from types import SimpleNamespace

import jax
import jax.numpy as jnp
from jax import lax
from jax.experimental import pallas as pl
from jax.experimental.pallas import tpu as pltpu
from jax.sharding import PartitionSpec as P

HEADS = 4
EPSILON = 1e-05
MESH = pl.DeviceIdType.MESH
F32, BF = jnp.float32, jnp.bfloat16
PRECISE = lax.Precision.HIGHEST
NN = (((1,), (0,)), ((), ()))
NT = (((1,), (1,)), ((), ()))
TN = (((0,), (0,)), ((), ()))
MASKED = -1e30


def dot(a, b, dims=NN, precision=None):
    return lax.dot_general(a, b, dims, precision=precision, preferred_element_type=F32)


def mean(v):
    return jnp.mean(v, axis=-1, keepdims=True)


def layer_norm(values):
    centred = values - mean(values)
    inverse = lax.rsqrt(mean(centred * centred) + EPSILON)
    return centred * inverse, inverse


def norm_back(grad, normed, inverse):
    return inverse * (grad - mean(grad) - normed * mean(grad * normed))


def iota(shape, axis):
    return lax.broadcasted_iota(jnp.int32, shape, axis)


def loop(count, body):
    lax.fori_loop(0, count, lambda i, c: (body(i), c)[1], 0)


def remote(src, dst, sems, index, device):
    send, recv = sems
    return pltpu.make_async_remote_copy(
        src_ref=src,
        dst_ref=dst,
        send_sem=send.at[index],
        recv_sem=recv.at[index],
        device_id=device,
        device_id_type=MESH,
    )


class Sum:
    def __init__(self, out, dtype, bufs, sems, base, place, over_mlp):
        self.part, self.out, self.dtype, self.bufs = bufs.part, out, dtype, bufs
        self.sems, self.base, self.over_mlp = sems, base, over_mlp
        self.r, self.m, self.M, self.core, self.x, self.z, self.nz = place
        self.rows, cols = out.shape
        self.half = self.rows // 2
        self.piece = self.half // self.nz
        self.width = cols // 2
        self.mine = pl.ds(pl.multiple_of(self.core * self.width, self.width), self.width)
        self.other = pl.ds(pl.multiple_of((1 - self.core) * self.width, self.width), self.width)
        self.sent = []

    def row(self, z, x, core):
        return z * 4 + x * 2 + core

    def copy(self, src, dst, slot, row, m):
        c = remote(src, dst, self.sems, self.base + slot, (row, m))
        c.start()
        if slot > 0:
            self.sent.append(c)
        return c

    def cut(self, start, size):
        return pl.ds(pl.multiple_of(start, size), size)

    def core_send(self):
        b = self.bufs
        self.c_core = self.copy(b.cs, b.cr, 0, self.row(self.z, self.x, 1 - self.core), self.m)

    def x_send(self):
        b = self.bufs
        self.c_core.wait()
        rows = self.cut((1 - self.x) * self.half, self.half)
        stage = b.cs.at[0 : self.half]
        stage[...] = (self.part[rows, :] + b.cr[rows, :].astype(F32)).astype(self.dtype)
        self.c_x = self.copy(stage, b.xr, 1, self.row(self.z, 1 - self.x, self.core), self.m)

    def z_send(self):
        b = self.bufs
        self.c_x.wait_recv()
        rows = self.cut(self.x * self.half, self.half)
        value = self.part[rows, :] + b.cr[rows, :].astype(F32) + b.xr[...].astype(F32)
        self.part[rows, :] = value
        stage = b.cs.at[self.half :]
        stage[...] = value.astype(self.dtype)
        self.c_z = []
        for t in range(1, self.nz):
            to = lax.rem(self.z + t, self.nz)
            self.c_z.append(
                self.copy(
                    b.cs.at[self.cut(self.half + to * self.piece, self.piece)],
                    b.zr.at[t - 1],
                    1 + t,
                    self.row(to, self.x, self.core),
                    self.m,
                )
            )

    def z_sum(self):
        b = self.bufs
        value = self.part[self.cut(self.x * self.half + self.z * self.piece, self.piece), :]
        for t in range(1, self.nz):
            self.c_z[t - 1].wait_recv()
            value = value + b.zr[t - 1].astype(F32)
        return value

    def m_send(self):
        b = self.bufs
        b.mr[self.m] = self.z_sum().astype(self.dtype)
        self.c_m = []
        for t in range(1, self.M):
            self.c_m.append(
                self.copy(
                    b.mr.at[self.m],
                    b.mr.at[self.m],
                    self.nz + t,
                    self.r,
                    lax.rem(self.m + t, self.M),
                )
            )

    def z_gather(self):
        b = self.bufs
        if self.over_mlp:
            for c in self.c_m:
                c.wait_recv()
            value = b.mr[0].astype(F32)
            for t in range(1, self.M):
                value = value + b.mr[t].astype(F32)
        else:
            value = self.z_sum()
        here = (self.cut(self.x * self.half + self.z * self.piece, self.piece), self.mine)
        self.out[here[0], here[1]] = value.astype(self.dtype)
        block = self.out.at[here[0], here[1]]
        first = self.nz + self.M
        self.c_gz = []
        for t in range(1, self.nz):
            to = lax.rem(self.z + t, self.nz)
            self.c_gz.append(
                self.copy(block, block, first + t - 1, self.row(to, self.x, self.core), self.m)
            )

    def x_gather(self):
        for c in self.c_gz:
            c.wait_recv()
        block = self.out.at[self.cut(self.x * self.half, self.half), self.mine]
        slot = 2 * self.nz + self.M - 1
        self.c_gx = self.copy(block, block, slot, self.row(self.z, 1 - self.x, self.core), self.m)

    def core_gather(self):
        self.c_gx.wait_recv()
        block = self.out.at[:, self.mine]
        slot = 2 * self.nz + self.M
        self.c_gc = self.copy(block, block, slot, self.row(self.z, self.x, 1 - self.core), self.m)

    def finish(self):
        self.c_gc.wait_recv()
        for c in self.sent:
            c.wait_send()

    @staticmethod
    def slots(nz, m):
        return 2 * nz + m + 1


SUMS = ("up", "down", "out", "query", "keyval", "tail")
BUFFERS = ("part", "cs", "cr", "xr", "zr", "mr")


def kernel(static, names, *refs):
    ref = SimpleNamespace(**dict(zip(names, refs)))
    R, M, rows, D, F, S, near = static
    nz = R // 4
    G = rows // S
    W = 3 * G
    head = D // HEADS
    factor = 1.0 / math.sqrt(head)
    r, y = lax.axis_index("rows"), lax.axis_index("mlp")
    core, xi, z = lax.rem(r, 2), lax.rem(r // 2, 2), r // 4
    me = r * M + y
    devices = R * M
    pairs = M == 2
    up_row, down_row = lax.rem(r + 1, R), lax.rem(r + R - 1, R)
    after, before = lax.rem(me + 1, devices), lax.rem(me + devices - 1, devices)

    local = []
    lsem = ref.lsem
    for i, (src, dst) in enumerate(
        (
            (ref.x, ref.xb.at[1]),
            (ref.wq, ref.wqkv.at[:, 0:D]),
            (ref.wkv, ref.wqkv.at[:, D : 3 * D]),
            (ref.cot, ref.cotn),
            (ref.wo, ref.wob),
            (ref.wup, ref.wupb),
            (ref.wdn, ref.wdnb),
        )
    ):
        c = pltpu.make_async_copy(src, dst, lsem.at[i])
        c.start()
        local.append(c)

    barrier = pltpu.get_barrier_semaphore()
    others = [(r, lax.rem(y + t, M)) for t in range(1, M)]
    others.append((z * 4 + xi * 2 + 1 - core, y))
    others.append((z * 4 + (1 - xi) * 2 + core, y))
    for t in range(1, nz):
        others.append((lax.rem(z + t, nz) * 4 + xi * 2 + core, y))
    if pairs:
        others += [(up_row, y), (down_row, y)]
    else:
        others += [(after // M, lax.rem(after, M)), (before // M, lax.rem(before, M))]
    for device in others:
        pl.semaphore_signal(barrier, inc=1, device_id=device, device_id_type=MESH)
    pl.semaphore_wait(barrier, len(others))

    def halo(source, at, sems):
        def first(k):
            if pairs:
                return [remote(source(k), at(2 * y, k), sems, (0, k), (r, 1 - y))]
            return [
                remote(source(k), at(0, k), sems, (0, k), (after // M, lax.rem(after, M))),
                remote(source(k), at(2, k), sems, (1, k), (before // M, lax.rem(before, M))),
            ]

        def second(k):
            if pairs:
                to = jnp.where(y == 0, up_row, down_row)
                return remote(at(2 * (1 - y), k), at(2 * y, k), sems, (1, k), (to, y))
            return first(k)[1]

        def send(k):
            for c in first(k):
                c.start()

        def pass_on(k):
            first(k)[0].wait_recv()
            if pairs:
                second(k).start()

        def arrive(k):
            second(k).wait_recv()

        def drain(k):
            first(k)[0].wait_send()
            second(k).wait_send()

        return send, pass_on, arrive, drain

    near_slot = 2 * (1 - y) if pairs else 0
    far_slot = 2 * y if pairs else 2
    xb = ref.xb
    quarter = rows // 4

    def part(k, n=quarter):
        return pl.ds(pl.multiple_of(k * n, n), n)

    x_send, x_pass, x_arrive, x_drain = halo(
        lambda k: ref.x.at[part(k)], lambda slot, k: xb.at[slot, part(k)], ref.xsem
    )
    loop(4, x_send)

    def build(k):
        at = part(k)
        a, b = iota((quarter, rows), 0) + k * quarter, iota((quarter, rows), 1)
        ref.pm[at, :] = jnp.where(b == lax.rem(a, G) * S + a // G, 1.0, 0.0).astype(BF)
        ref.pt[at, :] = jnp.where(a == lax.rem(b, G) * S + b // G, 1.0, 0.0).astype(BF)

    loop(4, build)
    pm, pt = ref.pm, ref.pt

    nodes = devices * G
    place = ref.nbr[...] // S - me * G + G
    place = jnp.where(place < 0, place + nodes, place)
    place = jnp.where(place >= nodes, place - nodes, place)
    place = place.astype(F32).astype(BF)
    lws = ref.lws
    lws[rows : rows + G, :] = jnp.zeros((G, near), F32)
    lws[0:rows, :] = dot(pm[...], place)
    lwt = ref.lwt
    eye = jnp.where(iota((near, near), 0) == iota((near, near), 1), 1.0, 0.0).astype(BF)

    def turn(s):
        block = lws[pl.ds(pl.multiple_of(s * G, G), 2 * G), :].astype(BF)
        lwt[1, s] = dot(eye, block, NT).astype(BF)

    loop(S, turn)
    l_send, l_pass, l_arrive, l_drain = halo(
        lambda k: lwt.at[1], lambda slot, k: lwt.at[slot], ref.lwsem
    )
    l_send(0)

    modulation = dot(ref.nc[...], ref.adaw[...]) + ref.adab[...].astype(F32)
    ref.mod[...] = modulation
    mods = ref.mods
    for s in range(S):
        mods[s : s + 1, :] = ref.mod[pl.ds(ref.sid[s], 1), :]

    n1n, n1s, qkv = ref.n1n, ref.n1s, ref.qkv
    wqkv = ref.wqkv

    def norm_block(slot, k):
        at = part(k)
        normed, _ = layer_norm(xb[slot, at, :].astype(F32))
        scaled = normed.reshape(quarter // S, S, D) * (1.0 + mods[:, 0:D])[None]
        scaled = scaled + mods[:, D : 2 * D][None]
        n1n[at, :] = scaled.reshape(quarter, D).astype(BF)

    def project(slot, k):
        ordered = dot(pm[part(k), :], n1n[...]).astype(BF)
        wide = dot(ordered, wqkv[...]).astype(BF)
        two = quarter // G
        qkv[pl.ds(two * k, two), pl.ds(pl.multiple_of(slot * G, G), G), :] = wide.reshape(
            two, G, 3 * D
        )
        return ordered

    local[0].wait()
    loop(4, lambda k: norm_block(1, k))
    local[1].wait()
    local[2].wait()

    def own_project(k):
        n1s[part(k), :] = project(1, k)

    loop(4, own_project)
    local[3].wait()
    xs, cotb = ref.xs, ref.cotb

    def order(k):
        xs[part(k), :] = dot(pm[part(k), :], xb[1]).astype(BF)
        cotb[y, part(k), :] = dot(pm[part(k), :], ref.cotn[...]).astype(BF)

    loop(4, order)

    cnt, cntt = ref.cnt, ref.cntt

    def count(s):
        block = lws[pl.ds(pl.multiple_of(s * G, G), G), :].astype(jnp.int32)
        lane = iota((G, W), 1)
        total = jnp.zeros((G, W), F32)
        for j in range(near):
            total = total + jnp.where(block[:, j : j + 1] == lane, 1.0, 0.0)
        cnt[s] = total

    loop(S, count)

    def near_norm(k):
        x_pass(k)
        norm_block(near_slot, k)

    loop(4, near_norm)
    l_pass(0)

    half = rows // 2

    def mlp_copies(buf, sems, k, n):
        block = buf.at[y, part(k, n)]
        return [
            remote(block, block, sems, (t - 1, k), (r, lax.rem(y + t, M))) for t in range(1, M)
        ]

    def start_all(copies):
        for c in copies:
            c.start()

    loop(2, lambda k: start_all(mlp_copies(cotb, ref.cotsem, k, half)))
    loop(4, lambda k: project(near_slot, k))

    def far_norm(k):
        x_arrive(k)
        norm_block(far_slot, k)

    loop(4, far_norm)
    l_arrive(0)
    loop(4, lambda k: project(far_slot, k))

    mixs, mixx, prob, lsec = ref.mixs, ref.mixx, ref.prob, ref.lsec
    ntb, mid = ref.ntb, ref.mid
    local[4].wait()
    wo = ref.wob

    def attend(k):
        def sample(s2):
            s = 2 * k + s2
            at = pl.ds(pl.multiple_of(s * G, G), G)
            times = cnt[s]
            lane = iota((G, 128), 1)
            logs = jnp.zeros((G, 128), F32)
            for h in range(HEADS):
                lo, hi = h * head, (h + 1) * head
                scores = dot(qkv[s, G : 2 * G, lo:hi], qkv[s, :, D + lo : D + hi], NT) * factor
                scores = jnp.where(times > 0.0, scores, MASKED)
                top = jnp.max(scores, axis=-1, keepdims=True)
                power = jnp.exp(scores - top)
                total = jnp.sum(power * times, axis=-1, keepdims=True)
                probs = power * (1.0 / total)
                prob[s * HEADS + h] = probs
                weight = (times * probs.astype(BF).astype(F32)).astype(BF)
                rest = (times * probs - weight.astype(F32)).astype(BF)
                values = qkv[s, :, 2 * D + lo : 2 * D + hi]
                mixed = dot(weight, values)
                mixs[at, lo:hi] = mixed.astype(BF)
                mixx[at, lo:hi] = mixed + dot(rest, values)
                logs = jnp.where(lane == h, top + jnp.log(total), logs)
            lsec[at, :] = logs

        loop(2, sample)
        middle = xs[part(k), :].astype(F32) + dot(mixs[part(k), :], wo[...])
        mid[part(k), :] = middle
        normed, _ = layer_norm(middle)
        for s2 in range(2):
            at = pl.ds(pl.multiple_of(k * quarter + s2 * G, G), G)
            scale = mods[pl.ds(2 * k + s2, 1), 2 * D : 3 * D]
            shift = mods[pl.ds(2 * k + s2, 1), 3 * D : 4 * D]
            ntb[y, at, :] = (normed[s2 * G : (s2 + 1) * G] * (1.0 + scale) + shift).astype(BF)
        start_all(mlp_copies(ntb, ref.ntsem, k, quarter))

    loop(4, attend)

    local[5].wait()
    local[6].wait()
    wup, wdn, actb, ghb = ref.wupb, ref.wdnb, ref.actb, ref.ghb
    bupg, g2s, g2r, g2o = ref.bupg, ref.g2s, ref.g2r, ref.g2o
    brr = ref.brr
    bupg[...] = jnp.zeros_like(bupg)
    tile = 256

    def back_copy(src, dst, sems, j, c):
        owner = lax.rem(y + 2 * M - 1 - j, M)
        return remote(src.at[j, part(c, half)], dst.at[j, part(c, half)], sems, (j, c), (r, owner))

    def feed(i):
        j, c = i // 2, lax.rem(i, 2)
        slot = lax.rem(y + 2 * M - 1 - j, M)
        away = j < M - 1

        @pl.when(away)
        def _():
            for q in range(2):
                k = 2 * c + q
                block = ntb.at[slot, part(k)]
                remote(block, block, ref.ntsem, (j, k), (r, y)).wait_recv()
            block = cotb.at[slot, part(c, half)]
            remote(block, block, ref.cotsem, (j, c), (r, y)).wait_recv()

        at = part(c, half)
        flat = pl.ds(pl.multiple_of(slot * rows + c * half, half), half)

        def column(f):
            cols = part(f, tile)
            hidden = dot(ntb[slot, at, :], wup[:, cols]) + ref.bup[:, cols].astype(F32)
            gate = jax.nn.sigmoid(hidden)
            actb[flat, cols] = (hidden * gate).astype(BF)
            grad = dot(cotb[slot, at, :], wdn[cols, :], NT)
            grad = (grad * gate * (1.0 + hidden * (1.0 - gate))).astype(BF)
            ghb[flat, cols] = grad
            bupg[:, cols] += jnp.sum(grad.astype(F32), axis=0, keepdims=True)

        loop(F // tile, column)
        for q in range(D // tile):
            lo, hi = q * tile, (q + 1) * tile
            two = dot(ghb[flat, :], wup[lo:hi, :], NT)

            @pl.when(away)
            def _():
                jj = jnp.minimum(j, M - 2)
                g2s[jj, at, lo:hi] = two.astype(BF)

            @pl.when(jnp.logical_not(away))
            def _():
                g2o[at, lo:hi] = two

        @pl.when(away)
        def _():
            back_copy(g2s, g2r, ref.g2sem, j, c).start()

    loop(2 * M, feed)

    place_of = (r, y, M, core, xi, z, nz)
    count_of = Sum.slots(nz, M)
    sums = SimpleNamespace()
    targets = (ref.o_up, ref.o_dn, ref.o_out, ref.o_q, ref.o_kv, ref.tailo)
    for i, (name, out, bufs) in enumerate(zip(SUMS, targets, ref.sums)):
        bufs = SimpleNamespace(**dict(zip(BUFFERS, bufs)))
        dtype = F32 if out is ref.tailo else BF
        total = Sum(out, dtype, bufs, ref.sumsem, i * count_of, place_of, i > 1)
        setattr(sums, name, total)

    def weight_grad(total, left, right):
        rows_of, width = total.rows, total.width
        step = min(tile, width)
        for out, start, kind in (
            (total.bufs.cs, (1 - core) * width, BF),
            (total.part, core * width, F32),
        ):

            def tile_row(a):
                lhs = left(a)

                def column(f):
                    at = pl.ds(pl.multiple_of(start + f * step, step), step)
                    out[part(a, tile), part(f, step)] = dot(lhs, right(at), TN).astype(kind)

                loop(width // step, column)

            loop(rows_of // tile, tile_row)
            if kind == BF:
                total.core_send()

    weight_grad(
        sums.up,
        lambda a: ntb[:, :, part(a, tile)].reshape(M * rows, tile),
        lambda at: ghb[:, at],
    )
    weight_grad(
        sums.down,
        lambda a: actb[:, part(a, tile)],
        lambda at: cotb[:, :, at].reshape(M * rows, at.size),
    )

    gmid, gmw, stw, gatt, gmod = ref.gmid, ref.gmw, ref.stw, ref.cotn, ref.gmod
    pick_log = jnp.where(
        (iota((8, 128), 0) == iota((8, 128), 1)) & (iota((8, 128), 0) < HEADS), 1.0, 0.0
    )
    pick_head = jnp.where(iota((8, D), 0) == iota((8, D), 1) // head + HEADS, 1.0, 0.0)
    m_send, m_pass, m_arrive, m_drain = halo(
        lambda k: gmw.at[pl.ds(2 * k, 2), pl.ds(G, G)],
        lambda slot, k: gmw.at[pl.ds(2 * k, 2), pl.ds(pl.multiple_of(slot * G, G), G)],
        ref.gmsem,
    )
    s_send, s_pass, s_arrive, s_drain = halo(
        lambda k: stw.at[1, pl.ds(2 * k, 2)],
        lambda slot, k: stw.at[slot, pl.ds(2 * k, 2)],
        ref.stsem,
    )

    def middle_back(k):
        @pl.when(lax.rem(k, 2) == 0)
        def _():
            for j in range(M - 1):
                back_copy(g2s, g2r, ref.g2sem, j, k // 2).wait_recv()

        at = part(k)
        grad = g2o[at, :]
        for j in range(M - 1):
            grad = grad + g2r[j, at, :].astype(F32)
        normed, inverse = layer_norm(mid[at, :])
        weighted = []
        for s2 in range(2):
            s = 2 * k + s2
            lo, hi = s2 * G, (s2 + 1) * G
            scale = mods[pl.ds(s, 1), 2 * D : 3 * D]
            weighted.append(grad[lo:hi] * (1.0 + scale))
            gmod[pl.ds(s, 1), 2 * D : 3 * D] = jnp.sum(
                grad[lo:hi] * normed[lo:hi], axis=0, keepdims=True
            )
            gmod[pl.ds(s, 1), 3 * D : 4 * D] = jnp.sum(grad[lo:hi], axis=0, keepdims=True)
        weighted = jnp.concatenate(weighted, axis=0)
        middle = cotb[y, at, :].astype(F32) + norm_back(weighted, normed, inverse)
        gmid[at, :] = middle
        rounded = middle.astype(BF)
        gatt[at, :] = rounded
        mixture = dot(rounded, wo[...], NT).astype(BF)
        gmw[pl.ds(2 * k, 2), G : 2 * G, :] = mixture.reshape(2, G, D)
        product = mixture.astype(F32) * mixx[at, :]
        stats = dot(pick_log, lsec[at, :], NT, PRECISE) + dot(pick_head, product, NT, PRECISE)
        stw[1, 2 * k] = stats
        stw[1, 2 * k + 1] = pltpu.roll(stats, G, 1)
        m_send(k)
        s_send(k)

    loop(4, middle_back)
    sums.up.x_send()
    sums.down.x_send()

    def branch_copy(j, c):
        owner = lax.rem(y + 2 * M - 1 - j, M)
        at = part(c, half)
        return remote(ntb.at[owner, at], brr.at[j, at], ref.brsem, (j, c), (r, owner))

    def branch(i):
        j, c = i // 2, lax.rem(i, 2)
        slot = lax.rem(y + 2 * M - 1 - j, M)
        flat = pl.ds(pl.multiple_of(slot * rows + c * half, half), half)
        for q in range(D // tile):
            lo, hi = q * tile, (q + 1) * tile
            ntb[slot, part(c, half), lo:hi] = dot(actb[flat, :], wdn[:, lo:hi]).astype(BF)
        branch_copy(j, c).start()

    loop(2 * (M - 1), branch)

    weight_grad(sums.out, lambda a: mixs[:, part(a, tile)], lambda at: gatt[:, at])

    gqkv = ref.gqkv

    def query_back(s):
        at = pl.ds(pl.multiple_of(s * G, G), G)
        times = cnt[s]
        for h in range(HEADS):
            lo, hi = h * head, (h + 1) * head
            grad = gmw[s, G : 2 * G, lo:hi]
            delta = jnp.sum(grad.astype(F32) * mixx[at, lo:hi], axis=-1, keepdims=True)
            gprob = dot(grad, qkv[s, :, 2 * D + lo : 2 * D + hi], NT)
            gscore = (prob[s * HEADS + h] * (gprob - delta)).astype(BF).astype(F32)
            weight = (times * gscore).astype(BF)
            gqkv[at, lo:hi] = (dot(weight, qkv[s, :, D + lo : D + hi]) * factor).astype(BF)

    def query_pass(s):
        query_back(s)

        @pl.when(s >= 4)
        def _():
            m_pass(s - 4)
            s_pass(s - 4)

    loop(S, query_pass)

    weight_grad(sums.query, lambda a: n1s[:, part(a, tile)], lambda at: gqkv[:, at])
    sums.out.x_send()

    def count_back(s):
        shift = [2 * G, G, 0]
        block = jnp.concatenate(
            [lwt[b, s][:, 0:G].astype(F32) - float(shift[b]) for b in range(3)], axis=1
        ).astype(jnp.int32)
        key = iota((G, W), 0)
        total = jnp.zeros((G, W), F32)
        for j in range(near):
            total = total + jnp.where(block[j : j + 1, :] == key, 1.0, 0.0)
        cntt[s] = total

    loop(S, count_back)
    sums.up.z_send()
    sums.down.z_send()

    def key_back(s):
        @pl.when(lax.rem(s, 2) == 0)
        def _():
            m_arrive(s // 2)
            s_arrive(s // 2)

        at = pl.ds(pl.multiple_of(s * G, G), G)
        times = cntt[s]
        stats = jnp.concatenate([stw[b, s][:, 0:G] for b in range(3)], axis=1)
        for h in range(HEADS):
            lo, hi = h * head, (h + 1) * head
            queries = qkv[s, :, lo:hi]
            grads = gmw[s, :, lo:hi]
            scores = dot(qkv[s, G : 2 * G, D + lo : D + hi], queries, NT) * factor
            probs = jnp.exp(jnp.where(times > 0.0, scores - stats[h : h + 1], MASKED))
            gprob = dot(qkv[s, G : 2 * G, 2 * D + lo : 2 * D + hi], grads, NT)
            gscore = probs * (gprob - stats[HEADS + h : HEADS + h + 1])
            gscore = (times * gscore.astype(BF).astype(F32)).astype(BF)
            weight = (times * probs.astype(BF).astype(F32)).astype(BF)
            gqkv[at, D + lo : D + hi] = (dot(gscore, queries) * factor).astype(BF)
            gqkv[at, 2 * D + lo : 2 * D + hi] = dot(weight, grads).astype(BF)

    loop(S, key_back)

    keyval = gqkv.at[:, D : 3 * D]
    weight_grad(sums.keyval, lambda a: n1s[:, part(a, tile)], lambda at: keyval[:, at])
    sums.query.x_send()

    gdbs = ref.gdbs
    out_rows = ref.o_rows

    def first_back(s):
        at = pl.ds(pl.multiple_of(s * G, G), G)
        grad = dot(gqkv[at, :], wqkv[...], NT)
        normed, inverse = layer_norm(xs[at, :].astype(F32))
        gmod[pl.ds(s, 1), 0:D] = jnp.sum(grad * normed, axis=0, keepdims=True)
        gmod[pl.ds(s, 1), D : 2 * D] = jnp.sum(grad, axis=0, keepdims=True)
        gdbs[pl.ds(s, 1), :] = jnp.sum(cotb[y, at, :].astype(F32), axis=0, keepdims=True)
        weighted = grad * (1.0 + mods[pl.ds(s, 1), 0:D])
        g2o[at, :] = gmid[at, :] + norm_back(weighted, normed, inverse)

    loop(S, first_back)
    sums.keyval.x_send()

    tail, tailo = ref.tail, ref.tailo
    tail[...] = jnp.zeros_like(tail)
    for c in range(4 * D // tile):
        tail[c * S : (c + 1) * S, :] = gmod[:, c * tile : (c + 1) * tile]
    base = 4 * D // tile * S
    for c in range(D // tile):
        tail[base + c * S : base + (c + 1) * S, :] = gdbs[:, c * tile : (c + 1) * tile]
    base_up = base + D // tile * S
    for c in range(F // tile):
        tail[pl.ds(base_up + y * (F // tile) + c, 1), :] = bupg[:, c * tile : (c + 1) * tile]
    sums.tail.bufs.cs[...] = tail[:, sums.tail.other]
    sums.tail.part[...] = tail[:, sums.tail.mine]
    sums.tail.core_send()
    sums.out.z_send()
    sums.query.z_send()
    sums.tail.x_send()
    sums.up.z_gather()
    sums.down.z_gather()
    sums.keyval.z_send()
    sums.tail.z_send()
    sums.out.m_send()
    sums.query.m_send()

    for c in range(D // 128):
        lo, hi = c * 128, (c + 1) * 128
        for s in range(S):
            ref.turn[c, pl.ds(s, G, stride=S), :] = g2o[s * G : (s + 1) * G, lo:hi]
        out_rows[:, lo:hi] = ref.turn[c]

    sums.keyval.m_send()
    sums.tail.m_send()
    sums.up.x_gather()
    sums.down.x_gather()
    sums.out.z_gather()
    sums.query.z_gather()
    sums.keyval.z_gather()
    sums.tail.z_gather()

    def finish_out(k):
        @pl.when(lax.rem(k, 2) == 0)
        def _():
            for j in range(M - 1):
                branch_copy(j, k // 2).wait_recv()

        at = part(k)
        flat = pl.ds(pl.multiple_of(y * rows + k * quarter, quarter), quarter)
        value = mid[at, :] + dot(actb[flat, :], wdn[...]) + ref.bdn[...].astype(F32)
        for j in range(M - 1):
            value = value + brr[j, at, :].astype(F32)
        n1n[at, :] = value.astype(BF)

    loop(4, finish_out)

    def order_back(k):
        ref.o_layer[part(k), :] = dot(pt[part(k), :], n1n[...]).astype(BF)

    loop(4, order_back)

    sums.up.core_gather()
    sums.down.core_gather()
    late = (sums.out, sums.query, sums.keyval, sums.tail)
    for total in late:
        total.x_gather()
    for total in late:
        total.core_gather()
    sums.tail.finish()

    gms = ref.gms
    pick = jnp.zeros((S, S), F32)
    for s in range(S):
        hit = (iota((S, S), 1) == s) & (iota((S, S), 0) == ref.sid[s])
        pick = pick + jnp.where(hit, 1.0, 0.0)
    for c in range(4 * D // tile):
        gms[:, c * tile : (c + 1) * tile] = dot(
            pick, tailo[c * S : (c + 1) * S, :], NN, PRECISE
        )
    total = gms[...]
    ref.o_ada[...] = dot(ref.nc[...].astype(F32), total, TN, PRECISE)
    ref.o_adab[...] = jnp.sum(total, axis=0, keepdims=True)
    ref.o_cond[...] = dot(total, ref.adaw[...].astype(F32), NT, PRECISE)
    for c in range(D // tile):
        ref.o_downb[:, c * tile : (c + 1) * tile] = jnp.sum(
            tailo[base + c * S : base + (c + 1) * S, :], axis=0, keepdims=True
        )
    for c in range(F // tile):
        ref.o_upb[:, c * tile : (c + 1) * tile] = tailo[
            pl.ds(base_up + y * (F // tile) + c, 1), :
        ]

    for total in (sums.up, sums.down, sums.out, sums.query, sums.keyval):
        total.finish()

    loop(4, x_drain)
    l_drain(0)
    loop(4, m_drain)
    loop(4, s_drain)

    def drained(copies):
        for c in copies:
            c.wait_send()

    loop(2, lambda k: drained(mlp_copies(cotb, ref.cotsem, k, half)))
    loop(4, lambda k: drained(mlp_copies(ntb, ref.ntsem, k, quarter)))
    for j in range(M - 1):
        for c in range(2):
            back_copy(g2s, g2r, ref.g2sem, j, c).wait_send()
            branch_copy(j, c).wait_send()


def shards(
    node_rows,
    noise_cond,
    sample_id,
    neighbours,
    ada_weight,
    ada_bias,
    query_weight,
    keyval_weight,
    out_weight,
    up_weight,
    up_bias,
    down_weight,
    down_bias,
    cotangent,
):
    rows, D = node_rows.shape
    F = up_weight.shape[1]
    S, cond = noise_cond.shape
    near = neighbours.shape[1]
    R, M = lax.axis_size("rows"), lax.axis_size("mlp")
    nz = R // 4
    G = rows // S
    W = 3 * G
    small = 16 * nz if 16 * nz > 88 else 128
    V, H = pltpu.VMEM, pl.ANY
    shape = jax.ShapeDtypeStruct
    arguments = dict(
        x=(node_rows, H),
        nc=(noise_cond, V),
        sid=(sample_id, pltpu.SMEM),
        nbr=(neighbours, V),
        adaw=(ada_weight, V),
        adab=(ada_bias[None], V),
        wq=(query_weight, H),
        wkv=(keyval_weight, H),
        wo=(out_weight, H),
        wup=(up_weight, H),
        bup=(up_bias[None], V),
        wdn=(down_weight, H),
        bdn=(down_bias[None], V),
        cot=(cotangent, H),
    )
    outputs = dict(
        o_layer=shape((rows, D), BF),
        o_rows=shape((rows, D), F32),
        o_cond=shape((S, cond), F32),
        o_ada=shape((cond, 4 * D), F32),
        o_adab=shape((1, 4 * D), F32),
        o_q=shape((D, D), BF),
        o_kv=shape((D, 2 * D), BF),
        o_out=shape((D, D), BF),
        o_up=shape((D, F), BF),
        o_upb=shape((1, F), F32),
        o_dn=shape((F, D), BF),
        o_downb=shape((1, D), F32),
    )
    scratch = dict(
        xb=V((3, rows, D), BF),
        cotn=V((rows, D), BF),
        wqkv=V((D, 3 * D), BF),
        wob=V((D, D), BF),
        wupb=V((D, F), BF),
        wdnb=V((F, D), BF),
        pm=V((rows, rows), BF),
        pt=V((rows, rows), BF),
        lws=V((rows + G, near), F32),
        lwt=V((3, S, near, 2 * G), BF),
        mod=V((S, 4 * D), F32),
        mods=V((S, 4 * D), F32),
        n1n=V((rows, D), BF),
        n1s=V((rows, D), BF),
        xs=V((rows, D), BF),
        qkv=V((S, W, 3 * D), BF),
        cotb=V((M, rows, D), BF),
        cnt=V((S, G, W), F32),
        cntt=V((S, G, W), F32),
        mixs=V((rows, D), BF),
        mixx=V((rows, D), F32),
        prob=V((S * HEADS, G, W), F32),
        lsec=V((rows, 128), F32),
        ntb=V((M, rows, D), BF),
        mid=V((rows, D), F32),
        actb=V((M * rows, F), BF),
        ghb=V((M * rows, F), BF),
        bupg=V((1, F), F32),
        g2s=V((M - 1, rows, D), BF),
        g2r=V((M - 1, rows, D), BF),
        g2o=V((rows, D), F32),
        brr=V((M - 1, rows, D), BF),
        gmid=V((rows, D), F32),
        gmw=V((S, W, D), BF),
        stw=V((3, S, 8, 2 * G), F32),
        gmod=V((S, 4 * D), F32),
        gms=V((S, 4 * D), F32),
        gqkv=V((rows, 3 * D), BF),
        gdbs=V((S, D), F32),
        turn=V((D // 128, rows, 128), F32),
        tail=V((small, 256), F32),
        tailo=V((small, 256), F32),
    )
    sums = []
    for i, (n, c) in enumerate(((D, F), (F, D), (D, D), (D, D), (D, 2 * D), (small, 256))):
        dtype = F32 if i == 5 else BF
        bufs = [
            V((n, c // 2), F32),
            V((n, c // 2), dtype),
            V((n, c // 2), dtype),
            V((n // 2, c // 2), dtype),
            V((nz - 1, n // (2 * nz), c // 2), dtype),
        ]
        if i > 1:
            bufs.append(V((M, n // (2 * nz), c // 2), dtype))
        sums.append(tuple(bufs))
    scratch.update(sums=tuple(sums))
    sem = pltpu.SemaphoreType.DMA
    for name, dims in dict(
        xsem=(2, 4),
        lwsem=(2, 1),
        cotsem=(M - 1, 2),
        ntsem=(M - 1, 4),
        g2sem=(M - 1, 2),
        brsem=(M - 1, 2),
        gmsem=(2, 4),
        stsem=(2, 4),
        sumsem=(len(SUMS) * Sum.slots(nz, M),),
    ).items():
        scratch[name] = (sem(dims), sem(dims))
    scratch.update(lsem=sem((7,)))
    names = [*arguments, *outputs, *scratch]
    results = pl.pallas_call(
        functools.partial(kernel, (R, M, rows, D, F, S, near), names),
        out_shape=[*outputs.values()],
        in_specs=[pl.BlockSpec(memory_space=m) for _, m in arguments.values()],
        out_specs=[pl.BlockSpec(memory_space=V) for _ in outputs],
        scratch_shapes=[*scratch.values()],
        name="layer",
        compiler_params=pltpu.CompilerParams(
            collective_id=0, has_side_effects=True, vmem_limit_bytes=63 * 2**20
        ),
    )(*[a for a, _ in arguments.values()])
    got = SimpleNamespace(**dict(zip(outputs, results)))
    return (
        got.o_layer,
        got.o_rows,
        got.o_cond,
        got.o_ada,
        got.o_adab[0],
        got.o_q.astype(F32),
        got.o_kv.astype(F32),
        got.o_out.astype(F32),
        got.o_up.astype(F32),
        got.o_upb[0],
        got.o_dn.astype(F32),
        got.o_downb[0],
    )


def solution(mesh):
    both = P(("rows", "mlp"), None)
    placed = (
        both,
        P(),
        P(("rows", "mlp")),
        both,
        P(),
        P(),
        P(),
        P(),
        P(),
        P(None, "mlp"),
        P("mlp"),
        P("mlp", None),
        P(),
        both,
    )
    return jax.shard_map(
        shards,
        mesh=mesh,
        in_specs=placed,
        out_specs=(
            both,
            both,
            P(),
            P(),
            P(),
            P(),
            P(),
            P(),
            P(None, "mlp"),
            P("mlp"),
            P("mlp", None),
            P(),
        ),
        check_vma=False,
    )
```

```python
import functools
import math
from types import SimpleNamespace

import jax
import jax.numpy as jnp
from jax import lax
from jax.experimental import pallas as pl
from jax.experimental.pallas import tpu as pltpu
from jax.sharding import PartitionSpec as P

HEADS = 4
PAIRS = HEADS // 2
EPSILON = 1e-05
MESH = pl.DeviceIdType.MESH
F32, BF = jnp.float32, jnp.bfloat16
PRECISE = lax.Precision.HIGHEST
NN = (((1,), (0,)), ((), ()))
NT = (((1,), (1,)), ((), ()))
TN = (((0,), (0,)), ((), ()))
MASKED = -1e30


def dot(a, b, dims=NN, precision=None):
    return lax.dot_general(a, b, dims, precision=precision, preferred_element_type=F32)


def mean(v):
    return jnp.mean(v, axis=-1, keepdims=True)


def layer_norm(values):
    centred = values - mean(values)
    inverse = lax.rsqrt(mean(centred * centred) + EPSILON)
    return centred * inverse, inverse


def norm_back(grad, normed, inverse):
    return inverse * (grad - mean(grad) - normed * mean(grad * normed))


def iota(shape, axis):
    return lax.broadcasted_iota(jnp.int32, shape, axis)


def loop(count, body):
    lax.fori_loop(0, count, lambda i, c: (body(i), c)[1], 0)


def remote(src, dst, sems, index, device):
    send, recv = sems
    return pltpu.make_async_remote_copy(
        src_ref=src,
        dst_ref=dst,
        send_sem=send.at[index],
        recv_sem=recv.at[index],
        device_id=device,
        device_id_type=MESH,
    )


class Sum:
    def __init__(self, out, dtype, bufs, sems, base, place, order, role):
        self.out, self.dtype, self.sems, self.base = out, dtype, sems, base
        self.part, self.cs, self.cr, self.rr = bufs[:4]
        self.place = place
        self.order = order
        self.role = role
        self.all_sum = role == PLAIN and 0 not in order
        self.back = order if role != OTHERS else ()
        self.mr = bufs[4] if len(bufs) > 4 else None
        r, m, M, core, x, z, nz = place
        self.index = (m, x, z, x * nz + z)
        self.size = (M, 2, nz, 2 * nz)
        self.width = self.part.shape[1]
        self.mine = pl.ds(pl.multiple_of(core * self.width, self.width), self.width)
        self.other = pl.ds(pl.multiple_of((1 - core) * self.width, self.width), self.width)
        self.start, self.length, self.stage = [0], [self.part.shape[0]], [0]
        for axis in order:
            length = self.length[-1] // self.size[axis]
            self.start.append(self.start[-1] + self.index[axis] * length)
            self.stage.append(self.stage[-1] + self.length[-1] - length)
            self.length.append(length)
        if role != OTHERS:
            self.begin, self.extent = [0], [out.shape[0]]
            for axis in order:
                self.extent.append(self.extent[-1] // self.size[axis])
                self.begin.append(self.begin[-1] + self.index[axis] * self.extent[-1])
        self.todo = [functools.partial(self.share, i) for i in range(len(order))]
        if role == OTHERS:
            self.todo.append(self.send_over)
            return
        if self.all_sum:
            self.todo.append(self.send_mlp)
        self.todo.append(self.settle)
        self.todo += [functools.partial(self.gather, i) for i in reversed(range(len(self.back)))]
        self.todo.append(self.gather_core)

    def step(self, count=1):
        for _ in range(min(count, len(self.todo))):
            self.todo.pop(0)()

    def peer(self, axis, t):
        r, m, M, core, x, z, nz = self.place
        if axis == 0:
            return r, lax.rem(m + t, M)
        if axis == 1:
            return z * 4 + (1 - x) * 2 + core, m
        if axis == 2:
            return lax.rem(z + t, nz) * 4 + x * 2 + core, m
        to = lax.rem(x * nz + z + t, 2 * nz)
        return lax.rem(to, nz) * 4 + to // nz * 2 + core, m

    def slot(self, phase, axis, t):
        M, _, nz, _ = self.size
        return phase * (M + 3 * nz - 2) + (0, M - 1, M, M + nz - 1)[axis] + t - 1

    def copy(self, src, dst, slot, device):
        return remote(src, dst, self.sems, self.base + slot, device)

    def core_copy(self, phase):
        r, m, M, core, x, z, nz = self.place
        device = (z * 4 + x * 2 + 1 - core, m)
        slot = 2 * (M + 3 * nz - 2) + phase
        if phase == 0:
            return self.copy(self.cs, self.cr, slot, device)
        block = self.out.at[:, self.mine]
        return self.copy(block, block, slot, device)

    def share_copy(self, i, t):
        axis, length = self.order[i], self.length[i + 1]
        at = pl.ds(self.stage[i] + (t - 1) * length, length)
        return self.copy(
            self.cs.at[at], self.rr.at[at], self.slot(0, axis, t), self.peer(axis, t)
        )

    def gather_copy(self, i, t):
        axis = self.back[i]
        block = self.out.at[self.cut(self.begin[i + 1], self.extent[i + 1]), self.mine]
        return self.copy(block, block, self.slot(1, axis, t), self.peer(axis, t))

    def mlp_copy(self, t):
        r, m, M, core, x, z, nz = self.place
        block = self.mr.at[m]
        return self.copy(block, block, 2 * (M + 3 * nz - 2) + 1 + t, (r, lax.rem(m + t, M)))

    def cut(self, start, size):
        return pl.ds(pl.multiple_of(start, size), size)

    def core_send(self):
        self.core_copy(0).start()

    def take(self, i):
        if i == 0:
            self.core_copy(0).wait()
            return
        at = self.cut(self.start[i], self.length[i])
        value = self.part[at, :]
        for t in range(1, self.size[self.order[i - 1]]):
            self.share_copy(i - 1, t).wait_recv()
            here = pl.ds(self.stage[i - 1] + (t - 1) * self.length[i], self.length[i])
            value = value + self.rr[here, :].astype(F32)
        if i == 1:
            value = value + self.cr[at, :].astype(F32)
        self.part[at, :] = value

    def share(self, i):
        self.take(i)
        axis, length = self.order[i], self.length[i + 1]
        for t in range(1, self.size[axis]):
            block = lax.rem(self.index[axis] + t, self.size[axis])
            at = self.cut(self.start[i] + block * length, length)
            value = self.part[at, :]
            if i == 0:
                value = value + self.cr[at, :].astype(F32)
            self.cs[pl.ds(self.stage[i] + (t - 1) * length, length), :] = value.astype(self.dtype)
            self.share_copy(i, t).start()

    def send_mlp(self):
        n = len(self.order)
        self.take(n)
        r, m, M, core, x, z, nz = self.place
        self.mr[m] = self.part[self.cut(self.start[n], self.length[n]), :].astype(self.dtype)
        for t in range(1, M):
            self.mlp_copy(t).start()

    def over_copy(self, t):
        r, m, M, core, x, z, nz = self.place
        length = self.length[-1] // (M - 1)
        source = self.cs.at[pl.ds(self.stage[-1] + (t - 1) * length, length)]
        slot = 2 * (M + 3 * nz - 2) + 1 + t
        return self.copy(source, self.mate.mr.at[t - 1], slot, (r, lax.rem(m + t, M)))

    def send_over(self):
        n = len(self.order)
        self.take(n)
        value = self.part[self.cut(self.start[n], self.length[n]), :]
        self.cs[pl.ds(self.stage[n], self.length[n]), :] = value.astype(self.dtype)
        for t in range(1, self.size[0]):
            self.over_copy(t).start()

    def settle(self):
        n = len(self.order)
        at = self.cut(self.start[n], self.length[n])
        if self.all_sum:
            for t in range(1, self.size[0]):
                self.mlp_copy(t).wait_recv()
            value = self.mr[0].astype(F32)
            for t in range(1, self.size[0]):
                value = value + self.mr[t].astype(F32)
        else:
            self.take(n)
            value = self.part[at, :]
        if self.role == OWN:
            for t in range(1, self.size[0]):
                self.mate.over_copy(t).wait_recv()
                value = value + self.mr[t - 1].astype(F32)
        here = self.cut(self.begin[-1], self.extent[-1])
        self.out[here, self.mine] = value.astype(self.dtype)

    def gather(self, i):
        if i < len(self.back) - 1:
            for t in range(1, self.size[self.back[i + 1]]):
                self.gather_copy(i + 1, t).wait_recv()
        for t in range(1, self.size[self.back[i]]):
            self.gather_copy(i, t).start()

    def gather_core(self):
        for t in range(1, self.size[self.back[0]]):
            self.gather_copy(0, t).wait_recv()
        self.core_copy(1).start()

    def arrive(self):
        self.core_copy(1).wait_recv()

    def finish(self):
        assert not self.todo
        for i, axis in enumerate(self.order):
            for t in range(1, self.size[axis]):
                self.share_copy(i, t).wait_send()
        if self.role == OTHERS:
            for t in range(1, self.size[0]):
                self.over_copy(t).wait_send()
            return
        self.core_copy(1).wait_send()
        for i, axis in enumerate(self.back):
            for t in range(1, self.size[axis]):
                self.gather_copy(i, t).wait_send()
        if self.all_sum:
            for t in range(1, self.size[0]):
                self.mlp_copy(t).wait_send()

    @staticmethod
    def slots(nz, m):
        return 2 * (m + 3 * nz - 2) + 1 + m


class Spread:
    def __init__(self, source, parts, sems, base, place, z_first):
        self.source, self.parts, self.sems, self.base = source, parts, sems, base
        self.z_first = z_first
        self.place = place
        r, m, M, core, x, z, nz = place
        _, rows, cols = parts.shape
        self.rows, self.piece, width = rows, rows // (2 * nz), cols // 2
        self.mine = pl.ds(pl.multiple_of(core * width, width), width)
        self.here = self.cut((x * nz + z if z_first else z * 2 + x) * self.piece, self.piece)

    def cut(self, start, size):
        return pl.ds(pl.multiple_of(start, size), size)

    def copies(self, stage, t):
        r, m, M, core, x, z, nz = self.place
        base = self.base + (t - 1) * (nz + 2)
        if stage == 0:
            source = self.source.at[self.here, self.mine]
            target = self.parts.at[m, self.here, self.mine]
            return [remote(source, target, self.sems, base, (r, lax.rem(m + t, M)))]
        part = self.parts.at[lax.rem(m + M - t, M)]
        over_z = [lax.rem(z + u, nz) * 4 + x * 2 + core for u in range(1, nz)]
        over_x = [z * 4 + (1 - x) * 2 + core]
        if stage == 1:
            block = part.at[self.here, self.mine]
            rows = over_z if self.z_first else over_x
        elif stage == 2:
            many = (nz if self.z_first else 2) * self.piece
            block = part.at[self.cut((x if self.z_first else z) * many, many), self.mine]
            rows = over_x if self.z_first else over_z
        else:
            block = part.at[:, self.mine]
            rows = [z * 4 + x * 2 + 1 - core]
        first = base + (0, 1, nz if self.z_first else 2, nz + 1)[stage]
        return [
            remote(block, block, self.sems, first + i, (row, m)) for i, row in enumerate(rows)
        ]

    def each(self, stage):
        return [c for t in range(1, self.place[2]) for c in self.copies(stage, t)]

    def send(self, stage):
        if stage > 0:
            self.arrive(stage - 1)
        for c in self.each(stage):
            c.start()

    def arrive(self, stage):
        for c in self.each(stage):
            c.wait_recv()

    def drain(self):
        for stage in range(4):
            for c in self.each(stage):
                c.wait_send()


PLAIN, OWN, OTHERS = 0, 1, 2
SUMS = ("up", "down", "up2", "down2", "out", "query", "key", "value", "tail")
ROLES = (OWN, OWN, OTHERS, OTHERS, PLAIN, PLAIN, PLAIN, PLAIN, PLAIN)
FLAT, ALL = (1, 2), (0, 1, 2)
ORDERS = (FLAT, FLAT, FLAT, FLAT, ALL, ALL, ALL, (1, 2, 0), (0, 3))


def sharing(i, rows, M, nz):
    if rows % (16 * 2 * nz * M) == 0 or (i == len(SUMS) - 1 and rows % (8 * 2 * nz * M) == 0):
        return ORDERS[i]
    return tuple(axis for axis in ORDERS[i] if axis != 0)


def kernel(static, names, *refs):
    ref = SimpleNamespace(**dict(zip(names, refs)))
    R, M, rows, D, F, S, near = static
    nz = R // 4
    G = rows // S
    W = 3 * G
    head = D // HEADS
    factor = 1.0 / math.sqrt(head)
    r, y = lax.axis_index("rows"), lax.axis_index("mlp")
    core, xi, z = lax.rem(r, 2), lax.rem(r // 2, 2), r // 4
    me = r * M + y
    devices = R * M
    pairs = M == 2
    up_row, down_row = lax.rem(r + 1, R), lax.rem(r + R - 1, R)
    after, before = lax.rem(me + 1, devices), lax.rem(me + devices - 1, devices)

    local = []
    lsem = ref.lsem
    for i, (src, dst) in enumerate(
        (
            (ref.x, ref.xb.at[1]),
            (ref.wq, ref.wqkv.at[:, 0:D]),
            (ref.wkv, ref.wqkv.at[:, D : 3 * D]),
            (ref.cot, ref.cotn),
            (ref.wo, ref.wob),
            (ref.wup, ref.wupb.at[y]),
            (ref.wdn, ref.wdnb.at[y]),
        )
    ):
        c = pltpu.make_async_copy(src, dst, lsem.at[i])
        c.start()
        local.append(c)

    barrier = pltpu.get_barrier_semaphore()
    others = [(r, lax.rem(y + t, M)) for t in range(1, M)]
    others.append((z * 4 + xi * 2 + 1 - core, y))
    for t in range(1, 2 * nz):
        to = lax.rem(xi * nz + z + t, 2 * nz)
        others.append((lax.rem(to, nz) * 4 + to // nz * 2 + core, y))
    if pairs:
        others += [(up_row, y), (down_row, y)]
    else:
        others += [(after // M, lax.rem(after, M)), (before // M, lax.rem(before, M))]
    for device in others:
        pl.semaphore_signal(barrier, inc=1, device_id=device, device_id_type=MESH)
    pl.semaphore_wait(barrier, len(others))

    def halo(source, at, sems):
        def first(k):
            if pairs:
                return [remote(source(k), at(2 * y, k), sems, (0, k), (r, 1 - y))]
            return [
                remote(source(k), at(0, k), sems, (0, k), (after // M, lax.rem(after, M))),
                remote(source(k), at(2, k), sems, (1, k), (before // M, lax.rem(before, M))),
            ]

        def second(k):
            if pairs:
                to = jnp.where(y == 0, up_row, down_row)
                return remote(at(2 * (1 - y), k), at(2 * y, k), sems, (1, k), (to, y))
            return first(k)[1]

        def send(k):
            for c in first(k):
                c.start()

        def pass_on(k):
            first(k)[0].wait_recv()
            if pairs:
                second(k).start()

        def arrive(k):
            second(k).wait_recv()

        def drain(k):
            first(k)[0].wait_send()
            second(k).wait_send()

        return send, pass_on, arrive, drain

    near_slot = 2 * (1 - y) if pairs else 0
    far_slot = 2 * y if pairs else 2
    xb = ref.xb
    quarter = rows // 4

    def part(k, n=quarter):
        return pl.ds(pl.multiple_of(k * n, n), n)

    x_send, x_pass, x_arrive, x_drain = halo(
        lambda k: ref.x.at[part(k)], lambda slot, k: xb.at[slot, part(k)], ref.xsem
    )
    loop(4, x_send)
    place_of = (r, y, M, core, xi, z, nz)
    spread = [
        Spread(source, parts, ref.spsem, i * (M - 1) * (nz + 2), place_of, i == 0)
        for i, (source, parts) in enumerate(((ref.wup, ref.wupb), (ref.wdn, ref.wdnb)))
    ]
    for part_of in spread:
        part_of.send(0)
    upb = ref.upb
    upb[y] = jnp.broadcast_to(ref.bup[...].astype(F32).reshape(1, F), (8, F))

    def bias_copy(t):
        return remote(upb.at[y], upb.at[y], ref.ubsem, t - 1, (r, lax.rem(y + t, M)))

    for t in range(1, M):
        bias_copy(t).start()

    def build(k):
        at = part(k)
        a, b = iota((quarter, rows), 0) + k * quarter, iota((quarter, rows), 1)
        ref.pm[at, :] = jnp.where(b == lax.rem(a, G) * S + a // G, 1.0, 0.0).astype(BF)
        ref.pt[at, :] = jnp.where(a == lax.rem(b, G) * S + b // G, 1.0, 0.0).astype(BF)

    loop(4, build)
    a, b = iota((quarter, quarter), 0), iota((quarter, quarter), 1)
    few = quarter // S
    ref.pq[...] = jnp.where(b == lax.rem(a, few) * S + a // few, 1.0, 0.0).astype(BF)
    pm, pt = ref.pm, ref.pt

    nodes = devices * G
    place = ref.nbr[...] // S - me * G + G
    place = jnp.where(place < 0, place + nodes, place)
    place = jnp.where(place >= nodes, place - nodes, place)
    place = place.astype(F32).astype(BF)
    lws = ref.lws
    lws[rows : rows + G, :] = jnp.zeros((G, near), F32)
    lws[0:rows, :] = dot(pm[...], place, NT)
    lwt = ref.lwt
    eye = jnp.where(iota((near, near), 0) == iota((near, near), 1), 1.0, 0.0).astype(BF)

    def turn(s):
        block = lws[pl.ds(pl.multiple_of(s * G, G), 2 * G), :].astype(BF)
        lwt[1, s] = dot(eye, block, NT).astype(BF)

    loop(S, turn)
    l_send, l_pass, l_arrive, l_drain = halo(
        lambda k: lwt.at[1], lambda slot, k: lwt.at[slot], ref.lwsem
    )
    l_send(0)

    modulation = dot(ref.nc[...], ref.adaw[...]) + ref.adab[...].astype(F32).reshape(1, 4 * D)
    ref.mod[...] = modulation
    mods = ref.mods
    for s in range(S):
        mods[s : s + 1, :] = ref.mod[pl.ds(ref.sid[s], 1), :]

    n1s, qkv = ref.n1s, ref.qkv
    wqkv = ref.wqkv

    turn16 = quarter // S

    def norm_block(slot, k):
        at = part(k)
        normed, _ = layer_norm(xb[slot, at, :].astype(F32))
        scaled = normed.reshape(turn16, S, D) * (1.0 + mods[:, 0:D])[None]
        scaled = scaled + mods[:, D : 2 * D][None]
        ordered = dot(ref.pq[...], scaled.reshape(quarter, D).astype(BF)).astype(BF)
        wide = dot(ordered, wqkv[...]).astype(BF).reshape(S, turn16, 3 * D)
        here = pl.ds(pl.multiple_of(slot * G + k * turn16, turn16), turn16)
        qkv[:, here, :] = wide
        return ordered.reshape(S, turn16, D)

    local[0].wait()
    local[1].wait()
    local[2].wait()

    def own_norm(k):
        n1s[:, pl.ds(pl.multiple_of(k * turn16, turn16), turn16), :] = norm_block(1, k)

    loop(4, own_norm)
    local[3].wait()
    xs, cotb = ref.xs, ref.cotb

    def order(k):
        xs[part(k), :] = dot(pm[part(k), :], xb[1]).astype(BF)
        cotb[part(k), :] = dot(pm[part(k), :], ref.cotn[...]).astype(BF)

    loop(4, order)

    cnt, cntt = ref.cnt, ref.cntt

    def count(s):
        block = lwt[1, s].astype(F32)
        block = jnp.where(iota((near, 2 * G), 1) < G, block, pltpu.roll(block, G, 1))
        key = iota((W, 2 * G), 0).astype(F32)
        total = jnp.zeros((W, 2 * G), F32)
        for j in range(near):
            total = total + jnp.where(block[j : j + 1, :] == key, 1.0, 0.0)
        cnt[s] = total

    loop(S, count)

    def near_norm(k):
        x_pass(k)
        norm_block(near_slot, k)

    loop(4, near_norm)


    def far_norm(k):
        x_arrive(k)
        norm_block(far_slot, k)

        @pl.when(k == 2)
        def _():
            spread[0].send(1)
            spread[1].send(1)

    loop(4, far_norm)

    mixs, mixx, prob, stw = ref.mixs, ref.mixx, ref.prob, ref.stw
    ntb, mid = ref.ntb, ref.mid
    pair = 2 * head

    def apart(block):
        nothing = jnp.zeros((block.shape[0], head), block.dtype)
        left = jnp.concatenate([block[:, 0:head], nothing], axis=1)
        right = jnp.concatenate([nothing, block[:, head:pair]], axis=1)
        return jnp.concatenate([left, right], axis=0)

    def attend(k):
        for s2 in range(2):
            s = 2 * k + s2
            at = pl.ds(pl.multiple_of(s * G, G), G)
            times = cnt[s]
            logs = []
            for p in range(PAIRS):
                lo, hi = p * pair, (p + 1) * pair
                queries = apart(qkv[s, G : 2 * G, lo:hi])
                scores = dot(qkv[s, :, D + lo : D + hi], queries, NT) * factor
                scores = jnp.where(times > 0.0, scores, MASKED)
                top = jnp.max(scores, axis=0, keepdims=True)
                power = jnp.exp(scores - top)
                total = jnp.sum(power * times, axis=0, keepdims=True)
                probs = power * (1.0 / total)
                prob[s * PAIRS + p] = probs
                weight = (times * probs.astype(BF).astype(F32)).astype(BF)
                rest = (times * probs - weight.astype(F32)).astype(BF)
                both = jnp.concatenate([weight, rest], axis=1)
                mixed = dot(both, qkv[s, :, 2 * D + lo : 2 * D + hi], TN)
                one, two = mixed[0:G, 0:head], mixed[G : 2 * G, head:pair]
                mixs[at, lo : lo + head] = one.astype(BF)
                mixs[at, lo + head : hi] = two.astype(BF)
                mixx[at, lo : lo + head] = one + mixed[2 * G : 3 * G, 0:head]
                mixx[at, lo + head : hi] = two + mixed[3 * G : 4 * G, head:pair]
                logs.append(top + jnp.log(total))
            logs.append(jnp.zeros((8 - PAIRS, 2 * G), F32))
            stw[1, s] = jnp.concatenate(logs, axis=0)

    loop(4, attend)

    local[4].wait()
    wo = ref.wob
    half = rows // 2
    group = half // G

    def mix_out(c):
        at = part(c, half)
        middle = xs[at, :].astype(F32) + dot(mixs[at, :], wo[...])
        mid[at, :] = middle
        normed, _ = layer_norm(middle)
        for i in range(group):
            lo = i * G
            scale = mods[pl.ds(c * group + i, 1), 2 * D : 3 * D]
            shift = mods[pl.ds(c * group + i, 1), 3 * D : 4 * D]
            here = pl.ds(pl.multiple_of(c * half + lo, G), G)
            ntb[here, :] = (normed[lo : lo + G] * (1.0 + scale) + shift).astype(BF)

    loop(2, mix_out)

    local[5].wait()
    local[6].wait()
    l_pass(0)
    spread[0].send(2)
    spread[1].send(2)
    wup, wdn, actb, ghb = ref.wupb, ref.wdnb, ref.actb, ref.ghb
    bupg, g2o = ref.bupg, ref.g2o
    bupg[...] = jnp.zeros_like(bupg)
    g2o[...] = jnp.zeros_like(g2o)
    tile = 256

    def feed(p):
        def column(f):
            cols = part(f, tile)
            hidden = dot(ntb[...], wup[p, :, cols]) + upb[p, 0:1, cols]
            gate = jax.nn.sigmoid(hidden)
            active = hidden * gate
            actb[p, :, cols] = active.astype(BF)
            grad = dot(cotb[...], wdn[p, cols, :], NT)
            grad = (grad * (gate + active * (1.0 - gate))).astype(BF)
            ghb[p, :, cols] = grad
            bupg[p, 0:1, cols] += jnp.sum(grad.astype(F32), axis=0, keepdims=True)

        loop(F // tile, column)
        for q in range(D // tile):
            lo, hi = q * tile, (q + 1) * tile
            g2o[:, lo:hi] += dot(ghb[p], wup[p, lo:hi, :], NT)

    feed(y)

    count_of = Sum.slots(nz, M)
    sums = SimpleNamespace()
    written = []

    def write(source, result):
        c = pltpu.make_async_copy(source, result, ref.wsem.at[len(written)])
        c.start()
        written.append(c)

    for i, (name, bufs) in enumerate(zip(SUMS, ref.sums)):
        out, *bufs = bufs
        dtype = F32 if i == len(SUMS) - 1 else BF
        order = sharing(i, bufs[0].shape[0], M, nz)
        total = Sum(out, dtype, bufs, ref.sumsem, i * count_of, place_of, order, ROLES[i])
        setattr(sums, name, total)
    sums.up.mate, sums.down.mate, sums.up2.mate, sums.down2.mate = (
        sums.up2,
        sums.down2,
        sums.up,
        sums.down,
    )

    def weight_grad(total, left, right):
        width = total.width
        for out, start, kind in (
            (total.cs, (1 - core) * width, BF),
            (total.part, core * width, F32),
        ):
            at = pl.ds(pl.multiple_of(start, width), width)
            out[...] = dot(left, right(at), TN).astype(kind)
            if kind == BF:
                total.core_send()

    def ffn_grad(total, count, which, rows_of, left, right):
        width = total.width
        many, block = min(rows_of, 512), rows_of // (2 * nz)
        for out, start, kind in (
            (total.cs, (1 - core) * width, BF),
            (total.part, core * width, F32),
        ):
            at = pl.ds(pl.multiple_of(start, width), width)

            def tile_row(i):
                u, f = i // (rows_of // many), lax.rem(i, rows_of // many)
                p = which(u)
                value = dot(left(p, part(f, many)), right(p, at), TN).astype(kind)
                if count == 1:
                    out[part(f, many), :] = value
                    return
                for v in range(many // block):
                    row = ((f * (many // block) + v) * count + u) * block
                    here = pl.ds(pl.multiple_of(row, block), block)
                    out[here, :] = value[v * block : (v + 1) * block]

            loop(count * rows_of // many, tile_row)
            if kind == BF:
                total.core_send()

    def up_grad(total, count, which):
        ffn_grad(total, count, which, D, lambda p, f: ntb[:, f], lambda p, at: ghb[p, :, at])

    def down_grad(total, count, which):
        ffn_grad(total, count, which, F, lambda p, f: actb[p, :, f], lambda p, at: cotb[:, at])

    up_grad(sums.up, 1, lambda u: y)
    down_grad(sums.down, 1, lambda u: y)
    sums.up.step()
    sums.down.step()

    def feed_other(t):
        @pl.when(t == 0)
        def _():
            spread[0].send(3)
            spread[1].send(3)
            spread[0].arrive(3)
            spread[1].arrive(3)
            for u in range(1, M):
                bias_copy(u).wait_recv()

        feed(lax.rem(y + t + 1, M))

    loop(M - 1, feed_other)

    def steps(i, plan):
        for when, which in plan.items():

            @pl.when(i == when)
            def _():
                for total in which:
                    total.step()

    gmid, gmw, gatt, gmod = ref.gmid, ref.gmw, ref.cotn, ref.gmod
    row, lane = iota((8, D), 0), iota((8, D), 1) // head
    pick_one = jnp.where((row >= PAIRS) & (lane == 2 * (row - PAIRS)), 1.0, 0.0)
    pick_two = jnp.where((row >= PAIRS) & (lane == 2 * (row - PAIRS) + 1), 1.0, 0.0)
    m_send, m_pass, m_arrive, m_drain = halo(
        lambda k: gmw.at[pl.ds(2 * k, 2), pl.ds(G, G)],
        lambda slot, k: gmw.at[pl.ds(2 * k, 2), pl.ds(pl.multiple_of(slot * G, G), G)],
        ref.gmsem,
    )
    s_send, s_pass, s_arrive, s_drain = halo(
        lambda k: stw.at[1, pl.ds(2 * k, 2)],
        lambda slot, k: stw.at[slot, pl.ds(2 * k, 2)],
        ref.stsem,
    )

    def middle_back(c):
        at = part(c, half)
        grad = g2o[at, :]
        normed, inverse = layer_norm(mid[at, :])
        weighted = []
        for i in range(group):
            s = c * group + i
            lo, hi = i * G, (i + 1) * G
            scale = mods[pl.ds(s, 1), 2 * D : 3 * D]
            weighted.append(grad[lo:hi] * (1.0 + scale))
            gmod[pl.ds(s, 1), 2 * D : 3 * D] = jnp.sum(
                grad[lo:hi] * normed[lo:hi], axis=0, keepdims=True
            )
            gmod[pl.ds(s, 1), 3 * D : 4 * D] = jnp.sum(grad[lo:hi], axis=0, keepdims=True)
        weighted = jnp.concatenate(weighted, axis=0)
        middle = cotb[at, :].astype(F32) + norm_back(weighted, normed, inverse)
        gmid[at, :] = middle
        rounded = middle.astype(BF)
        gatt[at, :] = rounded
        mixture = dot(rounded, wo[...], NT).astype(BF)
        gmw[pl.ds(c * group, group), G : 2 * G, :] = mixture.reshape(group, G, D)
        product = mixture.astype(F32) * mixx[at, :]
        ones = dot(pick_one, product, NT, PRECISE)
        twos = dot(pick_two, product, NT, PRECISE)
        first_lanes = iota((8, 2 * G), 1) < G
        for g in range(group // 2):
            lo, hi = g * 2 * G, (g + 1) * 2 * G
            one, two = ones[:, lo:hi], twos[:, lo:hi]
            s = c * group + 2 * g
            stw[1, s] += jnp.where(first_lanes, one, pltpu.roll(two, G, 1))
            stw[1, s + 1] += jnp.where(first_lanes, pltpu.roll(one, G, 1), two)
        for k in range(2):
            m_send(2 * c + k)
            s_send(2 * c + k)

    loop(2, middle_back)

    def pass_on(k):
        m_pass(k)
        s_pass(k)

    sums.up.step()
    up_grad(sums.up2, M - 1, lambda u: lax.rem(y + u + 1, M))
    down_grad(sums.down2, M - 1, lambda u: lax.rem(y + u + 1, M))
    pass_on(0)
    sums.up2.step()
    weight_grad(sums.out, mixs[...], lambda at: gatt[:, at])
    sums.down.step()

    gqkv = ref.gqkv

    def query_back(s):
        at = pl.ds(pl.multiple_of(s * G, G), G)
        times = cnt[s]
        for p in range(PAIRS):
            lo, hi = p * pair, (p + 1) * pair
            grads = apart(gmw[s, G : 2 * G, lo:hi])
            gprob = dot(qkv[s, :, 2 * D + lo : 2 * D + hi], grads, NT)
            gscore = prob[s * PAIRS + p] * (gprob - stw[1, s, PAIRS + p : PAIRS + p + 1, :])
            weight = (times * gscore.astype(BF).astype(F32)).astype(BF)
            gquery = dot(weight, qkv[s, :, D + lo : D + hi], TN) * factor
            gqkv[at, lo : lo + head] = gquery[0:G, 0:head].astype(BF)
            gqkv[at, lo + head : hi] = gquery[G : 2 * G, head:pair].astype(BF)

    def query_pass(k):
        query_back(2 * k)
        query_back(2 * k + 1)

        @pl.when(k == 1)
        def _():
            pass_on(1)

        steps(k, {1: [sums.down2]})

    loop(4, query_pass)

    sums.out.step()
    pass_on(2)
    weight_grad(sums.query, n1s[...].reshape(rows, D), lambda at: gqkv[:, at])
    l_arrive(0)

    def count_back(s):
        shift = [2 * G, G, 0]
        block = jnp.concatenate(
            [lwt[b, s][:, 0:G].astype(F32) - float(shift[b]) for b in range(3)], axis=1
        ).astype(jnp.int32)
        key = iota((G, W), 0)
        total = jnp.zeros((G, W), F32)
        for j in range(near):
            total = total + jnp.where(block[j : j + 1, :] == key, 1.0, 0.0)
        cntt[s] = total

    loop(S, count_back)

    def finish_out(k):
        at = part(k)
        value = mid[at, :] + ref.bdn[...].astype(F32).reshape(1, D)
        for p in range(M):
            value = value + dot(actb[p, at, :], wdn[p])
        ref.n1n[at, :] = value.astype(BF)

    loop(4, finish_out)
    pass_on(3)
    sums.query.step()
    sums.up2.step()

    def key_back(s):
        at = pl.ds(pl.multiple_of(s * G, G), G)
        times = cntt[s]
        stats = [
            jnp.concatenate([stw[b, s][:, i * G : (i + 1) * G] for b in range(3)], axis=1)
            for i in range(2)
        ]
        for p in range(PAIRS):
            lo, hi = p * pair, (p + 1) * pair
            queries, grads = qkv[s, :, lo:hi], gmw[s, :, lo:hi]
            scores = dot(apart(qkv[s, G : 2 * G, D + lo : D + hi]), queries, NT) * factor
            gprob = dot(apart(qkv[s, G : 2 * G, 2 * D + lo : 2 * D + hi]), grads, NT)
            gscores, weights = [], []
            for i in range(2):
                rows_of = slice(i * G, (i + 1) * G)
                log, delta = stats[i][p : p + 1], stats[i][PAIRS + p : PAIRS + p + 1]
                probs = jnp.exp(jnp.where(times > 0.0, scores[rows_of] - log, MASKED))
                gscore = probs * (gprob[rows_of] - delta)
                gscores.append((times * gscore.astype(BF).astype(F32)).astype(BF))
                weights.append((times * probs.astype(BF).astype(F32)).astype(BF))
            gkey = dot(jnp.concatenate(gscores, axis=0), queries) * factor
            gvalue = dot(jnp.concatenate(weights, axis=0), grads)
            for i in range(2):
                cols = pl.ds(D + lo + i * head, head)
                gqkv[at, cols] = gkey[i * G : (i + 1) * G, i * head : (i + 1) * head].astype(BF)
                cols = pl.ds(2 * D + lo + i * head, head)
                gqkv[at, cols] = gvalue[i * G : (i + 1) * G, i * head : (i + 1) * head].astype(BF)

    def key_pass(k):
        m_arrive(k)
        s_arrive(k)
        key_back(2 * k)
        key_back(2 * k + 1)

    loop(4, key_pass)

    keys, values = gqkv.at[:, D : 2 * D], gqkv.at[:, 2 * D : 3 * D]
    weight_grad(sums.key, n1s[...].reshape(rows, D), lambda at: keys[:, at])
    weight_grad(sums.value, n1s[...].reshape(rows, D), lambda at: values[:, at])
    sums.down2.step()
    sums.out.step()
    sums.up2.step()
    sums.key.step()
    sums.value.step()

    gdbs = ref.gdbs
    out_rows = ref.outr

    def first_back(c):
        at = part(c, half)
        grad = dot(gqkv[at, :], wqkv[...], NT)
        normed, inverse = layer_norm(xs[at, :].astype(F32))
        weighted = []
        for i in range(group):
            s = c * group + i
            lo, hi = i * G, (i + 1) * G
            here = pl.ds(pl.multiple_of(s * G, G), G)
            gmod[pl.ds(s, 1), 0:D] = jnp.sum(grad[lo:hi] * normed[lo:hi], axis=0, keepdims=True)
            gmod[pl.ds(s, 1), D : 2 * D] = jnp.sum(grad[lo:hi], axis=0, keepdims=True)
            gdbs[pl.ds(s, 1), :] = jnp.sum(cotb[here, :].astype(F32), axis=0, keepdims=True)
            weighted.append(grad[lo:hi] * (1.0 + mods[pl.ds(s, 1), 0:D]))
        weighted = jnp.concatenate(weighted, axis=0)
        g2o[at, :] = gmid[at, :] + norm_back(weighted, normed, inverse)
        steps(c, {0: [sums.query], 1: [sums.down2]})

    loop(2, first_back)

    tail = ref.tail
    tail[...] = jnp.zeros_like(tail)
    for c in range(4 * D // tile):
        tail[c * S : (c + 1) * S, :] = gmod[:, c * tile : (c + 1) * tile]
    base = 4 * D // tile * S
    for c in range(D // tile):
        tail[base + c * S : base + (c + 1) * S, :] = gdbs[:, c * tile : (c + 1) * tile]
    base_up = base + D // tile * S
    for c in range(F // tile):
        for p in range(M):
            row = base_up + p * (F // tile) + c
            tail[row : row + 1, :] = bupg[p, 0:1, c * tile : (c + 1) * tile]
    sums.tail.cs[...] = tail[:, sums.tail.other]
    sums.tail.part[...] = tail[:, sums.tail.mine]
    sums.tail.core_send()
    sums.key.step()
    sums.value.step()
    sums.out.step()

    for c in range(D // 128):
        lo, hi = c * 128, (c + 1) * 128
        for s in range(S):
            ref.turn[c, pl.ds(s, G, stride=S), :] = g2o[s * G : (s + 1) * G, lo:hi]
        out_rows[:, lo:hi] = ref.turn[c]
    write(out_rows, ref.o_rows)

    sums.tail.step()
    sums.up.step(2)
    sums.query.step()

    def order_back(k):
        ref.outl[part(k), :] = dot(pt[part(k), :], ref.n1n[...]).astype(BF)

    loop(4, order_back)
    write(ref.outl, ref.o_layer)
    sums.down.step(2)
    sums.key.step()
    sums.value.step()
    sums.tail.step()
    sums.out.step(2)
    sums.up.step()
    sums.query.step(2)
    sums.value.step(2)
    sums.key.step(2)
    sums.down.step()
    sums.tail.step(2)
    sums.out.step()
    sums.query.step()
    sums.value.step()
    sums.key.step()
    sums.up.step()
    sums.tail.step()
    sums.out.step()
    sums.query.step()
    sums.value.step()
    sums.key.step()
    sums.down.step()
    sums.tail.step()
    late = (sums.up, sums.down, sums.query, sums.out, sums.key, sums.value, sums.tail)
    results = (ref.o_up, ref.o_dn, ref.o_q, ref.o_out, ref.o_k, ref.o_v, ref.o_tail)
    for total, result in zip(late, results):
        while total.todo:
            total.step()
        total.arrive()
        write(total.out, result)
    for total in (*late, sums.up2, sums.down2):
        total.finish()
    for c in written:
        c.wait()

    loop(4, x_drain)
    l_drain(0)
    loop(4, m_drain)
    loop(4, s_drain)

    for part_of in spread:
        part_of.drain()
    for t in range(1, M):
        bias_copy(t).wait_send()


WIDE = ("o_up", "o_dn", "o_out", "o_q", "o_k", "o_v")


def widen(static, names, *refs):
    ref = SimpleNamespace(**dict(zip(names, refs)))
    M, D, F, S = static
    tile = 256
    y = lax.axis_index("mlp")
    sources = (ref.o_up, ref.o_dn, ref.o_out, ref.o_q, ref.o_k, ref.o_v)
    targets = (
        ref.f_up,
        ref.f_dn,
        ref.f_out,
        ref.f_q,
        ref.f_kv.at[:, 0:D],
        ref.f_kv.at[:, D : 2 * D],
    )
    n = len(sources)
    tail_in = pltpu.make_async_copy(ref.o_tail, ref.tail, ref.isem.at[n])
    tail_in.start()
    loads = []
    for i, source in enumerate(sources):
        loads.append(pltpu.make_async_copy(source, ref.inb[i], ref.isem.at[i]))
        loads[-1].start()
    straight = [
        (ref.o_layer, ref.layer, ref.f_layer),
        (ref.o_rows, ref.rows, ref.f_rows),
    ]
    for i, (source, middle, _) in enumerate(straight):
        pltpu.make_async_copy(source, middle, ref.isem.at[n + 1 + i]).start()
    stores = []
    for i in range(n):
        loads[i].wait()
        count = sources[i].shape[0] // 128

        def part(k):
            at = pl.ds(pl.multiple_of(k * 128, 128), 128)
            ref.outb[i][at, :] = ref.inb[i][at, :].astype(F32)

        loop(count, part)
        stores.append(pltpu.make_async_copy(ref.outb[i], targets[i], ref.osem.at[i]))
        stores[-1].start()
    for i, (source, middle, target) in enumerate(straight):
        pltpu.make_async_copy(source, middle, ref.isem.at[n + 1 + i]).wait()
        stores.append(pltpu.make_async_copy(middle, target, ref.osem.at[n + 1 + i]))
        stores[-1].start()
    tail_in.wait()
    tail, gms = ref.tail, ref.gms
    pick = jnp.zeros((S, S), F32)
    for s in range(S):
        hit = (iota((S, S), 1) == s) & (iota((S, S), 0) == ref.sid[s])
        pick = pick + jnp.where(hit, 1.0, 0.0)
    for c in range(4 * D // tile):
        gms[:, c * tile : (c + 1) * tile] = dot(pick, tail[c * S : (c + 1) * S, :], NN, PRECISE)
    total = gms[...]
    ref.ada[...] = dot(ref.nc[...].astype(F32), total, TN, PRECISE)
    stores.append(pltpu.make_async_copy(ref.ada, ref.f_ada, ref.osem.at[n]))
    stores[-1].start()
    ref.f_adab[...] = jnp.sum(total, axis=0)
    ref.f_cond[...] = dot(total, ref.adaw[...].astype(F32), NT, PRECISE)
    base = 4 * D // tile * S
    for c in range(D // tile):
        ref.f_downb[c * tile : (c + 1) * tile] = jnp.sum(
            tail[base + c * S : base + (c + 1) * S, :], axis=0
        )
    base += D // tile * S
    for c in range(F // tile):
        row = tail[pl.ds(base + y * (F // tile) + c, 1), :]
        ref.f_upb[c * tile : (c + 1) * tile] = row.reshape(tile)
    for c in stores:
        c.wait()


def shards(
    node_rows,
    noise_cond,
    sample_id,
    neighbours,
    ada_weight,
    ada_bias,
    query_weight,
    keyval_weight,
    out_weight,
    up_weight,
    up_bias,
    down_weight,
    down_bias,
    cotangent,
):
    rows, D = node_rows.shape
    F = up_weight.shape[1]
    S, cond = noise_cond.shape
    near = neighbours.shape[1]
    R, M = lax.axis_size("rows"), lax.axis_size("mlp")
    nz = R // 4
    G = rows // S
    W = 3 * G
    small = 16 * nz if 16 * nz > 88 else 128
    V, H = pltpu.VMEM, pl.ANY
    shape = jax.ShapeDtypeStruct
    arguments = dict(
        x=(node_rows, H),
        nc=(noise_cond, V),
        sid=(sample_id, pltpu.SMEM),
        nbr=(neighbours.T, V),
        adaw=(ada_weight, V),
        adab=(ada_bias, V),
        wq=(query_weight, H),
        wkv=(keyval_weight, H),
        wo=(out_weight, H),
        wup=(up_weight, H),
        bup=(up_bias, V),
        wdn=(down_weight, H),
        bdn=(down_bias, V),
        cot=(cotangent, H),
    )
    outputs = dict(
        o_layer=shape((rows, D), BF),
        o_rows=shape((rows, D), F32),
        o_q=shape((D, D), BF),
        o_k=shape((D, D), BF),
        o_v=shape((D, D), BF),
        o_out=shape((D, D), BF),
        o_up=shape((D, F), BF),
        o_dn=shape((F, D), BF),
        o_tail=shape((small, 256), F32),
    )
    scratch = dict(
        xb=V((3, rows, D), BF),
        cotn=V((rows, D), BF),
        wqkv=V((D, 3 * D), BF),
        wob=V((D, D), BF),
        wupb=V((M, D, F), BF),
        wdnb=V((M, F, D), BF),
        pm=V((rows, rows), BF),
        pt=V((rows, rows), BF),
        lws=V((rows + G, near), F32),
        lwt=V((3, S, near, 2 * G), BF),
        mod=V((S, 4 * D), F32),
        mods=V((S, 4 * D), F32),
        n1n=V((rows, D), BF),
        n1s=V((S, G, D), BF),
        pq=V((rows // 4, rows // 4), BF),
        xs=V((rows, D), BF),
        qkv=V((S, W, 3 * D), BF),
        cotb=V((rows, D), BF),
        cnt=V((S, W, 2 * G), F32),
        cntt=V((S, G, W), F32),
        mixs=V((rows, D), BF),
        mixx=V((rows, D), F32),
        prob=V((S * PAIRS, W, 2 * G), F32),
        ntb=V((rows, D), BF),
        mid=V((rows, D), F32),
        actb=V((M, rows, F), BF),
        ghb=V((M, rows, F), BF),
        bupg=V((M, 8, F), F32),
        upb=V((M, 8, F), F32),
        g2o=V((rows, D), F32),
        gmid=V((rows, D), F32),
        gmw=V((S, W, D), BF),
        stw=V((3, S, 8, 2 * G), F32),
        gmod=V((S, 4 * D), F32),
        gqkv=V((rows, 3 * D), BF),
        gdbs=V((S, D), F32),
        turn=V((D // 128, rows, 128), F32),
        tail=V((small, 256), F32),
        outr=V((rows, D), F32),
        outl=V((rows, D), BF),
    )
    sums = []
    wide = ((D, F), (F, D), (D, F), (F, D), *[(D, D)] * 4, (small, 256))
    for i, (n, c) in enumerate(wide):
        dtype = F32 if i == len(SUMS) - 1 else BF
        times = M - 1 if ROLES[i] == OTHERS else 1
        stage = (n * times, c // 2)
        out = V((8, 128) if ROLES[i] == OTHERS else (n, c), dtype)
        bufs = [out, V(stage, F32)] + [V(stage, dtype)] * 3
        if ROLES[i] == OWN:
            bufs.append(V((M - 1, n // (2 * nz), c // 2), dtype))
        elif ROLES[i] == PLAIN and 0 not in sharing(i, n, M, nz):
            bufs.append(V((M, n // (2 * nz), c // 2), dtype))
        sums.append(tuple(bufs))
    scratch.update(sums=tuple(sums))
    sem = pltpu.SemaphoreType.DMA
    for name, dims in dict(
        xsem=(2, 4),
        spsem=(2 * (M - 1) * (nz + 2),),
        ubsem=(M - 1,),
        lwsem=(2, 1),
        gmsem=(2, 4),
        stsem=(2, 4),
        sumsem=(len(SUMS) * Sum.slots(nz, M),),
    ).items():
        scratch[name] = (sem(dims), sem(dims))
    scratch.update(lsem=sem((7,)), wsem=sem((len(outputs),)))
    names = [*arguments, *outputs, *scratch]
    results = pl.pallas_call(
        functools.partial(kernel, (R, M, rows, D, F, S, near), names),
        out_shape=[*outputs.values()],
        in_specs=[pl.BlockSpec(memory_space=m) for _, m in arguments.values()],
        out_specs=[pl.BlockSpec(memory_space=H) for _ in outputs],
        scratch_shapes=[*scratch.values()],
        name="layer",
        compiler_params=pltpu.CompilerParams(
            collective_id=0, has_side_effects=True, vmem_limit_bytes=63 * 2**20
        ),
    )(*[a for a, _ in arguments.values()])
    got = dict(zip(outputs, results))
    inputs = dict(
        nc=(noise_cond, V),
        sid=(sample_id, pltpu.SMEM),
        adaw=(ada_weight, V),
        **{name: (value, H) for name, value in got.items()},
    )
    finals = dict(
        f_layer=shape((rows, D), BF),
        f_rows=shape((rows, D), F32),
        f_cond=shape((S, cond), F32),
        f_ada=shape((cond, 4 * D), F32),
        f_adab=shape((4 * D,), F32),
        f_q=shape((D, D), F32),
        f_kv=shape((D, 2 * D), F32),
        f_out=shape((D, D), F32),
        f_up=shape((D, F), F32),
        f_upb=shape((F,), F32),
        f_dn=shape((F, D), F32),
        f_downb=shape((D,), F32),
    )
    small_ones = ("f_cond", "f_adab", "f_upb", "f_downb")
    room = dict(
        inb=tuple(V(got[name].shape, BF) for name in WIDE),
        outb=tuple(V(got[name].shape, F32) for name in WIDE),
        tail=V((small, 256), F32),
        ada=V((cond, 4 * D), F32),
        layer=V((rows, D), BF),
        rows=V((rows, D), F32),
        gms=V((S, 4 * D), F32),
        isem=sem((len(WIDE) + 3,)),
        osem=sem((len(WIDE) + 3,)),
    )
    return pl.pallas_call(
        functools.partial(widen, (M, D, F, S), [*inputs, *finals, *room]),
        out_shape=[*finals.values()],
        in_specs=[pl.BlockSpec(memory_space=m) for _, m in inputs.values()],
        out_specs=[
            pl.BlockSpec(memory_space=V if name in small_ones else H) for name in finals
        ],
        scratch_shapes=[*room.values()],
        name="widen",
        compiler_params=pltpu.CompilerParams(vmem_limit_bytes=62 * 2**20),
    )(*[a for a, _ in inputs.values()])


def solution(mesh):
    both = P(("rows", "mlp"), None)
    placed = (
        both,
        P(),
        P(("rows", "mlp")),
        both,
        P(),
        P(),
        P(),
        P(),
        P(),
        P(None, "mlp"),
        P("mlp"),
        P("mlp", None),
        P(),
        both,
    )
    return jax.shard_map(
        shards,
        mesh=mesh,
        in_specs=placed,
        out_specs=(
            both,
            both,
            P(),
            P(),
            P(),
            P(),
            P(),
            P(),
            P(None, "mlp"),
            P("mlp"),
            P("mlp", None),
            P(),
        ),
        check_vma=False,
    )
```

```python
import functools
import math
from types import SimpleNamespace

import jax
import jax.numpy as jnp
from jax import lax
from jax.experimental import pallas as pl
from jax.experimental.pallas import tpu as pltpu
from jax.sharding import PartitionSpec as P

HEADS = 4
PAIRS = HEADS // 2
EPSILON = 1e-05
MESH = pl.DeviceIdType.MESH
F32, BF = jnp.float32, jnp.bfloat16
PRECISE = lax.Precision.HIGHEST
NN = (((1,), (0,)), ((), ()))
NT = (((1,), (1,)), ((), ()))
TN = (((0,), (0,)), ((), ()))
MASKED = -1e30


def dot(a, b, dims=NN, precision=None):
    return lax.dot_general(a, b, dims, precision=precision, preferred_element_type=F32)


def mean(v):
    return jnp.mean(v, axis=-1, keepdims=True)


def layer_norm(values):
    centred = values - mean(values)
    inverse = lax.rsqrt(mean(centred * centred) + EPSILON)
    return centred * inverse, inverse


def norm_back(grad, normed, inverse):
    return inverse * (grad - mean(grad) - normed * mean(grad * normed))


def iota(shape, axis):
    return lax.broadcasted_iota(jnp.int32, shape, axis)


def cut(start, size):
    return pl.ds(start if isinstance(start, int) else pl.multiple_of(start, size), size)


def loop(count, body):
    lax.fori_loop(0, count, lambda i, c: (body(i), c)[1], 0)


def remote(src, dst, sems, index, device):
    send, recv = sems
    return pltpu.make_async_remote_copy(
        src_ref=src,
        dst_ref=dst,
        send_sem=send.at[index],
        recv_sem=recv.at[index],
        device_id=device,
        device_id_type=MESH,
    )


def sizes(m, nz):
    return m, 2, nz, 2 * nz, 2, nz // 2


class Sum:
    def __init__(self, out, dtype, bufs, sems, base, place, order, role):
        self.out, self.dtype, self.sems, self.base = out, dtype, sems, base
        self.part, self.cs, self.cr, self.rr = bufs[:4]
        self.place = place
        self.order = order
        r, m, M, core, x, z, nz = place
        self.index = (m, x, z, x * nz + z, lax.rem(z, 2), z // 2)
        self.size = sizes(M, nz)
        self.role = role
        self.shares = sum(self.size[axis] - 1 for axis in order)
        self.last = self.shares if role == OTHERS else 2 * self.shares
        self.all_sum = role == PLAIN and 0 not in order
        self.back = order if role != OTHERS else ()
        self.mr = bufs[4] if len(bufs) > 4 else None
        self.width = self.part.shape[1]
        self.mine = cut(core * self.width, self.width)
        self.other = cut((1 - core) * self.width, self.width)
        self.start, self.length, self.stage = [0], [self.part.shape[0]], [0]
        for axis in order:
            length = self.length[-1] // self.size[axis]
            self.start.append(self.start[-1] + self.index[axis] * length)
            self.stage.append(self.stage[-1] + self.length[-1] - length)
            self.length.append(length)
        if role != OTHERS:
            self.begin, self.extent = [0], [out.shape[0]]
            for axis in order:
                self.extent.append(self.extent[-1] // self.size[axis])
                self.begin.append(self.begin[-1] + self.index[axis] * self.extent[-1])
        self.todo = [functools.partial(self.share, i) for i in range(len(order))]
        if role == OTHERS:
            self.todo.append(self.send_over)
            return
        if self.all_sum:
            self.todo.append(self.send_mlp)
        self.todo.append(self.settle)
        self.todo += [functools.partial(self.gather, i) for i in reversed(range(len(self.back)))]
        self.todo.append(self.gather_core)

    def step(self, count=1):
        for _ in range(min(count, len(self.todo))):
            self.todo.pop(0)()

    def peer(self, axis, t):
        r, m, M, core, x, z, nz = self.place
        if axis == 0:
            return r, lax.rem(m + t, M)
        if axis == 1:
            return z * 4 + (1 - x) * 2 + core, m
        if axis == 2:
            return lax.rem(z + t, nz) * 4 + x * 2 + core, m
        if axis == 4:
            return (z + 1 - 2 * lax.rem(z, 2)) * 4 + x * 2 + core, m
        if axis == 5:
            return lax.rem(z + 2 * t, nz) * 4 + x * 2 + core, m
        to = lax.rem(x * nz + z + t, 2 * nz)
        return lax.rem(to, nz) * 4 + to // nz * 2 + core, m

    def slot(self, phase, i, t):
        before = sum(self.size[axis] - 1 for axis in self.order[:i])
        return phase * self.shares + before + t - 1

    def copy(self, src, dst, slot, device):
        return remote(src, dst, self.sems, self.base + slot, device)

    def core_copy(self, phase):
        r, m, M, core, x, z, nz = self.place
        device = (z * 4 + x * 2 + 1 - core, m)
        slot = self.last + phase
        if phase == 0:
            return self.copy(self.cs, self.cr, slot, device)
        block = self.out.at[:, self.mine]
        return self.copy(block, block, slot, device)

    def share_copy(self, i, t):
        axis, length = self.order[i], self.length[i + 1]
        at = pl.ds(self.stage[i] + (t - 1) * length, length)
        return self.copy(
            self.cs.at[at], self.rr.at[at], self.slot(0, i, t), self.peer(axis, t)
        )

    def gather_copy(self, i, t):
        axis = self.back[i]
        block = self.out.at[cut(self.begin[i + 1], self.extent[i + 1]), self.mine]
        return self.copy(block, block, self.slot(1, i, t), self.peer(axis, t))

    def mlp_copy(self, t):
        r, m, M, core, x, z, nz = self.place
        block = self.mr.at[m]
        return self.copy(block, block, self.last + 1 + t, (r, lax.rem(m + t, M)))

    def core_send(self):
        self.core_copy(0).start()

    def take(self, i):
        if i == 0:
            self.core_copy(0).wait()
            return
        at = cut(self.start[i], self.length[i])
        value = self.part[at, :]
        for t in range(1, self.size[self.order[i - 1]]):
            self.share_copy(i - 1, t).wait_recv()
            here = pl.ds(self.stage[i - 1] + (t - 1) * self.length[i], self.length[i])
            value = value + self.rr[here, :].astype(F32)
        if i == 1:
            value = value + self.cr[at, :].astype(F32)
        self.part[at, :] = value

    def share(self, i):
        self.take(i)
        axis, length = self.order[i], self.length[i + 1]
        for t in range(1, self.size[axis]):
            block = lax.rem(self.index[axis] + t, self.size[axis])
            at = cut(self.start[i] + block * length, length)
            value = self.part[at, :]
            if i == 0:
                value = value + self.cr[at, :].astype(F32)
            self.cs[pl.ds(self.stage[i] + (t - 1) * length, length), :] = value.astype(self.dtype)
            self.share_copy(i, t).start()

    def send_mlp(self):
        n = len(self.order)
        self.take(n)
        r, m, M, core, x, z, nz = self.place
        self.mr[m] = self.part[cut(self.start[n], self.length[n]), :].astype(self.dtype)
        for t in range(1, M):
            self.mlp_copy(t).start()

    def over_copy(self, t):
        r, m, M, core, x, z, nz = self.place
        length = self.length[-1] // (M - 1)
        source = self.cs.at[pl.ds(self.stage[-1] + (t - 1) * length, length)]
        slot = self.last + t
        return self.copy(source, self.mate.mr.at[t - 1], slot, (r, lax.rem(m + t, M)))

    def send_over(self):
        n = len(self.order)
        self.take(n)
        value = self.part[cut(self.start[n], self.length[n]), :]
        self.cs[pl.ds(self.stage[n], self.length[n]), :] = value.astype(self.dtype)
        for t in range(1, self.size[0]):
            self.over_copy(t).start()

    def settle(self):
        n = len(self.order)
        at = cut(self.start[n], self.length[n])
        if self.all_sum:
            for t in range(1, self.size[0]):
                self.mlp_copy(t).wait_recv()
            value = self.mr[0].astype(F32)
            for t in range(1, self.size[0]):
                value = value + self.mr[t].astype(F32)
        else:
            self.take(n)
            value = self.part[at, :]
        if self.role == OWN:
            for t in range(1, self.size[0]):
                self.mate.over_copy(t).wait_recv()
                value = value + self.mr[t - 1].astype(F32)
        here = cut(self.begin[-1], self.extent[-1])
        self.out[here, self.mine] = value.astype(self.dtype)

    def gather(self, i):
        if i < len(self.back) - 1:
            for t in range(1, self.size[self.back[i + 1]]):
                self.gather_copy(i + 1, t).wait_recv()
        for t in range(1, self.size[self.back[i]]):
            self.gather_copy(i, t).start()

    def gather_core(self):
        for t in range(1, self.size[self.back[0]]):
            self.gather_copy(0, t).wait_recv()
        self.core_copy(1).start()

    def arrive(self):
        self.core_copy(1).wait_recv()

    def finish(self):
        assert not self.todo
        for i, axis in enumerate(self.order):
            for t in range(1, self.size[axis]):
                self.share_copy(i, t).wait_send()
        if self.role == OTHERS:
            for t in range(1, self.size[0]):
                self.over_copy(t).wait_send()
            return
        self.core_copy(1).wait_send()
        for i, axis in enumerate(self.back):
            for t in range(1, self.size[axis]):
                self.gather_copy(i, t).wait_send()
        if self.all_sum:
            for t in range(1, self.size[0]):
                self.mlp_copy(t).wait_send()

    @staticmethod
    def slots(order, role, nz, m):
        shares = sum(sizes(m, nz)[axis] - 1 for axis in order)
        if role == OTHERS:
            return shares + m
        return 2 * shares + 2 + (m - 1 if role == PLAIN and 0 not in order else 0)


class Spread:
    def __init__(self, source, parts, sems, base, place, sliced):
        self.source, self.parts, self.sems, self.base = source, parts, sems, base
        self.place, self.sliced = place, sliced
        r, m, M, core, x, z, nz = place
        _, rows, cols = parts.shape
        self.rows, width = rows, cols // 2
        self.mine = pl.ds(pl.multiple_of(core * width, width), width)
        piece = rows // (2 * nz)
        self.here = cut((x * nz + z) * piece, piece) if sliced else pl.ds(0, rows)
        self.each_peer = nz + 2 if sliced else 2

    def copies(self, stage, t):
        r, m, M, core, x, z, nz = self.place
        base = self.base + (t - 1) * self.each_peer
        if stage == 0:
            source = self.source.at[self.here, self.mine]
            target = self.parts.at[m, self.here, self.mine]
            return [remote(source, target, self.sems, base, (r, lax.rem(m + t, M)))]
        part = self.parts.at[lax.rem(m + M - t, M)]
        if stage == 1:
            block = part.at[self.here, self.mine]
            rows = [lax.rem(z + u, nz) * 4 + x * 2 + core for u in range(1, nz)]
        elif stage == 2:
            block = part.at[cut(x * (self.rows // 2), self.rows // 2), self.mine]
            rows = [z * 4 + (1 - x) * 2 + core]
        else:
            block = part.at[:, self.mine]
            rows = [z * 4 + x * 2 + 1 - core]
        first = base + ((0, 1, nz, nz + 1)[stage] if self.sliced else 1)
        return [
            remote(block, block, self.sems, first + i, (row, m)) for i, row in enumerate(rows)
        ]

    def stages(self):
        return (0, 1, 2, 3) if self.sliced else (0, 3)

    def each(self, stage):
        return [c for t in range(1, self.place[2]) for c in self.copies(stage, t)]

    def send(self, stage):
        before = [i for i in self.stages() if i < stage]
        if before:
            self.arrive(before[-1])
        for c in self.each(stage):
            c.start()

    def arrive(self, stage):
        for c in self.each(stage):
            c.wait_recv()

    def drain(self):
        for stage in self.stages():
            for c in self.each(stage):
                c.wait_send()


PLAIN, OWN, OTHERS = 0, 1, 2
SUMS = ("up", "down", "up2", "down2", "out", "query", "key", "value", "tail")
ROLES = (OWN, OWN, OTHERS, OTHERS, PLAIN, PLAIN, PLAIN, PLAIN, PLAIN)
FLAT = (1, 4, 5)
ORDERS = (FLAT, FLAT, FLAT, FLAT, (0, 1, 2), (0, 1, 2), (0, 1, 2), (0, 1, 2), (0, 3))


def sharing(i, rows, M, nz):
    if rows % (16 * 2 * nz * M) == 0 or (i == len(SUMS) - 1 and rows % (8 * 2 * nz * M) == 0):
        return ORDERS[i]
    return tuple(axis for axis in ORDERS[i] if axis != 0)


def kernel(static, names, *refs):
    ref = SimpleNamespace(**dict(zip(names, refs)))
    R, M, rows, D, F, S, near = static
    nz = R // 4
    G = rows // S
    W = 3 * G
    head = D // HEADS
    factor = 1.0 / math.sqrt(head)
    r, y = lax.axis_index("rows"), lax.axis_index("mlp")
    core, xi, z = lax.rem(r, 2), lax.rem(r // 2, 2), r // 4
    me = r * M + y
    devices = R * M
    pairs = M == 2
    up_row, down_row = lax.rem(r + 1, R), lax.rem(r + R - 1, R)
    after, before = lax.rem(me + 1, devices), lax.rem(me + devices - 1, devices)

    local = []
    lsem = ref.lsem
    for i, (src, dst) in enumerate(
        (
            (ref.x, ref.xb.at[1]),
            (ref.wq, ref.wqkv.at[:, 0:D]),
            (ref.wkv, ref.wqkv.at[:, D : 3 * D]),
            (ref.cot, ref.cotn),
            (ref.wo, ref.wob),
            (ref.wup, ref.wupb.at[y]),
            (ref.wdn, ref.wdnb.at[y]),
        )
    ):
        c = pltpu.make_async_copy(src, dst, lsem.at[i])
        c.start()
        local.append(c)

    barrier = pltpu.get_barrier_semaphore()
    others = [(r, lax.rem(y + t, M)) for t in range(1, M)]
    others.append((z * 4 + xi * 2 + 1 - core, y))
    for t in range(1, 2 * nz):
        to = lax.rem(xi * nz + z + t, 2 * nz)
        others.append((lax.rem(to, nz) * 4 + to // nz * 2 + core, y))
    if pairs:
        others += [(up_row, y), (down_row, y)]
    else:
        others += [(after // M, lax.rem(after, M)), (before // M, lax.rem(before, M))]
    for device in others:
        pl.semaphore_signal(barrier, inc=1, device_id=device, device_id_type=MESH)
    pl.semaphore_wait(barrier, len(others))

    def halo(source, at, sems):
        def first(k):
            if pairs:
                return [remote(source(k), at(2 * y, k), sems, (0, k), (r, 1 - y))]
            return [
                remote(source(k), at(0, k), sems, (0, k), (after // M, lax.rem(after, M))),
                remote(source(k), at(2, k), sems, (1, k), (before // M, lax.rem(before, M))),
            ]

        def second(k):
            if pairs:
                to = jnp.where(y == 0, up_row, down_row)
                return remote(at(2 * (1 - y), k), at(2 * y, k), sems, (1, k), (to, y))
            return first(k)[1]

        def send(k):
            for c in first(k):
                c.start()

        def pass_on(k):
            first(k)[0].wait_recv()
            if pairs:
                second(k).start()

        def arrive(k):
            second(k).wait_recv()

        def drain(k):
            first(k)[0].wait_send()
            second(k).wait_send()

        return send, pass_on, arrive, drain

    near_slot = 2 * (1 - y) if pairs else 0
    far_slot = 2 * y if pairs else 2
    xb = ref.xb
    quarter = rows // 4

    def part(k, n=quarter):
        return cut(k * n, n)

    x_send, x_pass, x_arrive, x_drain = halo(
        lambda k: ref.x.at[part(k)], lambda slot, k: xb.at[slot, part(k)], ref.xsem
    )
    loop(4, x_send)
    place_of = (r, y, M, core, xi, z, nz)
    spread = [
        Spread(source, parts, ref.spsem, i * (M - 1) * (nz + 2), place_of, i == 0)
        for i, (source, parts) in enumerate(((ref.wup, ref.wupb), (ref.wdn, ref.wdnb)))
    ]
    for part_of in spread:
        part_of.send(0)
    upb = ref.upb
    upb[y] = jnp.broadcast_to(ref.bup[...].astype(F32).reshape(1, F), (8, F))

    def bias_copy(t):
        return remote(upb.at[y], upb.at[y], ref.ubsem, t - 1, (r, lax.rem(y + t, M)))

    for t in range(1, M):
        bias_copy(t).start()

    def build(k):
        at = part(k)
        a, b = iota((quarter, rows), 0) + k * quarter, iota((quarter, rows), 1)
        ref.pm[at, :] = jnp.where(b == lax.rem(a, G) * S + a // G, 1.0, 0.0).astype(BF)
        ref.pt[at, :] = jnp.where(a == lax.rem(b, G) * S + b // G, 1.0, 0.0).astype(BF)

    loop(4, build)
    a, b = iota((quarter, quarter), 0), iota((quarter, quarter), 1)
    few = quarter // S
    ref.pq[...] = jnp.where(b == lax.rem(a, few) * S + a // few, 1.0, 0.0).astype(BF)
    pm, pt = ref.pm, ref.pt

    nodes = devices * G
    place = ref.nbr[...] // S - me * G + G
    place = jnp.where(place < 0, place + nodes, place)
    place = jnp.where(place >= nodes, place - nodes, place)
    place = place.astype(F32).astype(BF)
    lws = ref.lws
    lws[rows : rows + G, :] = jnp.zeros((G, near), F32)
    lws[0:rows, :] = dot(pm[...], place, NT)
    lwt = ref.lwt
    eye = jnp.where(iota((near, near), 0) == iota((near, near), 1), 1.0, 0.0).astype(BF)

    def turn(s):
        block = lws[pl.ds(pl.multiple_of(s * G, G), 2 * G), :].astype(BF)
        lwt[1, s] = dot(eye, block, NT).astype(BF)

    loop(S, turn)
    l_send, l_pass, l_arrive, l_drain = halo(
        lambda k: lwt.at[1], lambda slot, k: lwt.at[slot], ref.lwsem
    )
    l_send(0)

    modulation = dot(ref.nc[...], ref.adaw[...]) + ref.adab[...].astype(F32).reshape(1, 4 * D)
    ref.mod[...] = modulation
    mods = ref.mods
    for s in range(S):
        mods[s : s + 1, :] = ref.mod[pl.ds(ref.sid[s], 1), :]

    n1w, qkv = ref.n1w, ref.qkv
    wqkv = ref.wqkv

    turn16 = quarter // S

    def norm_block(slot, k):
        at = part(k)
        normed, _ = layer_norm(xb[slot, at, :].astype(F32))
        scaled = normed.reshape(turn16, S, D) * (1.0 + mods[:, 0:D])[None]
        scaled = scaled + mods[:, D : 2 * D][None]
        ordered = dot(ref.pq[...], scaled.reshape(quarter, D).astype(BF)).astype(BF)
        wide = dot(ordered, wqkv[...]).astype(BF).reshape(S, turn16, 3 * D)
        here = cut(slot * G + k * turn16, turn16)
        qkv[:, here, :] = wide
        n1w[:, here, :] = ordered.reshape(S, turn16, D)

    local[0].wait()
    local[1].wait()
    local[2].wait()

    loop(4, lambda k: norm_block(1, k))
    local[3].wait()
    xs, cotb = ref.xs, ref.cotb

    def order(k):
        xs[part(k), :] = dot(pm[part(k), :], xb[1]).astype(BF)
        cotb[part(k), :] = dot(pm[part(k), :], ref.cotn[...]).astype(BF)

    loop(4, order)

    cnt, cntt = ref.cnt, ref.cntt

    def count(s):
        block = lwt[1, s].astype(F32)
        block = jnp.where(iota((near, 2 * G), 1) < G, block, pltpu.roll(block, G, 1))
        key = iota((W, 2 * G), 0).astype(F32)
        total = jnp.zeros((W, 2 * G), F32)
        for j in range(near):
            total = total + jnp.where(block[j : j + 1, :] == key, 1.0, 0.0)
        cnt[s] = total

    loop(S, count)

    def near_norm(k):
        x_pass(k)
        norm_block(near_slot, k)

    loop(4, near_norm)


    def far_norm(k):
        x_arrive(k)
        norm_block(far_slot, k)

        @pl.when(k == 1)
        def _():
            spread[0].send(1)

    loop(4, far_norm)

    mixs, mixx, prob, stw = ref.mixs, ref.mixx, ref.prob, ref.stw
    ntb, mid = ref.ntb, ref.mid
    pair = 2 * head

    def apart(block):
        nothing = jnp.zeros((block.shape[0], head), block.dtype)
        left = jnp.concatenate([block[:, 0:head], nothing], axis=1)
        right = jnp.concatenate([nothing, block[:, head:pair]], axis=1)
        return jnp.concatenate([left, right], axis=0)

    def attend(k):
        for s2 in range(2):
            s = 2 * k + s2
            at = cut(s * G, G)
            times = cnt[s]
            logs = []
            for p in range(PAIRS):
                lo, hi = p * pair, (p + 1) * pair
                queries = apart(qkv[s, G : 2 * G, lo:hi])
                scores = dot(qkv[s, :, D + lo : D + hi], queries, NT) * factor
                scores = jnp.where(times > 0.0, scores, MASKED)
                top = jnp.max(scores, axis=0, keepdims=True)
                power = jnp.exp(scores - top)
                total = jnp.sum(power * times, axis=0, keepdims=True)
                probs = power * (1.0 / total)
                prob[s * PAIRS + p] = probs
                weight = (times * probs.astype(BF).astype(F32)).astype(BF)
                rest = (times * probs - weight.astype(F32)).astype(BF)
                both = jnp.concatenate([weight, rest], axis=1)
                mixed = dot(both, qkv[s, :, 2 * D + lo : 2 * D + hi], TN)
                one, two = mixed[0:G, 0:head], mixed[G : 2 * G, head:pair]
                mixs[at, lo : lo + head] = one.astype(BF)
                mixs[at, lo + head : hi] = two.astype(BF)
                mixx[at, lo : lo + head] = one + mixed[2 * G : 3 * G, 0:head]
                mixx[at, lo + head : hi] = two + mixed[3 * G : 4 * G, head:pair]
                logs.append(top + jnp.log(total))
            logs.append(jnp.zeros((8 - PAIRS, 2 * G), F32))
            stw[1, s] = jnp.concatenate(logs, axis=0)

    loop(4, attend)

    local[4].wait()
    wo = ref.wob
    half = rows // 2
    group = half // G

    def mix_out(c):
        at = part(c, half)
        middle = xs[at, :].astype(F32) + dot(mixs[at, :], wo[...])
        mid[at, :] = middle
        normed, _ = layer_norm(middle)
        for i in range(group):
            lo = i * G
            scale = mods[pl.ds(c * group + i, 1), 2 * D : 3 * D]
            shift = mods[pl.ds(c * group + i, 1), 3 * D : 4 * D]
            here = cut(c * half + lo, G)
            ntb[here, :] = (normed[lo : lo + G] * (1.0 + scale) + shift).astype(BF)

    loop(2, mix_out)

    local[5].wait()
    local[6].wait()
    spread[0].send(2)
    wup, wdn, actb, ghb = ref.wupb, ref.wdnb, ref.actb, ref.ghb
    bupg, g2o = ref.bupg, ref.g2o
    bupg[...] = jnp.zeros_like(bupg)
    g2o[...] = jnp.zeros_like(g2o)
    tile = 256

    def feed(p):
        def column(f):
            cols = part(f, tile)
            hidden = dot(ntb[...], wup[p, :, cols]) + upb[p, 0:1, cols]
            gate = jax.nn.sigmoid(hidden)
            active = hidden * gate
            actb[p, :, cols] = active.astype(BF)
            grad = dot(cotb[...], wdn[p, cols, :], NT)
            grad = (grad * (gate + active * (1.0 - gate))).astype(BF)
            ghb[p, :, cols] = grad
            bupg[p, 0:1, cols] += jnp.sum(grad.astype(F32), axis=0, keepdims=True)

        loop(F // tile, column)
        for q in range(D // tile):
            lo, hi = q * tile, (q + 1) * tile
            g2o[:, lo:hi] += dot(ghb[p], wup[p, lo:hi, :], NT)

    feed(y)

    base = 0
    sums = SimpleNamespace()
    written = []

    def write(source, result):
        c = pltpu.make_async_copy(source, result, ref.wsem.at[len(written)])
        c.start()
        written.append(c)

    for i, (name, bufs) in enumerate(zip(SUMS, ref.sums)):
        out, *bufs = bufs
        dtype = F32 if i == len(SUMS) - 1 else BF
        order = sharing(i, bufs[0].shape[0], M, nz)
        total = Sum(out, dtype, bufs, ref.sumsem, base, place_of, order, ROLES[i])
        base += Sum.slots(order, ROLES[i], nz, M)
        setattr(sums, name, total)
    sums.up.mate, sums.down.mate, sums.up2.mate, sums.down2.mate = (
        sums.up2,
        sums.down2,
        sums.up,
        sums.down,
    )

    def weight_grad(total, left, right):
        width = total.width
        for out, start, kind in (
            (total.cs, (1 - core) * width, BF),
            (total.part, core * width, F32),
        ):
            at = cut(start, width)
            out[...] = dot(left, right(at), TN).astype(kind)
            if kind == BF:
                total.core_send()

    def ffn_grad(total, count, which, rows_of, left, right):
        width = total.width
        many, block = min(rows_of, 512), rows_of // (2 * nz)
        for out, start, kind in (
            (total.cs, (1 - core) * width, BF),
            (total.part, core * width, F32),
        ):
            at = cut(start, width)

            def tile_row(i):
                u, f = i // (rows_of // many), lax.rem(i, rows_of // many)
                p = which(u)
                value = dot(left(p, part(f, many)), right(p, at), TN).astype(kind)
                if count == 1:
                    out[part(f, many), :] = value
                    return
                for v in range(many // block):
                    row = ((f * (many // block) + v) * count + u) * block
                    here = cut(row, block)
                    out[here, :] = value[v * block : (v + 1) * block]

            loop(count * rows_of // many, tile_row)
            if kind == BF:
                total.core_send()

    def up_grad(total, count, which):
        ffn_grad(total, count, which, D, lambda p, f: ntb[:, f], lambda p, at: ghb[p, :, at])

    def down_grad(total, count, which):
        ffn_grad(total, count, which, F, lambda p, f: actb[p, :, f], lambda p, at: cotb[:, at])

    l_pass(0)
    up_grad(sums.up, 1, lambda u: y)
    down_grad(sums.down, 1, lambda u: y)
    sums.up.step()
    sums.down.step()

    def feed_other(t):
        @pl.when(t == 0)
        def _():
            spread[0].send(3)
            spread[1].send(3)
            spread[0].arrive(3)
            spread[1].arrive(3)
            for u in range(1, M):
                bias_copy(u).wait_recv()

        feed(lax.rem(y + t + 1, M))

    loop(M - 1, feed_other)

    gmid, gmw, gatt, gmod = ref.gmid, ref.gmw, ref.cotn, ref.gmod
    row, lane = iota((8, D), 0), iota((8, D), 1) // head
    pick_one = jnp.where((row >= PAIRS) & (lane == 2 * (row - PAIRS)), 1.0, 0.0)
    pick_two = jnp.where((row >= PAIRS) & (lane == 2 * (row - PAIRS) + 1), 1.0, 0.0)
    m_send, m_pass, m_arrive, m_drain = halo(
        lambda k: gmw.at[pl.ds(2 * k, 2), pl.ds(G, G)],
        lambda slot, k: gmw.at[pl.ds(2 * k, 2), cut(slot * G, G)],
        ref.gmsem,
    )
    s_send, s_pass, s_arrive, s_drain = halo(
        lambda k: stw.at[1, pl.ds(2 * k, 2)],
        lambda slot, k: stw.at[slot, pl.ds(2 * k, 2)],
        ref.stsem,
    )

    def middle_back(c):
        at = part(c, half)
        grad = g2o[at, :]
        normed, inverse = layer_norm(mid[at, :])
        weighted = []
        for i in range(group):
            s = c * group + i
            lo, hi = i * G, (i + 1) * G
            scale = mods[pl.ds(s, 1), 2 * D : 3 * D]
            weighted.append(grad[lo:hi] * (1.0 + scale))
            gmod[pl.ds(s, 1), 2 * D : 3 * D] = jnp.sum(
                grad[lo:hi] * normed[lo:hi], axis=0, keepdims=True
            )
            gmod[pl.ds(s, 1), 3 * D : 4 * D] = jnp.sum(grad[lo:hi], axis=0, keepdims=True)
        weighted = jnp.concatenate(weighted, axis=0)
        middle = cotb[at, :].astype(F32) + norm_back(weighted, normed, inverse)
        gmid[at, :] = middle
        rounded = middle.astype(BF)
        gatt[at, :] = rounded
        mixture = dot(rounded, wo[...], NT).astype(BF)
        gmw[pl.ds(c * group, group), G : 2 * G, :] = mixture.reshape(group, G, D)
        product = mixture.astype(F32) * mixx[at, :]
        ones = dot(pick_one, product, NT, PRECISE)
        twos = dot(pick_two, product, NT, PRECISE)
        first_lanes = iota((8, 2 * G), 1) < G
        for g in range(group // 2):
            lo, hi = g * 2 * G, (g + 1) * 2 * G
            one, two = ones[:, lo:hi], twos[:, lo:hi]
            s = c * group + 2 * g
            stw[1, s] += jnp.where(first_lanes, one, pltpu.roll(two, G, 1))
            stw[1, s + 1] += jnp.where(first_lanes, pltpu.roll(one, G, 1), two)
        for k in range(2):
            m_send(2 * c + k)
            s_send(2 * c + k)

    def pass_on(k):
        m_pass(k)
        s_pass(k)

    def other_part(u):
        return lax.rem(y + u + 1, M)

    gqkv, gkvw = ref.gqkv, ref.gkvw

    def query_back(s):
        at = cut(s * G, G)
        times = cnt[s]
        for p in range(PAIRS):
            lo, hi = p * pair, (p + 1) * pair
            grads = apart(gmw[s, G : 2 * G, lo:hi])
            gprob = dot(qkv[s, :, 2 * D + lo : 2 * D + hi], grads, NT)
            gscore = prob[s * PAIRS + p] * (gprob - stw[1, s, PAIRS + p : PAIRS + p + 1, :])
            weight = (times * gscore.astype(BF).astype(F32)).astype(BF)
            gquery = dot(weight, qkv[s, :, D + lo : D + hi], TN) * factor
            gqkv[at, lo : lo + head] = gquery[0:G, 0:head].astype(BF)
            gqkv[at, lo + head : hi] = gquery[G : 2 * G, head:pair].astype(BF)
            queries = apart(qkv[s, G : 2 * G, lo:hi])
            gkvw[s, :, lo:hi] = (dot(weight, queries) * factor).astype(BF)
            weight = (times * prob[s * PAIRS + p].astype(BF).astype(F32)).astype(BF)
            gkvw[s, :, D + lo : D + hi] = dot(weight, grads).astype(BF)


    def count_back(s):
        shift = [2 * G, G, 0]
        block = jnp.concatenate(
            [lwt[b, s][:, 0:G].astype(F32) - float(shift[b]) for b in range(3)], axis=1
        ).astype(jnp.int32)
        key = iota((G, W), 0)
        total = jnp.zeros((G, W), F32)
        for j in range(near):
            total = total + jnp.where(block[j : j + 1, :] == key, 1.0, 0.0)
        cntt[s] = total

    def finish_out(k):
        at = part(k)
        value = mid[at, :] + ref.bdn[...].astype(F32).reshape(1, D)
        for p in range(M):
            value = value + dot(actb[p, at, :], wdn[p])
        ref.n1n[at, :] = value.astype(BF)


    def key_back(s):
        at = cut(s * G, G)
        times = cntt[s]
        stats = [
            jnp.concatenate([stw[b, s][:, i * G : (i + 1) * G] for b in range(3)], axis=1)
            for i in range(2)
        ]
        for p in range(PAIRS):
            lo, hi = p * pair, (p + 1) * pair
            queries, grads = qkv[s, :, lo:hi], gmw[s, :, lo:hi]
            scores = dot(apart(qkv[s, G : 2 * G, D + lo : D + hi]), queries, NT) * factor
            gprob = dot(apart(qkv[s, G : 2 * G, 2 * D + lo : 2 * D + hi]), grads, NT)
            gscores, weights = [], []
            for i in range(2):
                rows_of = slice(i * G, (i + 1) * G)
                log, delta = stats[i][p : p + 1], stats[i][PAIRS + p : PAIRS + p + 1]
                probs = jnp.exp(jnp.where(times > 0.0, scores[rows_of] - log, MASKED))
                gscore = probs * (gprob[rows_of] - delta)
                gscores.append((times * gscore.astype(BF).astype(F32)).astype(BF))
                weights.append((times * probs.astype(BF).astype(F32)).astype(BF))
            gkey = dot(jnp.concatenate(gscores, axis=0), queries) * factor
            gvalue = dot(jnp.concatenate(weights, axis=0), grads)
            for i in range(2):
                cols = pl.ds(D + lo + i * head, head)
                gqkv[at, cols] = gkey[i * G : (i + 1) * G, i * head : (i + 1) * head].astype(BF)
                cols = pl.ds(2 * D + lo + i * head, head)
                gqkv[at, cols] = gvalue[i * G : (i + 1) * G, i * head : (i + 1) * head].astype(BF)


    gdbs = ref.gdbs
    out_rows = ref.outr

    def first_back(c):
        at = part(c, half)
        grad = dot(gqkv[at, :], wqkv[...], NT)
        normed, inverse = layer_norm(xs[at, :].astype(F32))
        weighted = []
        for i in range(group):
            s = c * group + i
            lo, hi = i * G, (i + 1) * G
            here = cut(s * G, G)
            gmod[pl.ds(s, 1), 0:D] = jnp.sum(grad[lo:hi] * normed[lo:hi], axis=0, keepdims=True)
            gmod[pl.ds(s, 1), D : 2 * D] = jnp.sum(grad[lo:hi], axis=0, keepdims=True)
            gdbs[pl.ds(s, 1), :] = jnp.sum(cotb[here, :].astype(F32), axis=0, keepdims=True)
            weighted.append(grad[lo:hi] * (1.0 + mods[pl.ds(s, 1), 0:D]))
        weighted = jnp.concatenate(weighted, axis=0)
        g2o[at, :] = gmid[at, :] + norm_back(weighted, normed, inverse)

    tail = ref.tail
    base = 4 * D // tile * S
    base_up = base + D // tile * S

    def pack_tail():
        tail[...] = jnp.zeros_like(tail)
        for c in range(4 * D // tile):
            tail[c * S : (c + 1) * S, :] = gmod[:, c * tile : (c + 1) * tile]
        for c in range(D // tile):
            tail[base + c * S : base + (c + 1) * S, :] = gdbs[:, c * tile : (c + 1) * tile]
        for c in range(F // tile):
            for p in range(M):
                row = base_up + p * (F // tile) + c
                tail[row : row + 1, :] = bupg[p, 0:1, c * tile : (c + 1) * tile]
        sums.tail.cs[...] = tail[:, sums.tail.other]
        sums.tail.part[...] = tail[:, sums.tail.mine]
        sums.tail.core_send()

    def rows_back():
        for c in range(D // 128):
            lo, hi = c * 128, (c + 1) * 128
            for s in range(S):
                ref.turn[c, pl.ds(s, G, stride=S), :] = g2o[s * G : (s + 1) * G, lo:hi]
            out_rows[:, lo:hi] = ref.turn[c]
        write(out_rows, ref.o_rows)

    def order_back(k):
        ref.outl[part(k), :] = dot(pt[part(k), :], ref.n1n[...]).astype(BF)


    def drain():
        loop(4, x_drain)
        l_drain(0)
        loop(4, m_drain)
        loop(4, s_drain)
        for part_of in spread:
            part_of.drain()
        for t in range(1, M):
            bias_copy(t).wait_send()
        sums.up2.finish()
        sums.down2.finish()

    def out_grad():
        weight_grad(sums.out, mixs[...], lambda at: gatt[:, at])

    def query_grad():
        weight_grad(sums.query, n1w[:, G : 2 * G, :].reshape(rows, D), lambda at: gqkv[:, at])

    def window_grad(total, shares):
        left = n1w[...].reshape(S * W, D)
        weight_grad(total, left, lambda at: shares[:, :, at].reshape(S * W, at.size))

    def key_grad():
        window_grad(sums.key, gkvw.at[:, :, 0:D])

    def value_grad():
        window_grad(sums.value, gkvw.at[:, :, D : 2 * D])

    def queries_of(k):
        query_back(2 * k)
        query_back(2 * k + 1)

    def keys_of(k):
        m_arrive(k)
        s_arrive(k)
        key_back(2 * k)
        key_back(2 * k + 1)

    def counts():
        l_arrive(0)
        loop(S, count_back)

    def layer_out():
        loop(4, finish_out)

    def layer_order():
        loop(4, order_back)
        write(ref.outl, ref.o_layer)

    sums.up.step()
    up_grad(sums.up2, M - 1, other_part)
    down_grad(sums.down2, M - 1, other_part)
    sums.up2.step()
    middle_back(0)
    sums.up.step()
    sums.down.step()
    sums.down2.step()
    middle_back(1)
    out_grad()
    sums.out.step()
    queries_of(0)
    sums.down.step()
    queries_of(1)
    sums.up2.step()
    queries_of(2)
    queries_of(3)
    pass_on(0)
    pass_on(1)
    query_grad()
    sums.query.step()
    sums.up2.step()
    key_grad()
    sums.key.step()
    pass_on(2)
    sums.down2.step()
    value_grad()
    sums.value.step()
    pass_on(3)
    counts()
    sums.down2.step()
    layer_out()
    sums.out.step()
    sums.up2.step()
    keys_of(0)
    keys_of(1)
    sums.query.step()
    keys_of(2)
    keys_of(3)
    sums.out.step()
    sums.key.step()
    first_back(0)
    sums.query.step()
    sums.down2.step()
    first_back(1)
    pack_tail()
    sums.up.step(2)
    sums.value.step()
    rows_back()
    layer_order()
    sums.tail.step()
    sums.key.step()
    sums.out.step(2)
    sums.query.step(2)
    sums.value.step()
    sums.key.step(2)
    sums.tail.step()
    sums.down.step(2)
    sums.up.step()
    sums.out.step()
    sums.query.step()
    sums.value.step()
    sums.tail.step()
    sums.value.step()
    sums.up.step()
    sums.key.step()
    sums.out.step()
    sums.tail.step()
    sums.query.step()
    sums.down.step()
    sums.value.step()
    sums.up.step()
    sums.key.step()
    sums.out.step()
    sums.tail.step()
    sums.query.step()
    sums.value.step()
    sums.down.step()
    sums.key.step()
    drain()
    sums.value.step()
    sums.tail.step()
    sums.down.step()
    late = (sums.up, sums.out, sums.query, sums.key, sums.value, sums.tail, sums.down)
    results = (ref.o_up, ref.o_out, ref.o_q, ref.o_k, ref.o_v, ref.o_tail, ref.o_dn)
    for total, result in zip(late, results):
        while total.todo:
            total.step()
        total.arrive()
        write(total.out, result)
    for total in late:
        total.finish()
    for c in written:
        c.wait()


WIDE = ("o_up", "o_dn", "o_out", "o_q", "o_k", "o_v")


def widen(static, names, *refs):
    ref = SimpleNamespace(**dict(zip(names, refs)))
    M, D, F, S = static
    tile = 256
    y = lax.axis_index("mlp")
    sources = (ref.o_up, ref.o_dn, ref.o_out, ref.o_q, ref.o_k, ref.o_v)
    targets = (
        ref.f_up,
        ref.f_dn,
        ref.f_out,
        ref.f_q,
        ref.f_kv.at[:, 0:D],
        ref.f_kv.at[:, D : 2 * D],
    )
    n = len(sources)
    straight = ((ref.o_rows, ref.rows, ref.f_rows), (ref.o_layer, ref.layer, ref.f_layer))
    passing = []
    for i, (source, middle, target) in enumerate(straight):
        load = pltpu.make_async_copy(source, middle, ref.isem.at[n + 1 + i])
        passing.append((load, pltpu.make_async_copy(middle, target, ref.osem.at[n + 1 + i])))
        load.start()
    loads = [
        pltpu.make_async_copy(source, ref.inb[i], ref.isem.at[i])
        for i, source in enumerate(sources)
    ]
    tail_in = pltpu.make_async_copy(ref.o_tail, ref.tail, ref.isem.at[n])
    loads[0].start()
    loads[1].start()
    tail_in.start()
    for load in loads[2:]:
        load.start()
    stores = []

    def store(copy):
        copy.start()
        stores.append(copy)

    for load, out in passing:
        load.wait()
        store(out)

    def convert(i):
        loads[i].wait()
        at_once = 128

        def part(k):
            at = cut(k * at_once, at_once)
            ref.outb[i][at, :] = ref.inb[i][at, :].astype(F32)

        loop(sources[i].shape[0] // at_once, part)
        store(pltpu.make_async_copy(ref.outb[i], targets[i], ref.osem.at[i]))

    convert(0)
    convert(1)
    tail_in.wait()
    tail, gms = ref.tail, ref.gms
    pick = jnp.zeros((S, S), F32)
    for s in range(S):
        hit = (iota((S, S), 1) == s) & (iota((S, S), 0) == ref.sid[s])
        pick = pick + jnp.where(hit, 1.0, 0.0)
    for c in range(4 * D // tile):
        gms[:, c * tile : (c + 1) * tile] = dot(pick, tail[c * S : (c + 1) * S, :], NN, PRECISE)
    total = gms[...]
    ref.ada[...] = dot(ref.nc[...].astype(F32), total, TN, PRECISE)
    store(pltpu.make_async_copy(ref.ada, ref.f_ada, ref.osem.at[n]))
    for i in range(2, n):
        convert(i)
    ref.f_adab[...] = jnp.sum(total, axis=0)
    ref.f_cond[...] = dot(total, ref.adaw[...].astype(F32), NT, PRECISE)
    base = 4 * D // tile * S
    for c in range(D // tile):
        ref.f_downb[c * tile : (c + 1) * tile] = jnp.sum(
            tail[base + c * S : base + (c + 1) * S, :], axis=0
        )
    base += D // tile * S
    for c in range(F // tile):
        row = tail[pl.ds(base + y * (F // tile) + c, 1), :]
        ref.f_upb[c * tile : (c + 1) * tile] = row.reshape(tile)
    for c in stores:
        c.wait()


def shards(
    node_rows,
    noise_cond,
    sample_id,
    neighbours,
    ada_weight,
    ada_bias,
    query_weight,
    keyval_weight,
    out_weight,
    up_weight,
    up_bias,
    down_weight,
    down_bias,
    cotangent,
):
    rows, D = node_rows.shape
    F = up_weight.shape[1]
    S, cond = noise_cond.shape
    near = neighbours.shape[1]
    R, M = lax.axis_size("rows"), lax.axis_size("mlp")
    nz = R // 4
    G = rows // S
    W = 3 * G
    small = 16 * nz if 16 * nz > 88 else 128
    V, H = pltpu.VMEM, pl.ANY
    shape = jax.ShapeDtypeStruct
    arguments = dict(
        x=(node_rows, H),
        nc=(noise_cond, V),
        sid=(sample_id, pltpu.SMEM),
        nbr=(neighbours.T, V),
        adaw=(ada_weight, V),
        adab=(ada_bias, V),
        wq=(query_weight, H),
        wkv=(keyval_weight, H),
        wo=(out_weight, H),
        wup=(up_weight, H),
        bup=(up_bias, V),
        wdn=(down_weight, H),
        bdn=(down_bias, V),
        cot=(cotangent, H),
    )
    outputs = dict(
        o_layer=shape((rows, D), BF),
        o_rows=shape((rows, D), F32),
        o_q=shape((D, D), BF),
        o_k=shape((D, D), BF),
        o_v=shape((D, D), BF),
        o_out=shape((D, D), BF),
        o_up=shape((D, F), BF),
        o_dn=shape((F, D), BF),
        o_tail=shape((small, 256), F32),
    )
    scratch = dict(
        xb=V((3, rows, D), BF),
        cotn=V((rows, D), BF),
        wqkv=V((D, 3 * D), BF),
        wob=V((D, D), BF),
        wupb=V((M, D, F), BF),
        wdnb=V((M, F, D), BF),
        pm=V((rows, rows), BF),
        pt=V((rows, rows), BF),
        lws=V((rows + G, near), F32),
        lwt=V((3, S, near, 2 * G), BF),
        mod=V((S, 4 * D), F32),
        mods=V((S, 4 * D), F32),
        n1n=V((rows, D), BF),
        n1w=V((S, W, D), BF),
        gkvw=V((S, W, 2 * D), BF),
        pq=V((rows // 4, rows // 4), BF),
        xs=V((rows, D), BF),
        qkv=V((S, W, 3 * D), BF),
        cotb=V((rows, D), BF),
        cnt=V((S, W, 2 * G), F32),
        cntt=V((S, G, W), F32),
        mixs=V((rows, D), BF),
        mixx=V((rows, D), F32),
        prob=V((S * PAIRS, W, 2 * G), F32),
        ntb=V((rows, D), BF),
        mid=V((rows, D), F32),
        actb=V((M, rows, F), BF),
        ghb=V((M, rows, F), BF),
        bupg=V((M, 8, F), F32),
        upb=V((M, 8, F), F32),
        g2o=V((rows, D), F32),
        gmid=V((rows, D), F32),
        gmw=V((S, W, D), BF),
        stw=V((3, S, 8, 2 * G), F32),
        gmod=V((S, 4 * D), F32),
        gqkv=V((rows, 3 * D), BF),
        gdbs=V((S, D), F32),
        turn=V((D // 128, rows, 128), F32),
        tail=V((small, 256), F32),
        outr=V((rows, D), F32),
        outl=V((rows, D), BF),
    )
    sums = []
    wide = ((D, F), (F, D), (D, F), (F, D), *[(D, D)] * 4, (small, 256))
    count = 0
    for i, (n, c) in enumerate(wide):
        dtype = F32 if i == len(SUMS) - 1 else BF
        times = M - 1 if ROLES[i] == OTHERS else 1
        stage = (n * times, c // 2)
        count += Sum.slots(sharing(i, n * times, M, nz), ROLES[i], nz, M)
        out = V((8, 128) if ROLES[i] == OTHERS else (n, c), dtype)
        bufs = [out, V(stage, F32)] + [V(stage, dtype)] * 3
        if ROLES[i] == OWN:
            bufs.append(V((M - 1, n // (2 * nz), c // 2), dtype))
        elif ROLES[i] == PLAIN and 0 not in sharing(i, n, M, nz):
            bufs.append(V((M, n // (2 * nz), c // 2), dtype))
        sums.append(tuple(bufs))
    scratch.update(sums=tuple(sums))
    sem = pltpu.SemaphoreType.DMA
    for name, dims in dict(
        xsem=(2, 4),
        spsem=(2 * (M - 1) * (nz + 2),),
        ubsem=(M - 1,),
        lwsem=(2, 1),
        gmsem=(2, 4),
        stsem=(2, 4),
        sumsem=(count,),
    ).items():
        scratch[name] = (sem(dims), sem(dims))
    scratch.update(lsem=sem((7,)), wsem=sem((len(outputs),)))
    names = [*arguments, *outputs, *scratch]
    results = pl.pallas_call(
        functools.partial(kernel, (R, M, rows, D, F, S, near), names),
        out_shape=[*outputs.values()],
        in_specs=[pl.BlockSpec(memory_space=m) for _, m in arguments.values()],
        out_specs=[pl.BlockSpec(memory_space=H) for _ in outputs],
        scratch_shapes=[*scratch.values()],
        name="layer",
        compiler_params=pltpu.CompilerParams(
            collective_id=0, has_side_effects=True, vmem_limit_bytes=63 * 2**20
        ),
    )(*[a for a, _ in arguments.values()])
    got = dict(zip(outputs, results))
    inputs = dict(
        nc=(noise_cond, V),
        sid=(sample_id, pltpu.SMEM),
        adaw=(ada_weight, V),
        **{name: (value, H) for name, value in got.items()},
    )
    finals = dict(
        f_layer=shape((rows, D), BF),
        f_rows=shape((rows, D), F32),
        f_cond=shape((S, cond), F32),
        f_ada=shape((cond, 4 * D), F32),
        f_adab=shape((4 * D,), F32),
        f_q=shape((D, D), F32),
        f_kv=shape((D, 2 * D), F32),
        f_out=shape((D, D), F32),
        f_up=shape((D, F), F32),
        f_upb=shape((F,), F32),
        f_dn=shape((F, D), F32),
        f_downb=shape((D,), F32),
    )
    small_ones = ("f_cond", "f_adab", "f_upb", "f_downb")
    room = dict(
        inb=tuple(V(got[name].shape, BF) for name in WIDE),
        outb=tuple(V(got[name].shape, F32) for name in WIDE),
        tail=V((small, 256), F32),
        ada=V((cond, 4 * D), F32),
        layer=V((rows, D), BF),
        rows=V((rows, D), F32),
        gms=V((S, 4 * D), F32),
        isem=sem((len(WIDE) + 3,)),
        osem=sem((len(WIDE) + 3,)),
    )
    return pl.pallas_call(
        functools.partial(widen, (M, D, F, S), [*inputs, *finals, *room]),
        out_shape=[*finals.values()],
        in_specs=[pl.BlockSpec(memory_space=m) for _, m in inputs.values()],
        out_specs=[
            pl.BlockSpec(memory_space=V if name in small_ones else H) for name in finals
        ],
        scratch_shapes=[*room.values()],
        name="widen",
        compiler_params=pltpu.CompilerParams(vmem_limit_bytes=62 * 2**20),
    )(*[a for a, _ in inputs.values()])


def solution(mesh):
    both = P(("rows", "mlp"), None)
    placed = (
        both,
        P(),
        P(("rows", "mlp")),
        both,
        P(),
        P(),
        P(),
        P(),
        P(),
        P(None, "mlp"),
        P("mlp"),
        P("mlp", None),
        P(),
        both,
    )
    return jax.shard_map(
        shards,
        mesh=mesh,
        in_specs=placed,
        out_specs=(
            both,
            both,
            P(),
            P(),
            P(),
            P(),
            P(),
            P(),
            P(None, "mlp"),
            P("mlp"),
            P("mlp", None),
            P(),
        ),
        check_vma=False,
    )
```

```python
import functools
import math
from types import SimpleNamespace

import jax
import jax.numpy as jnp
from jax import lax
from jax.experimental import pallas as pl
from jax.experimental.pallas import tpu as pltpu
from jax.sharding import PartitionSpec as P

HEADS = 4
PAIRS = HEADS // 2
EPSILON = 1e-05
MESH = pl.DeviceIdType.MESH
F32, BF = jnp.float32, jnp.bfloat16
PRECISE = lax.Precision.HIGHEST
NN = (((1,), (0,)), ((), ()))
NT = (((1,), (1,)), ((), ()))
TN = (((0,), (0,)), ((), ()))
MASKED = -1e30


def dot(a, b, dims=NN, precision=None):
    return lax.dot_general(a, b, dims, precision=precision, preferred_element_type=F32)


def mean(v):
    return jnp.mean(v, axis=-1, keepdims=True)


def layer_norm(values):
    centred = values - mean(values)
    inverse = lax.rsqrt(mean(centred * centred) + EPSILON)
    return centred * inverse, inverse


def norm_back(grad, normed, inverse):
    return inverse * (grad - mean(grad) - normed * mean(grad * normed))


def iota(shape, axis):
    return lax.broadcasted_iota(jnp.int32, shape, axis)


def cut(start, size):
    return pl.ds(start if isinstance(start, int) else pl.multiple_of(start, size), size)


def loop(count, body):
    lax.fori_loop(0, count, lambda i, c: (body(i), c)[1], 0)


def remote(src, dst, sems, index, device):
    send, recv = sems
    return pltpu.make_async_remote_copy(
        src_ref=src,
        dst_ref=dst,
        send_sem=send.at[index],
        recv_sem=recv.at[index],
        device_id=device,
        device_id_type=MESH,
    )


def sizes(m, nz):
    return m, 2, nz, 2 * nz, 2, nz // 2


class Sum:
    def __init__(self, out, dtype, bufs, sems, base, place, order, role):
        self.out, self.dtype, self.sems, self.base = out, dtype, sems, base
        self.part, self.cs, self.cr, self.rr = bufs[:4]
        self.place = place
        self.order = order
        r, m, M, core, x, z, nz = place
        self.index = (m, x, z, x * nz + z, lax.rem(z, 2), z // 2)
        self.size = sizes(M, nz)
        self.role = role
        self.shares = sum(self.size[axis] - 1 for axis in order)
        self.last = self.shares if role == OTHERS else 2 * self.shares
        self.all_sum = role == PLAIN and 0 not in order
        self.back = order if role != OTHERS else ()
        self.mr = bufs[4] if len(bufs) > 4 else None
        self.width = self.part.shape[1]
        self.mine = cut(core * self.width, self.width)
        self.other = cut((1 - core) * self.width, self.width)
        self.start, self.length, self.stage = [0], [self.part.shape[0]], [0]
        for axis in order:
            length = self.length[-1] // self.size[axis]
            self.start.append(self.start[-1] + self.index[axis] * length)
            self.stage.append(self.stage[-1] + self.length[-1] - length)
            self.length.append(length)
        if role != OTHERS:
            self.begin, self.extent = [0], [out.shape[0]]
            for axis in order:
                self.extent.append(self.extent[-1] // self.size[axis])
                self.begin.append(self.begin[-1] + self.index[axis] * self.extent[-1])
        self.todo = [functools.partial(self.share, i) for i in range(len(order))]
        if role == OTHERS:
            self.todo.append(self.send_over)
            return
        if self.all_sum:
            self.todo.append(self.send_mlp)
        self.todo.append(self.settle)
        self.todo += [functools.partial(self.gather, i) for i in reversed(range(len(self.back)))]
        self.todo.append(self.gather_core)

    def step(self, count=1):
        for _ in range(min(count, len(self.todo))):
            self.todo.pop(0)()

    def peer(self, axis, t):
        r, m, M, core, x, z, nz = self.place
        if axis == 0:
            return r, lax.rem(m + t, M)
        if axis == 1:
            return z * 4 + (1 - x) * 2 + core, m
        if axis == 2:
            return lax.rem(z + t, nz) * 4 + x * 2 + core, m
        if axis == 4:
            return (z + 1 - 2 * lax.rem(z, 2)) * 4 + x * 2 + core, m
        if axis == 5:
            return lax.rem(z + 2 * t, nz) * 4 + x * 2 + core, m
        to = lax.rem(x * nz + z + t, 2 * nz)
        return lax.rem(to, nz) * 4 + to // nz * 2 + core, m

    def slot(self, phase, i, t):
        before = sum(self.size[axis] - 1 for axis in self.order[:i])
        return phase * self.shares + before + t - 1

    def copy(self, src, dst, slot, device):
        return remote(src, dst, self.sems, self.base + slot, device)

    def core_copy(self, phase):
        r, m, M, core, x, z, nz = self.place
        device = (z * 4 + x * 2 + 1 - core, m)
        slot = self.last + phase
        if phase == 0:
            return self.copy(self.cs, self.cr, slot, device)
        block = self.out.at[:, self.mine]
        return self.copy(block, block, slot, device)

    def share_copy(self, i, t):
        axis, length = self.order[i], self.length[i + 1]
        at = pl.ds(self.stage[i] + (t - 1) * length, length)
        return self.copy(
            self.cs.at[at], self.rr.at[at], self.slot(0, i, t), self.peer(axis, t)
        )

    def gather_copy(self, i, t):
        axis = self.back[i]
        block = self.out.at[cut(self.begin[i + 1], self.extent[i + 1]), self.mine]
        return self.copy(block, block, self.slot(1, i, t), self.peer(axis, t))

    def mlp_copy(self, t):
        r, m, M, core, x, z, nz = self.place
        block = self.mr.at[m]
        return self.copy(block, block, self.last + 1 + t, (r, lax.rem(m + t, M)))

    def core_send(self):
        self.core_copy(0).start()

    def take(self, i):
        if i == 0:
            self.core_copy(0).wait()
            return
        at = cut(self.start[i], self.length[i])
        value = self.part[at, :]
        for t in range(1, self.size[self.order[i - 1]]):
            self.share_copy(i - 1, t).wait_recv()
            here = pl.ds(self.stage[i - 1] + (t - 1) * self.length[i], self.length[i])
            value = value + self.rr[here, :].astype(F32)
        if i == 1:
            value = value + self.cr[at, :].astype(F32)
        self.part[at, :] = value

    def share(self, i):
        self.take(i)
        axis, length = self.order[i], self.length[i + 1]
        for t in range(1, self.size[axis]):
            block = lax.rem(self.index[axis] + t, self.size[axis])
            at = cut(self.start[i] + block * length, length)
            value = self.part[at, :]
            if i == 0:
                value = value + self.cr[at, :].astype(F32)
            self.cs[pl.ds(self.stage[i] + (t - 1) * length, length), :] = value.astype(self.dtype)
            self.share_copy(i, t).start()

    def send_mlp(self):
        n = len(self.order)
        self.take(n)
        r, m, M, core, x, z, nz = self.place
        self.mr[m] = self.part[cut(self.start[n], self.length[n]), :].astype(self.dtype)
        for t in range(1, M):
            self.mlp_copy(t).start()

    def over_copy(self, t):
        r, m, M, core, x, z, nz = self.place
        length = self.length[-1] // (M - 1)
        source = self.cs.at[pl.ds(self.stage[-1] + (t - 1) * length, length)]
        slot = self.last + t
        return self.copy(source, self.mate.mr.at[t - 1], slot, (r, lax.rem(m + t, M)))

    def send_over(self):
        n = len(self.order)
        self.take(n)
        value = self.part[cut(self.start[n], self.length[n]), :]
        self.cs[pl.ds(self.stage[n], self.length[n]), :] = value.astype(self.dtype)
        for t in range(1, self.size[0]):
            self.over_copy(t).start()

    def settle(self):
        n = len(self.order)
        at = cut(self.start[n], self.length[n])
        if self.all_sum:
            for t in range(1, self.size[0]):
                self.mlp_copy(t).wait_recv()
            value = self.mr[0].astype(F32)
            for t in range(1, self.size[0]):
                value = value + self.mr[t].astype(F32)
        else:
            self.take(n)
            value = self.part[at, :]
        if self.role == OWN:
            for t in range(1, self.size[0]):
                self.mate.over_copy(t).wait_recv()
                value = value + self.mr[t - 1].astype(F32)
        here = cut(self.begin[-1], self.extent[-1])
        self.out[here, self.mine] = value.astype(self.dtype)

    def gather(self, i):
        if i < len(self.back) - 1:
            for t in range(1, self.size[self.back[i + 1]]):
                self.gather_copy(i + 1, t).wait_recv()
        for t in range(1, self.size[self.back[i]]):
            self.gather_copy(i, t).start()

    def gather_core(self):
        for t in range(1, self.size[self.back[0]]):
            self.gather_copy(0, t).wait_recv()
        self.core_copy(1).start()

    def arrive(self):
        self.core_copy(1).wait_recv()

    def release(self):
        for i, axis in enumerate(self.order):
            for t in range(1, self.size[axis]):
                self.share_copy(i, t).wait_send()
        if self.role == OTHERS:
            for t in range(1, self.size[0]):
                self.over_copy(t).wait_send()
            return
        for i, axis in enumerate(self.back):
            for t in range(1, self.size[axis]):
                self.gather_copy(i, t).wait_send()
        if self.all_sum:
            for t in range(1, self.size[0]):
                self.mlp_copy(t).wait_send()

    def finish(self):
        assert not self.todo
        self.core_copy(1).wait_send()

    @staticmethod
    def slots(order, role, nz, m):
        shares = sum(sizes(m, nz)[axis] - 1 for axis in order)
        if role == OTHERS:
            return shares + m
        return 2 * shares + 2 + (m - 1 if role == PLAIN and 0 not in order else 0)


class Spread:
    def __init__(self, source, parts, sems, base, place, sliced):
        self.source, self.parts, self.sems, self.base = source, parts, sems, base
        self.place, self.sliced = place, sliced
        r, m, M, core, x, z, nz = place
        _, rows, cols = parts.shape
        self.rows, width = rows, cols // 2
        self.mine = pl.ds(pl.multiple_of(core * width, width), width)
        piece = rows // (2 * nz)
        self.here = cut((x * nz + z) * piece, piece) if sliced else pl.ds(0, rows)
        self.each_peer = nz + 2 if sliced else 2

    def copies(self, stage, t):
        r, m, M, core, x, z, nz = self.place
        base = self.base + (t - 1) * self.each_peer
        if stage == 0:
            source = self.source.at[self.here, self.mine]
            target = self.parts.at[m, self.here, self.mine]
            return [remote(source, target, self.sems, base, (r, lax.rem(m + t, M)))]
        part = self.parts.at[lax.rem(m + M - t, M)]
        if stage == 1:
            block = part.at[self.here, self.mine]
            rows = [lax.rem(z + u, nz) * 4 + x * 2 + core for u in range(1, nz)]
        elif stage == 2:
            block = part.at[cut(x * (self.rows // 2), self.rows // 2), self.mine]
            rows = [z * 4 + (1 - x) * 2 + core]
        else:
            block = part.at[:, self.mine]
            rows = [z * 4 + x * 2 + 1 - core]
        first = base + ((0, 1, nz, nz + 1)[stage] if self.sliced else 1)
        return [
            remote(block, block, self.sems, first + i, (row, m)) for i, row in enumerate(rows)
        ]

    def stages(self):
        return (0, 1, 2, 3) if self.sliced else (0, 3)

    def each(self, stage):
        return [c for t in range(1, self.place[2]) for c in self.copies(stage, t)]

    def send(self, stage):
        before = [i for i in self.stages() if i < stage]
        if before:
            self.arrive(before[-1])
        for c in self.each(stage):
            c.start()

    def arrive(self, stage):
        for c in self.each(stage):
            c.wait_recv()

    def drain(self):
        for stage in self.stages():
            for c in self.each(stage):
                c.wait_send()


PLAIN, OWN, OTHERS = 0, 1, 2
SUMS = ("up", "down", "up2", "down2", "out", "query", "key", "value", "tail")
ROLES = (OWN, OWN, OTHERS, OTHERS, PLAIN, PLAIN, PLAIN, PLAIN, PLAIN)
FLAT = (1, 4, 5)
ORDERS = (FLAT, FLAT, FLAT, FLAT, (0, 1, 2), (0, 1, 2), (0, 1, 2), (0, 1, 2), (0, 3))


def sharing(i, rows, M, nz):
    if rows % (16 * 2 * nz * M) == 0 or (i == len(SUMS) - 1 and rows % (8 * 2 * nz * M) == 0):
        return ORDERS[i]
    return tuple(axis for axis in ORDERS[i] if axis != 0)


def kernel(static, names, *refs):
    ref = SimpleNamespace(**dict(zip(names, refs)))
    R, M, rows, D, F, S, near = static
    nz = R // 4
    G = rows // S
    W = 3 * G
    head = D // HEADS
    factor = 1.0 / math.sqrt(head)
    r, y = lax.axis_index("rows"), lax.axis_index("mlp")
    core, xi, z = lax.rem(r, 2), lax.rem(r // 2, 2), r // 4
    me = r * M + y
    devices = R * M
    pairs = M == 2
    up_row, down_row = lax.rem(r + 1, R), lax.rem(r + R - 1, R)
    after, before = lax.rem(me + 1, devices), lax.rem(me + devices - 1, devices)

    local = []
    lsem = ref.lsem
    for i, (src, dst) in enumerate(
        (
            (ref.x, ref.xb.at[1]),
            (ref.wq, ref.wqkv.at[:, 0:D]),
            (ref.wkv, ref.wqkv.at[:, D : 3 * D]),
            (ref.cot, ref.cotn),
            (ref.wo, ref.wob),
            (ref.wup, ref.wupb.at[y]),
            (ref.wdn, ref.wdnb.at[y]),
        )
    ):
        c = pltpu.make_async_copy(src, dst, lsem.at[i])
        c.start()
        local.append(c)

    barrier = pltpu.get_barrier_semaphore()
    others = [(r, lax.rem(y + t, M)) for t in range(1, M)]
    others.append((z * 4 + xi * 2 + 1 - core, y))
    for t in range(1, 2 * nz):
        to = lax.rem(xi * nz + z + t, 2 * nz)
        others.append((lax.rem(to, nz) * 4 + to // nz * 2 + core, y))
    if pairs:
        others += [(up_row, y), (down_row, y)]
    else:
        others += [(after // M, lax.rem(after, M)), (before // M, lax.rem(before, M))]
    for device in others:
        pl.semaphore_signal(barrier, inc=1, device_id=device, device_id_type=MESH)
    pl.semaphore_wait(barrier, len(others))

    def halo(source, at, sems):
        def first(k):
            if pairs:
                return [remote(source(k), at(2 * y, k), sems, (0, k), (r, 1 - y))]
            return [
                remote(source(k), at(0, k), sems, (0, k), (after // M, lax.rem(after, M))),
                remote(source(k), at(2, k), sems, (1, k), (before // M, lax.rem(before, M))),
            ]

        def second(k):
            if pairs:
                to = jnp.where(y == 0, up_row, down_row)
                return remote(at(2 * (1 - y), k), at(2 * y, k), sems, (1, k), (to, y))
            return first(k)[1]

        def send(k):
            for c in first(k):
                c.start()

        def pass_on(k):
            first(k)[0].wait_recv()
            if pairs:
                second(k).start()

        def arrive(k):
            second(k).wait_recv()

        def drain(k):
            first(k)[0].wait_send()
            second(k).wait_send()

        return send, pass_on, arrive, drain

    near_slot = 2 * (1 - y) if pairs else 0
    far_slot = 2 * y if pairs else 2
    xb = ref.xb
    quarter = rows // 4

    def part(k, n=quarter):
        return cut(k * n, n)

    x_send, x_pass, x_arrive, x_drain = halo(
        lambda k: ref.x.at[part(k)], lambda slot, k: xb.at[slot, part(k)], ref.xsem
    )
    loop(4, x_send)
    place_of = (r, y, M, core, xi, z, nz)
    spread = [
        Spread(source, parts, ref.spsem, i * (M - 1) * (nz + 2), place_of, i == 0)
        for i, (source, parts) in enumerate(((ref.wup, ref.wupb), (ref.wdn, ref.wdnb)))
    ]
    for part_of in spread:
        part_of.send(0)
    upb = ref.upb
    upb[y] = jnp.broadcast_to(ref.bup[...].astype(F32).reshape(1, F), (8, F))

    def bias_copy(t):
        return remote(upb.at[y], upb.at[y], ref.ubsem, t - 1, (r, lax.rem(y + t, M)))

    for t in range(1, M):
        bias_copy(t).start()

    def build(k):
        at = part(k)
        a, b = iota((quarter, rows), 0) + k * quarter, iota((quarter, rows), 1)
        ref.pm[at, :] = jnp.where(b == lax.rem(a, G) * S + a // G, 1.0, 0.0).astype(BF)
        ref.pt[at, :] = jnp.where(a == lax.rem(b, G) * S + b // G, 1.0, 0.0).astype(BF)

    loop(4, build)
    a, b = iota((quarter, quarter), 0), iota((quarter, quarter), 1)
    few = quarter // S
    ref.pq[...] = jnp.where(b == lax.rem(a, few) * S + a // few, 1.0, 0.0).astype(BF)
    pm, pt = ref.pm, ref.pt

    nodes = devices * G
    place = ref.nbr[...] // S - me * G + G
    place = jnp.where(place < 0, place + nodes, place)
    place = jnp.where(place >= nodes, place - nodes, place)
    place = place.astype(F32).astype(BF)
    lws = ref.lws
    lws[rows : rows + G, :] = jnp.zeros((G, near), F32)
    lws[0:rows, :] = dot(pm[...], place, NT)
    lwt = ref.lwt
    eye = jnp.where(iota((near, near), 0) == iota((near, near), 1), 1.0, 0.0).astype(BF)

    def turn(s):
        block = lws[pl.ds(pl.multiple_of(s * G, G), 2 * G), :].astype(BF)
        lwt[1, s] = dot(eye, block, NT).astype(BF)

    loop(S, turn)
    l_send, l_pass, l_arrive, l_drain = halo(
        lambda k: lwt.at[1], lambda slot, k: lwt.at[slot], ref.lwsem
    )
    l_send(0)

    modulation = dot(ref.nc[...], ref.adaw[...]) + ref.adab[...].astype(F32).reshape(1, 4 * D)
    ref.mod[...] = modulation
    mods = ref.mods
    for s in range(S):
        mods[s : s + 1, :] = ref.mod[pl.ds(ref.sid[s], 1), :]

    n1w, qkv = ref.n1w, ref.qkv
    wqkv = ref.wqkv

    turn16 = quarter // S

    def norm_block(slot, k):
        at = part(k)
        normed, _ = layer_norm(xb[slot, at, :].astype(F32))
        scaled = normed.reshape(turn16, S, D) * (1.0 + mods[:, 0:D])[None]
        scaled = scaled + mods[:, D : 2 * D][None]
        ordered = dot(ref.pq[...], scaled.reshape(quarter, D).astype(BF)).astype(BF)
        wide = dot(ordered, wqkv[...]).astype(BF).reshape(S, turn16, 3 * D)
        here = cut(slot * G + k * turn16, turn16)
        qkv[:, here, :] = wide
        n1w[:, here, :] = ordered.reshape(S, turn16, D)

    local[0].wait()
    local[1].wait()
    local[2].wait()

    loop(4, lambda k: norm_block(1, k))
    local[3].wait()
    xs, cotb = ref.xs, ref.cotb

    def order(k):
        xs[part(k), :] = dot(pm[part(k), :], xb[1]).astype(BF)
        cotb[part(k), :] = dot(pm[part(k), :], ref.cotn[...]).astype(BF)

    loop(4, order)

    cnt, cntt = ref.cnt, ref.cntt

    def count(s):
        block = lwt[1, s].astype(F32)
        block = jnp.where(iota((near, 2 * G), 1) < G, block, pltpu.roll(block, G, 1))
        key = iota((W, 2 * G), 0).astype(F32)
        total = jnp.zeros((W, 2 * G), F32)
        for j in range(near):
            total = total + jnp.where(block[j : j + 1, :] == key, 1.0, 0.0)
        cnt[s] = total

    loop(S, count)

    def near_norm(k):
        x_pass(k)
        norm_block(near_slot, k)

    loop(4, near_norm)


    def far_norm(k):
        x_arrive(k)
        norm_block(far_slot, k)

        @pl.when(k == 1)
        def _():
            spread[0].send(1)

    loop(4, far_norm)

    mixs, mixx, prob, stw = ref.mixs, ref.mixx, ref.prob, ref.stw
    ntb, mid = ref.ntb, ref.mid
    pair = 2 * head

    def apart(block):
        nothing = jnp.zeros((block.shape[0], head), block.dtype)
        left = jnp.concatenate([block[:, 0:head], nothing], axis=1)
        right = jnp.concatenate([nothing, block[:, head:pair]], axis=1)
        return jnp.concatenate([left, right], axis=0)

    def attend(k):
        for s2 in range(2):
            s = 2 * k + s2
            at = cut(s * G, G)
            times = cnt[s]
            logs = []
            for p in range(PAIRS):
                lo, hi = p * pair, (p + 1) * pair
                queries = apart(qkv[s, G : 2 * G, lo:hi])
                scores = dot(qkv[s, :, D + lo : D + hi], queries, NT) * factor
                scores = jnp.where(times > 0.0, scores, MASKED)
                top = jnp.max(scores, axis=0, keepdims=True)
                power = jnp.exp(scores - top)
                total = jnp.sum(power * times, axis=0, keepdims=True)
                probs = power * (1.0 / total)
                prob[s * PAIRS + p] = probs
                weight = (times * probs.astype(BF).astype(F32)).astype(BF)
                rest = (times * probs - weight.astype(F32)).astype(BF)
                both = jnp.concatenate([weight, rest], axis=1)
                mixed = dot(both, qkv[s, :, 2 * D + lo : 2 * D + hi], TN)
                one, two = mixed[0:G, 0:head], mixed[G : 2 * G, head:pair]
                mixs[at, lo : lo + head] = one.astype(BF)
                mixs[at, lo + head : hi] = two.astype(BF)
                mixx[at, lo : lo + head] = one + mixed[2 * G : 3 * G, 0:head]
                mixx[at, lo + head : hi] = two + mixed[3 * G : 4 * G, head:pair]
                logs.append(top + jnp.log(total))
            logs.append(jnp.zeros((8 - PAIRS, 2 * G), F32))
            stw[1, s] = jnp.concatenate(logs, axis=0)

    loop(4, attend)

    local[4].wait()
    wo = ref.wob
    half = rows // 2
    group = half // G

    def mix_out(c):
        at = part(c, half)
        middle = xs[at, :].astype(F32) + dot(mixs[at, :], wo[...])
        mid[at, :] = middle
        normed, _ = layer_norm(middle)
        for i in range(group):
            lo = i * G
            scale = mods[pl.ds(c * group + i, 1), 2 * D : 3 * D]
            shift = mods[pl.ds(c * group + i, 1), 3 * D : 4 * D]
            here = cut(c * half + lo, G)
            ntb[here, :] = (normed[lo : lo + G] * (1.0 + scale) + shift).astype(BF)

    loop(2, mix_out)

    local[5].wait()
    local[6].wait()
    spread[0].send(2)
    wup, wdn, actb, ghb = ref.wupb, ref.wdnb, ref.actb, ref.ghb
    bupg, g2o = ref.bupg, ref.g2o
    bupg[...] = jnp.zeros_like(bupg)
    g2o[...] = jnp.zeros_like(g2o)
    tile = 256

    def feed(p):
        def column(f):
            cols = part(f, tile)
            hidden = dot(ntb[...], wup[p, :, cols]) + upb[p, 0:1, cols]
            gate = jax.nn.sigmoid(hidden)
            active = hidden * gate
            actb[p, :, cols] = active.astype(BF)
            grad = dot(cotb[...], wdn[p, cols, :], NT)
            grad = (grad * (gate + active * (1.0 - gate))).astype(BF)
            ghb[p, :, cols] = grad
            bupg[p, 0:1, cols] += jnp.sum(grad.astype(F32), axis=0, keepdims=True)

        loop(F // tile, column)
        for q in range(D // tile):
            lo, hi = q * tile, (q + 1) * tile
            g2o[:, lo:hi] += dot(ghb[p], wup[p, lo:hi, :], NT)

    feed(y)

    base = 0
    sums = SimpleNamespace()
    written = []

    def write(source, result):
        c = pltpu.make_async_copy(source, result, ref.wsem.at[len(written)])
        c.start()
        written.append(c)

    for i, (name, bufs) in enumerate(zip(SUMS, ref.sums)):
        out, *bufs = bufs
        dtype = F32 if i == len(SUMS) - 1 else BF
        order = sharing(i, bufs[0].shape[0], M, nz)
        total = Sum(out, dtype, bufs, ref.sumsem, base, place_of, order, ROLES[i])
        base += Sum.slots(order, ROLES[i], nz, M)
        setattr(sums, name, total)
    sums.up.mate, sums.down.mate, sums.up2.mate, sums.down2.mate = (
        sums.up2,
        sums.down2,
        sums.up,
        sums.down,
    )

    def weight_grad(total, left, right):
        width = total.width
        for out, start, kind in (
            (total.cs, (1 - core) * width, BF),
            (total.part, core * width, F32),
        ):
            at = cut(start, width)
            out[...] = dot(left, right(at), TN).astype(kind)
            if kind == BF:
                total.core_send()

    def ffn_grad(total, count, which, rows_of, left, right):
        width = total.width
        many, block = min(rows_of, 512), rows_of // (2 * nz)
        for out, start, kind in (
            (total.cs, (1 - core) * width, BF),
            (total.part, core * width, F32),
        ):
            at = cut(start, width)

            def tile_row(i):
                u, f = i // (rows_of // many), lax.rem(i, rows_of // many)
                p = which(u)
                value = dot(left(p, part(f, many)), right(p, at), TN).astype(kind)
                if count == 1:
                    out[part(f, many), :] = value
                    return
                for v in range(many // block):
                    row = ((f * (many // block) + v) * count + u) * block
                    here = cut(row, block)
                    out[here, :] = value[v * block : (v + 1) * block]

            loop(count * rows_of // many, tile_row)
            if kind == BF:
                total.core_send()

    def up_grad(total, count, which):
        ffn_grad(total, count, which, D, lambda p, f: ntb[:, f], lambda p, at: ghb[p, :, at])

    def down_grad(total, count, which):
        ffn_grad(total, count, which, F, lambda p, f: actb[p, :, f], lambda p, at: cotb[:, at])

    l_pass(0)
    up_grad(sums.up, 1, lambda u: y)
    down_grad(sums.down, 1, lambda u: y)
    sums.up.step()
    sums.down.step()

    def feed_other(t):
        @pl.when(t == 0)
        def _():
            spread[0].send(3)
            spread[1].send(3)
            spread[0].arrive(3)
            spread[1].arrive(3)
            for u in range(1, M):
                bias_copy(u).wait_recv()

        feed(lax.rem(y + t + 1, M))

    loop(M - 1, feed_other)

    gmid, gmw, gatt, gmod = ref.gmid, ref.gmw, ref.cotn, ref.gmod
    row, lane = iota((8, D), 0), iota((8, D), 1) // head
    pick_one = jnp.where((row >= PAIRS) & (lane == 2 * (row - PAIRS)), 1.0, 0.0)
    pick_two = jnp.where((row >= PAIRS) & (lane == 2 * (row - PAIRS) + 1), 1.0, 0.0)
    m_send, m_pass, m_arrive, m_drain = halo(
        lambda k: gmw.at[pl.ds(2 * k, 2), pl.ds(G, G)],
        lambda slot, k: gmw.at[pl.ds(2 * k, 2), cut(slot * G, G)],
        ref.gmsem,
    )
    s_send, s_pass, s_arrive, s_drain = halo(
        lambda k: stw.at[1, pl.ds(2 * k, 2)],
        lambda slot, k: stw.at[slot, pl.ds(2 * k, 2)],
        ref.stsem,
    )

    def middle_back(c):
        at = part(c, half)
        grad = g2o[at, :]
        normed, inverse = layer_norm(mid[at, :])
        weighted = []
        for i in range(group):
            s = c * group + i
            lo, hi = i * G, (i + 1) * G
            scale = mods[pl.ds(s, 1), 2 * D : 3 * D]
            weighted.append(grad[lo:hi] * (1.0 + scale))
            gmod[pl.ds(s, 1), 2 * D : 3 * D] = jnp.sum(
                grad[lo:hi] * normed[lo:hi], axis=0, keepdims=True
            )
            gmod[pl.ds(s, 1), 3 * D : 4 * D] = jnp.sum(grad[lo:hi], axis=0, keepdims=True)
        weighted = jnp.concatenate(weighted, axis=0)
        middle = cotb[at, :].astype(F32) + norm_back(weighted, normed, inverse)
        gmid[at, :] = middle
        rounded = middle.astype(BF)
        gatt[at, :] = rounded
        mixture = dot(rounded, wo[...], NT).astype(BF)
        gmw[pl.ds(c * group, group), G : 2 * G, :] = mixture.reshape(group, G, D)
        product = mixture.astype(F32) * mixx[at, :]
        ones = dot(pick_one, product, NT, PRECISE)
        twos = dot(pick_two, product, NT, PRECISE)
        first_lanes = iota((8, 2 * G), 1) < G
        for g in range(group // 2):
            lo, hi = g * 2 * G, (g + 1) * 2 * G
            one, two = ones[:, lo:hi], twos[:, lo:hi]
            s = c * group + 2 * g
            stw[1, s] += jnp.where(first_lanes, one, pltpu.roll(two, G, 1))
            stw[1, s + 1] += jnp.where(first_lanes, pltpu.roll(one, G, 1), two)
        for k in range(2):
            m_send(2 * c + k)
            s_send(2 * c + k)

    def pass_on(k):
        m_pass(k)
        s_pass(k)

    def other_part(u):
        return lax.rem(y + u + 1, M)

    gqkv, gkvw = ref.gqkv, ref.gkvw

    def query_back(s):
        at = cut(s * G, G)
        times = cnt[s]
        for p in range(PAIRS):
            lo, hi = p * pair, (p + 1) * pair
            grads = apart(gmw[s, G : 2 * G, lo:hi])
            gprob = dot(qkv[s, :, 2 * D + lo : 2 * D + hi], grads, NT)
            gscore = prob[s * PAIRS + p] * (gprob - stw[1, s, PAIRS + p : PAIRS + p + 1, :])
            weight = (times * gscore.astype(BF).astype(F32)).astype(BF)
            gquery = dot(weight, qkv[s, :, D + lo : D + hi], TN) * factor
            gqkv[at, lo : lo + head] = gquery[0:G, 0:head].astype(BF)
            gqkv[at, lo + head : hi] = gquery[G : 2 * G, head:pair].astype(BF)
            queries = apart(qkv[s, G : 2 * G, lo:hi])
            gkvw[s, :, lo:hi] = (dot(weight, queries) * factor).astype(BF)
            weight = (times * prob[s * PAIRS + p].astype(BF).astype(F32)).astype(BF)
            gkvw[s, :, D + lo : D + hi] = dot(weight, grads).astype(BF)


    def count_back(s):
        shift = [2 * G, G, 0]
        block = jnp.concatenate(
            [lwt[b, s][:, 0:G].astype(F32) - float(shift[b]) for b in range(3)], axis=1
        ).astype(jnp.int32)
        key = iota((G, W), 0)
        total = jnp.zeros((G, W), F32)
        for j in range(near):
            total = total + jnp.where(block[j : j + 1, :] == key, 1.0, 0.0)
        cntt[s] = total

    def finish_out(k):
        at = part(k)
        value = mid[at, :] + ref.bdn[...].astype(F32).reshape(1, D)
        for p in range(M):
            value = value + dot(actb[p, at, :], wdn[p])
        ref.n1n[at, :] = value.astype(BF)


    def key_back(s):
        at = cut(s * G, G)
        times = cntt[s]
        stats = [
            jnp.concatenate([stw[b, s][:, i * G : (i + 1) * G] for b in range(3)], axis=1)
            for i in range(2)
        ]
        for p in range(PAIRS):
            lo, hi = p * pair, (p + 1) * pair
            queries, grads = qkv[s, :, lo:hi], gmw[s, :, lo:hi]
            scores = dot(apart(qkv[s, G : 2 * G, D + lo : D + hi]), queries, NT) * factor
            gprob = dot(apart(qkv[s, G : 2 * G, 2 * D + lo : 2 * D + hi]), grads, NT)
            gscores, weights = [], []
            for i in range(2):
                rows_of = slice(i * G, (i + 1) * G)
                log, delta = stats[i][p : p + 1], stats[i][PAIRS + p : PAIRS + p + 1]
                probs = jnp.exp(jnp.where(times > 0.0, scores[rows_of] - log, MASKED))
                gscore = probs * (gprob[rows_of] - delta)
                gscores.append((times * gscore.astype(BF).astype(F32)).astype(BF))
                weights.append((times * probs.astype(BF).astype(F32)).astype(BF))
            gkey = dot(jnp.concatenate(gscores, axis=0), queries) * factor
            gvalue = dot(jnp.concatenate(weights, axis=0), grads)
            for i in range(2):
                cols = pl.ds(D + lo + i * head, head)
                gqkv[at, cols] = gkey[i * G : (i + 1) * G, i * head : (i + 1) * head].astype(BF)
                cols = pl.ds(2 * D + lo + i * head, head)
                gqkv[at, cols] = gvalue[i * G : (i + 1) * G, i * head : (i + 1) * head].astype(BF)


    gdbs = ref.gdbs
    out_rows = ref.outr

    def first_back(c):
        at = part(c, half)
        grad = dot(gqkv[at, :], wqkv[...], NT)
        normed, inverse = layer_norm(xs[at, :].astype(F32))
        weighted = []
        for i in range(group):
            s = c * group + i
            lo, hi = i * G, (i + 1) * G
            here = cut(s * G, G)
            gmod[pl.ds(s, 1), 0:D] = jnp.sum(grad[lo:hi] * normed[lo:hi], axis=0, keepdims=True)
            gmod[pl.ds(s, 1), D : 2 * D] = jnp.sum(grad[lo:hi], axis=0, keepdims=True)
            gdbs[pl.ds(s, 1), :] = jnp.sum(cotb[here, :].astype(F32), axis=0, keepdims=True)
            weighted.append(grad[lo:hi] * (1.0 + mods[pl.ds(s, 1), 0:D]))
        weighted = jnp.concatenate(weighted, axis=0)
        g2o[at, :] = gmid[at, :] + norm_back(weighted, normed, inverse)

    tail = ref.tail
    base = 4 * D // tile * S
    base_up = base + D // tile * S

    def pack_tail():
        tail[...] = jnp.zeros_like(tail)
        for c in range(4 * D // tile):
            tail[c * S : (c + 1) * S, :] = gmod[:, c * tile : (c + 1) * tile]
        for c in range(D // tile):
            tail[base + c * S : base + (c + 1) * S, :] = gdbs[:, c * tile : (c + 1) * tile]
        for c in range(F // tile):
            for p in range(M):
                row = base_up + p * (F // tile) + c
                tail[row : row + 1, :] = bupg[p, 0:1, c * tile : (c + 1) * tile]
        sums.tail.cs[...] = tail[:, sums.tail.other]
        sums.tail.part[...] = tail[:, sums.tail.mine]
        sums.tail.core_send()

    def rows_back():
        for c in range(D // 128):
            lo, hi = c * 128, (c + 1) * 128
            for s in range(S):
                ref.turn[c, pl.ds(s, G, stride=S), :] = g2o[s * G : (s + 1) * G, lo:hi]
            out_rows[:, lo:hi] = ref.turn[c]
        write(out_rows, ref.o_rows)

    def order_back(k):
        ref.outl[part(k), :] = dot(pt[part(k), :], ref.n1n[...]).astype(BF)


    def drain():
        loop(4, x_drain)
        l_drain(0)
        loop(4, m_drain)
        loop(4, s_drain)
        for part_of in spread:
            part_of.drain()
        for t in range(1, M):
            bias_copy(t).wait_send()
        sums.up2.release()
        sums.down2.release()

    def release():
        for total in (sums.up, sums.down, sums.out, sums.query, sums.key, sums.value, sums.tail):
            total.release()

    def out_grad():
        weight_grad(sums.out, mixs[...], lambda at: gatt[:, at])

    def query_grad():
        weight_grad(sums.query, n1w[:, G : 2 * G, :].reshape(rows, D), lambda at: gqkv[:, at])

    def window_grad(total, shares):
        left = n1w[...].reshape(S * W, D)
        weight_grad(total, left, lambda at: shares[:, :, at].reshape(S * W, at.size))

    def key_grad():
        window_grad(sums.key, gkvw.at[:, :, 0:D])

    def value_grad():
        window_grad(sums.value, gkvw.at[:, :, D : 2 * D])

    def queries_of(k):
        query_back(2 * k)
        query_back(2 * k + 1)

    def keys_of(k):
        m_arrive(k)
        s_arrive(k)
        key_back(2 * k)
        key_back(2 * k + 1)

    def counts():
        l_arrive(0)
        loop(S, count_back)

    def layer_out():
        loop(4, finish_out)

    def layer_order():
        loop(4, order_back)
        write(ref.outl, ref.o_layer)

    sums.up.step()
    up_grad(sums.up2, M - 1, other_part)
    down_grad(sums.down2, M - 1, other_part)
    sums.up2.step()
    middle_back(0)
    sums.up.step()
    sums.down.step()
    sums.down2.step()
    middle_back(1)
    out_grad()
    sums.out.step()
    queries_of(0)
    sums.down.step()
    queries_of(1)
    sums.up2.step()
    queries_of(2)
    queries_of(3)
    pass_on(0)
    pass_on(1)
    query_grad()
    sums.query.step()
    sums.up2.step()
    key_grad()
    sums.key.step()
    pass_on(2)
    sums.down2.step()
    value_grad()
    sums.value.step()
    pass_on(3)
    counts()
    layer_out()
    sums.out.step()
    sums.up2.step()
    keys_of(0)
    sums.down2.step()
    keys_of(1)
    sums.query.step()
    keys_of(2)
    keys_of(3)
    sums.out.step()
    sums.key.step()
    first_back(0)
    sums.query.step()
    sums.down2.step()
    first_back(1)
    pack_tail()
    sums.up.step()
    sums.value.step()
    sums.up.step()
    rows_back()
    layer_order()
    sums.tail.step()
    sums.key.step()
    sums.out.step(2)
    sums.query.step(2)
    sums.value.step()
    sums.key.step(2)
    sums.tail.step()
    sums.down.step(2)
    sums.up.step()
    sums.out.step()
    sums.query.step()
    sums.tail.step()
    sums.value.step(2)
    sums.up.step()
    sums.key.step()
    sums.out.step()
    sums.tail.step()
    sums.query.step()
    sums.down.step()
    sums.value.step()
    sums.up.step()
    sums.key.step()
    sums.out.step()
    sums.value.step()
    sums.tail.step()
    sums.query.step()
    sums.down.step()
    release()
    sums.key.step()
    drain()
    sums.value.step()
    sums.tail.step()
    sums.down.step()
    late = (sums.up, sums.out, sums.query, sums.key, sums.value, sums.tail, sums.down)
    results = (ref.o_up, ref.o_out, ref.o_q, ref.o_k, ref.o_v, ref.o_tail, ref.o_dn)
    for total, result in zip(late, results):
        while total.todo:
            total.step()
        total.arrive()
        write(total.out, result)
    for total in late:
        total.finish()
    for c in written:
        c.wait()


WIDE = ("o_up", "o_dn", "o_out", "o_q", "o_k", "o_v")


def widen(static, names, *refs):
    ref = SimpleNamespace(**dict(zip(names, refs)))
    M, D, F, S = static
    tile = 256
    y = lax.axis_index("mlp")
    sources = (ref.o_up, ref.o_dn, ref.o_out, ref.o_q, ref.o_k, ref.o_v)
    targets = (
        ref.f_up,
        ref.f_dn,
        ref.f_out,
        ref.f_q,
        ref.f_kv.at[:, 0:D],
        ref.f_kv.at[:, D : 2 * D],
    )
    n = len(sources)
    straight = ((ref.o_rows, ref.rows, ref.f_rows), (ref.o_layer, ref.layer, ref.f_layer))
    passing = []
    for i, (source, middle, target) in enumerate(straight):
        load = pltpu.make_async_copy(source, middle, ref.isem.at[n + 1 + i])
        passing.append((load, pltpu.make_async_copy(middle, target, ref.osem.at[n + 1 + i])))
        load.start()
    loads = [
        pltpu.make_async_copy(source, ref.inb[i], ref.isem.at[i])
        for i, source in enumerate(sources)
    ]
    tail_in = pltpu.make_async_copy(ref.o_tail, ref.tail, ref.isem.at[n])
    loads[0].start()
    loads[1].start()
    tail_in.start()
    for load in loads[2:]:
        load.start()
    stores = []

    def store(copy):
        copy.start()
        stores.append(copy)

    for load, out in passing:
        load.wait()
        store(out)

    def convert(i):
        loads[i].wait()
        at_once = 128

        def part(k):
            at = cut(k * at_once, at_once)
            ref.outb[i][at, :] = ref.inb[i][at, :].astype(F32)
            pltpu.make_async_copy(ref.outb[i].at[at], targets[i].at[at], ref.osem.at[i]).start()

        loop(sources[i].shape[0] // at_once, part)
        stores.append(pltpu.make_async_copy(ref.outb[i], targets[i], ref.osem.at[i]))

    convert(0)
    convert(1)
    tail_in.wait()
    tail, gms = ref.tail, ref.gms
    pick = jnp.zeros((S, S), F32)
    for s in range(S):
        hit = (iota((S, S), 1) == s) & (iota((S, S), 0) == ref.sid[s])
        pick = pick + jnp.where(hit, 1.0, 0.0)
    for c in range(4 * D // tile):
        gms[:, c * tile : (c + 1) * tile] = dot(pick, tail[c * S : (c + 1) * S, :], NN, PRECISE)
    total = gms[...]
    ref.ada[...] = dot(ref.nc[...].astype(F32), total, TN, PRECISE)
    store(pltpu.make_async_copy(ref.ada, ref.f_ada, ref.osem.at[n]))
    for i in range(2, n):
        convert(i)
    ref.f_adab[...] = jnp.sum(total, axis=0)
    ref.f_cond[...] = dot(total, ref.adaw[...].astype(F32), NT, PRECISE)
    base = 4 * D // tile * S
    for c in range(D // tile):
        ref.f_downb[c * tile : (c + 1) * tile] = jnp.sum(
            tail[base + c * S : base + (c + 1) * S, :], axis=0
        )
    base += D // tile * S
    for c in range(F // tile):
        row = tail[pl.ds(base + y * (F // tile) + c, 1), :]
        ref.f_upb[c * tile : (c + 1) * tile] = row.reshape(tile)
    for c in stores:
        c.wait()


def shards(
    node_rows,
    noise_cond,
    sample_id,
    neighbours,
    ada_weight,
    ada_bias,
    query_weight,
    keyval_weight,
    out_weight,
    up_weight,
    up_bias,
    down_weight,
    down_bias,
    cotangent,
):
    rows, D = node_rows.shape
    F = up_weight.shape[1]
    S, cond = noise_cond.shape
    near = neighbours.shape[1]
    R, M = lax.axis_size("rows"), lax.axis_size("mlp")
    nz = R // 4
    G = rows // S
    W = 3 * G
    small = 16 * nz if 16 * nz > 88 else 128
    V, H = pltpu.VMEM, pl.ANY
    shape = jax.ShapeDtypeStruct
    arguments = dict(
        x=(node_rows, H),
        nc=(noise_cond, V),
        sid=(sample_id, pltpu.SMEM),
        nbr=(neighbours.T, V),
        adaw=(ada_weight, V),
        adab=(ada_bias, V),
        wq=(query_weight, H),
        wkv=(keyval_weight, H),
        wo=(out_weight, H),
        wup=(up_weight, H),
        bup=(up_bias, V),
        wdn=(down_weight, H),
        bdn=(down_bias, V),
        cot=(cotangent, H),
    )
    outputs = dict(
        o_layer=shape((rows, D), BF),
        o_rows=shape((rows, D), F32),
        o_q=shape((D, D), BF),
        o_k=shape((D, D), BF),
        o_v=shape((D, D), BF),
        o_out=shape((D, D), BF),
        o_up=shape((D, F), BF),
        o_dn=shape((F, D), BF),
        o_tail=shape((small, 256), F32),
    )
    scratch = dict(
        xb=V((3, rows, D), BF),
        cotn=V((rows, D), BF),
        wqkv=V((D, 3 * D), BF),
        wob=V((D, D), BF),
        wupb=V((M, D, F), BF),
        wdnb=V((M, F, D), BF),
        pm=V((rows, rows), BF),
        pt=V((rows, rows), BF),
        lws=V((rows + G, near), F32),
        lwt=V((3, S, near, 2 * G), BF),
        mod=V((S, 4 * D), F32),
        mods=V((S, 4 * D), F32),
        n1n=V((rows, D), BF),
        n1w=V((S, W, D), BF),
        gkvw=V((S, W, 2 * D), BF),
        pq=V((rows // 4, rows // 4), BF),
        xs=V((rows, D), BF),
        qkv=V((S, W, 3 * D), BF),
        cotb=V((rows, D), BF),
        cnt=V((S, W, 2 * G), F32),
        cntt=V((S, G, W), F32),
        mixs=V((rows, D), BF),
        mixx=V((rows, D), F32),
        prob=V((S * PAIRS, W, 2 * G), F32),
        ntb=V((rows, D), BF),
        mid=V((rows, D), F32),
        actb=V((M, rows, F), BF),
        ghb=V((M, rows, F), BF),
        bupg=V((M, 8, F), F32),
        upb=V((M, 8, F), F32),
        g2o=V((rows, D), F32),
        gmid=V((rows, D), F32),
        gmw=V((S, W, D), BF),
        stw=V((3, S, 8, 2 * G), F32),
        gmod=V((S, 4 * D), F32),
        gqkv=V((rows, 3 * D), BF),
        gdbs=V((S, D), F32),
        turn=V((D // 128, rows, 128), F32),
        tail=V((small, 256), F32),
        outr=V((rows, D), F32),
        outl=V((rows, D), BF),
    )
    sums = []
    wide = ((D, F), (F, D), (D, F), (F, D), *[(D, D)] * 4, (small, 256))
    count = 0
    for i, (n, c) in enumerate(wide):
        dtype = F32 if i == len(SUMS) - 1 else BF
        times = M - 1 if ROLES[i] == OTHERS else 1
        stage = (n * times, c // 2)
        count += Sum.slots(sharing(i, n * times, M, nz), ROLES[i], nz, M)
        out = V((8, 128) if ROLES[i] == OTHERS else (n, c), dtype)
        bufs = [out, V(stage, F32)] + [V(stage, dtype)] * 3
        if ROLES[i] == OWN:
            bufs.append(V((M - 1, n // (2 * nz), c // 2), dtype))
        elif ROLES[i] == PLAIN and 0 not in sharing(i, n, M, nz):
            bufs.append(V((M, n // (2 * nz), c // 2), dtype))
        sums.append(tuple(bufs))
    scratch.update(sums=tuple(sums))
    sem = pltpu.SemaphoreType.DMA
    for name, dims in dict(
        xsem=(2, 4),
        spsem=(2 * (M - 1) * (nz + 2),),
        ubsem=(M - 1,),
        lwsem=(2, 1),
        gmsem=(2, 4),
        stsem=(2, 4),
        sumsem=(count,),
    ).items():
        scratch[name] = (sem(dims), sem(dims))
    scratch.update(lsem=sem((7,)), wsem=sem((len(outputs),)))
    names = [*arguments, *outputs, *scratch]
    results = pl.pallas_call(
        functools.partial(kernel, (R, M, rows, D, F, S, near), names),
        out_shape=[*outputs.values()],
        in_specs=[pl.BlockSpec(memory_space=m) for _, m in arguments.values()],
        out_specs=[pl.BlockSpec(memory_space=H) for _ in outputs],
        scratch_shapes=[*scratch.values()],
        name="layer",
        compiler_params=pltpu.CompilerParams(
            collective_id=0, has_side_effects=True, vmem_limit_bytes=63 * 2**20
        ),
    )(*[a for a, _ in arguments.values()])
    got = dict(zip(outputs, results))
    inputs = dict(
        nc=(noise_cond, V),
        sid=(sample_id, pltpu.SMEM),
        adaw=(ada_weight, V),
        **{name: (value, H) for name, value in got.items()},
    )
    finals = dict(
        f_layer=shape((rows, D), BF),
        f_rows=shape((rows, D), F32),
        f_cond=shape((S, cond), F32),
        f_ada=shape((cond, 4 * D), F32),
        f_adab=shape((4 * D,), F32),
        f_q=shape((D, D), F32),
        f_kv=shape((D, 2 * D), F32),
        f_out=shape((D, D), F32),
        f_up=shape((D, F), F32),
        f_upb=shape((F,), F32),
        f_dn=shape((F, D), F32),
        f_downb=shape((D,), F32),
    )
    small_ones = ("f_cond", "f_adab", "f_upb", "f_downb")
    room = dict(
        inb=tuple(V(got[name].shape, BF) for name in WIDE),
        outb=tuple(V(got[name].shape, F32) for name in WIDE),
        tail=V((small, 256), F32),
        ada=V((cond, 4 * D), F32),
        layer=V((rows, D), BF),
        rows=V((rows, D), F32),
        gms=V((S, 4 * D), F32),
        isem=sem((len(WIDE) + 3,)),
        osem=sem((len(WIDE) + 3,)),
    )
    return pl.pallas_call(
        functools.partial(widen, (M, D, F, S), [*inputs, *finals, *room]),
        out_shape=[*finals.values()],
        in_specs=[pl.BlockSpec(memory_space=m) for _, m in inputs.values()],
        out_specs=[
            pl.BlockSpec(memory_space=V if name in small_ones else H) for name in finals
        ],
        scratch_shapes=[*room.values()],
        name="widen",
        compiler_params=pltpu.CompilerParams(vmem_limit_bytes=62 * 2**20),
    )(*[a for a, _ in inputs.values()])


def solution(mesh):
    both = P(("rows", "mlp"), None)
    placed = (
        both,
        P(),
        P(("rows", "mlp")),
        both,
        P(),
        P(),
        P(),
        P(),
        P(),
        P(None, "mlp"),
        P("mlp"),
        P("mlp", None),
        P(),
        both,
    )
    return jax.shard_map(
        shards,
        mesh=mesh,
        in_specs=placed,
        out_specs=(
            both,
            both,
            P(),
            P(),
            P(),
            P(),
            P(),
            P(),
            P(None, "mlp"),
            P("mlp"),
            P("mlp", None),
            P(),
        ),
        check_vma=False,
    )
```

```python
import functools
import math
from types import SimpleNamespace

import jax
import jax.numpy as jnp
from jax import lax
from jax.experimental import pallas as pl
from jax.experimental.pallas import tpu as pltpu
from jax.sharding import PartitionSpec as P

HEADS = 4
PAIRS = HEADS // 2
EPSILON = 1e-05
MESH = pl.DeviceIdType.MESH
F32, BF = jnp.float32, jnp.bfloat16
PRECISE = lax.Precision.HIGHEST
NN = (((1,), (0,)), ((), ()))
NT = (((1,), (1,)), ((), ()))
TN = (((0,), (0,)), ((), ()))
MASKED = -1e30


def dot(a, b, dims=NN, precision=None):
    return lax.dot_general(a, b, dims, precision=precision, preferred_element_type=F32)


def mean(v):
    return jnp.mean(v, axis=-1, keepdims=True)


def layer_norm(values):
    centred = values - mean(values)
    inverse = lax.rsqrt(mean(centred * centred) + EPSILON)
    return centred * inverse, inverse


def norm_back(grad, normed, inverse):
    return inverse * (grad - mean(grad) - normed * mean(grad * normed))


def iota(shape, axis):
    return lax.broadcasted_iota(jnp.int32, shape, axis)


def cut(start, size):
    return pl.ds(start if isinstance(start, int) else pl.multiple_of(start, size), size)


def loop(count, body):
    lax.fori_loop(0, count, lambda i, c: (body(i), c)[1], 0)


def remote(src, dst, sems, index, device):
    send, recv = sems
    return pltpu.make_async_remote_copy(
        src_ref=src,
        dst_ref=dst,
        send_sem=send.at[index],
        recv_sem=recv.at[index],
        device_id=device,
        device_id_type=MESH,
    )


def sizes(m, nz):
    return m, 2, nz, 2 * nz, 2, nz // 2


class Sum:
    def __init__(self, out, dtype, bufs, sems, base, place, order, role):
        self.out, self.dtype, self.sems, self.base = out, dtype, sems, base
        self.part, self.cs, self.cr, self.rr = bufs[:4]
        self.place = place
        self.order = order
        r, m, M, core, x, z, nz = place
        self.index = (m, x, z, x * nz + z, lax.rem(z, 2), z // 2)
        self.size = sizes(M, nz)
        self.role = role
        self.shares = sum(self.size[axis] - 1 for axis in order)
        self.last = self.shares if role == OTHERS else 2 * self.shares
        self.all_sum = role == PLAIN and 0 not in order
        self.back = order if role != OTHERS else ()
        self.mr = bufs[4] if len(bufs) > 4 else None
        self.width = self.part.shape[1]
        self.mine = cut(core * self.width, self.width)
        self.other = cut((1 - core) * self.width, self.width)
        self.start, self.length, self.stage = [0], [self.part.shape[0]], [0]
        for axis in order:
            length = self.length[-1] // self.size[axis]
            self.start.append(self.start[-1] + self.index[axis] * length)
            self.stage.append(self.stage[-1] + self.length[-1] - length)
            self.length.append(length)
        if role != OTHERS:
            self.begin, self.extent = [0], [out.shape[0]]
            for axis in order:
                self.extent.append(self.extent[-1] // self.size[axis])
                self.begin.append(self.begin[-1] + self.index[axis] * self.extent[-1])
        self.todo = [functools.partial(self.share, i) for i in range(len(order))]
        if role == OTHERS:
            self.todo.append(self.send_over)
            return
        if self.all_sum:
            self.todo.append(self.send_mlp)
        self.todo.append(self.settle)
        self.todo += [functools.partial(self.gather, i) for i in reversed(range(len(self.back)))]
        self.todo.append(self.gather_core)

    def step(self, count=1):
        for _ in range(min(count, len(self.todo))):
            self.todo.pop(0)()

    def peer(self, axis, t):
        r, m, M, core, x, z, nz = self.place
        if axis == 0:
            return r, lax.rem(m + t, M)
        if axis == 1:
            return z * 4 + (1 - x) * 2 + core, m
        if axis == 2:
            return lax.rem(z + t, nz) * 4 + x * 2 + core, m
        if axis == 4:
            return (z + 1 - 2 * lax.rem(z, 2)) * 4 + x * 2 + core, m
        if axis == 5:
            return lax.rem(z + 2 * t, nz) * 4 + x * 2 + core, m
        to = lax.rem(x * nz + z + t, 2 * nz)
        return lax.rem(to, nz) * 4 + to // nz * 2 + core, m

    def slot(self, phase, i, t):
        before = sum(self.size[axis] - 1 for axis in self.order[:i])
        return phase * self.shares + before + t - 1

    def copy(self, src, dst, slot, device):
        return remote(src, dst, self.sems, self.base + slot, device)

    def core_copy(self, phase):
        r, m, M, core, x, z, nz = self.place
        device = (z * 4 + x * 2 + 1 - core, m)
        slot = self.last + phase
        if phase == 0:
            return self.copy(self.cs, self.cr, slot, device)
        block = self.out.at[:, self.mine]
        return self.copy(block, block, slot, device)

    def share_copy(self, i, t):
        axis, length = self.order[i], self.length[i + 1]
        at = pl.ds(self.stage[i] + (t - 1) * length, length)
        return self.copy(
            self.cs.at[at], self.rr.at[at], self.slot(0, i, t), self.peer(axis, t)
        )

    def gather_copy(self, i, t):
        axis = self.back[i]
        block = self.out.at[cut(self.begin[i + 1], self.extent[i + 1]), self.mine]
        return self.copy(block, block, self.slot(1, i, t), self.peer(axis, t))

    def mlp_copy(self, t):
        r, m, M, core, x, z, nz = self.place
        block = self.mr.at[m]
        return self.copy(block, block, self.last + 1 + t, (r, lax.rem(m + t, M)))

    def core_send(self):
        self.core_copy(0).start()

    def take(self, i):
        if i == 0:
            self.core_copy(0).wait()
            return
        at = cut(self.start[i], self.length[i])
        value = self.part[at, :]
        for t in range(1, self.size[self.order[i - 1]]):
            self.share_copy(i - 1, t).wait_recv()
            here = pl.ds(self.stage[i - 1] + (t - 1) * self.length[i], self.length[i])
            value = value + self.rr[here, :].astype(F32)
        if i == 1:
            value = value + self.cr[at, :].astype(F32)
        self.part[at, :] = value

    def share(self, i):
        self.take(i)
        axis, length = self.order[i], self.length[i + 1]
        for t in range(1, self.size[axis]):
            block = lax.rem(self.index[axis] + t, self.size[axis])
            at = cut(self.start[i] + block * length, length)
            value = self.part[at, :]
            if i == 0:
                value = value + self.cr[at, :].astype(F32)
            self.cs[pl.ds(self.stage[i] + (t - 1) * length, length), :] = value.astype(self.dtype)
            self.share_copy(i, t).start()

    def send_mlp(self):
        n = len(self.order)
        self.take(n)
        r, m, M, core, x, z, nz = self.place
        self.mr[m] = self.part[cut(self.start[n], self.length[n]), :].astype(self.dtype)
        for t in range(1, M):
            self.mlp_copy(t).start()

    def over_copy(self, t):
        r, m, M, core, x, z, nz = self.place
        length = self.length[-1] // (M - 1)
        source = self.cs.at[pl.ds(self.stage[-1] + (t - 1) * length, length)]
        slot = self.last + t
        return self.copy(source, self.mate.mr.at[t - 1], slot, (r, lax.rem(m + t, M)))

    def send_over(self):
        n = len(self.order)
        self.take(n)
        value = self.part[cut(self.start[n], self.length[n]), :]
        self.cs[pl.ds(self.stage[n], self.length[n]), :] = value.astype(self.dtype)
        for t in range(1, self.size[0]):
            self.over_copy(t).start()

    def settle(self):
        n = len(self.order)
        at = cut(self.start[n], self.length[n])
        if self.all_sum:
            for t in range(1, self.size[0]):
                self.mlp_copy(t).wait_recv()
            value = self.mr[0].astype(F32)
            for t in range(1, self.size[0]):
                value = value + self.mr[t].astype(F32)
        else:
            self.take(n)
            value = self.part[at, :]
        if self.role == OWN:
            for t in range(1, self.size[0]):
                self.mate.over_copy(t).wait_recv()
                value = value + self.mr[t - 1].astype(F32)
        here = cut(self.begin[-1], self.extent[-1])
        self.out[here, self.mine] = value.astype(self.dtype)

    def gather(self, i):
        if i < len(self.back) - 1:
            for t in range(1, self.size[self.back[i + 1]]):
                self.gather_copy(i + 1, t).wait_recv()
        for t in range(1, self.size[self.back[i]]):
            self.gather_copy(i, t).start()

    def gather_core(self):
        for t in range(1, self.size[self.back[0]]):
            self.gather_copy(0, t).wait_recv()
        self.core_copy(1).start()

    def arrive(self):
        self.core_copy(1).wait_recv()

    def release(self):
        for i, axis in enumerate(self.order):
            for t in range(1, self.size[axis]):
                self.share_copy(i, t).wait_send()
        if self.role == OTHERS:
            for t in range(1, self.size[0]):
                self.over_copy(t).wait_send()
            return
        for i, axis in enumerate(self.back):
            for t in range(1, self.size[axis]):
                self.gather_copy(i, t).wait_send()
        if self.all_sum:
            for t in range(1, self.size[0]):
                self.mlp_copy(t).wait_send()

    def finish(self):
        assert not self.todo
        self.core_copy(1).wait_send()

    @staticmethod
    def slots(order, role, nz, m):
        shares = sum(sizes(m, nz)[axis] - 1 for axis in order)
        if role == OTHERS:
            return shares + m
        return 2 * shares + 2 + (m - 1 if role == PLAIN and 0 not in order else 0)


class Spread:
    def __init__(self, source, parts, sems, base, place, sliced):
        self.source, self.parts, self.sems, self.base = source, parts, sems, base
        self.place, self.sliced = place, sliced
        r, m, M, core, x, z, nz = place
        _, rows, cols = parts.shape
        self.rows, width = rows, cols // 2
        self.mine = pl.ds(pl.multiple_of(core * width, width), width)
        piece = rows // (2 * nz)
        self.here = cut((x * nz + z) * piece, piece) if sliced else pl.ds(0, rows)
        self.each_peer = nz + 2 if sliced else 2

    def copies(self, stage, t):
        r, m, M, core, x, z, nz = self.place
        base = self.base + (t - 1) * self.each_peer
        if stage == 0:
            source = self.source.at[self.here, self.mine]
            target = self.parts.at[m, self.here, self.mine]
            return [remote(source, target, self.sems, base, (r, lax.rem(m + t, M)))]
        part = self.parts.at[lax.rem(m + M - t, M)]
        if stage == 1:
            block = part.at[self.here, self.mine]
            rows = [lax.rem(z + u, nz) * 4 + x * 2 + core for u in range(1, nz)]
        elif stage == 2:
            block = part.at[cut(x * (self.rows // 2), self.rows // 2), self.mine]
            rows = [z * 4 + (1 - x) * 2 + core]
        else:
            block = part.at[:, self.mine]
            rows = [z * 4 + x * 2 + 1 - core]
        first = base + ((0, 1, nz, nz + 1)[stage] if self.sliced else 1)
        return [
            remote(block, block, self.sems, first + i, (row, m)) for i, row in enumerate(rows)
        ]

    def stages(self):
        return (0, 1, 2, 3) if self.sliced else (0, 3)

    def each(self, stage):
        return [c for t in range(1, self.place[2]) for c in self.copies(stage, t)]

    def send(self, stage):
        before = [i for i in self.stages() if i < stage]
        if before:
            self.arrive(before[-1])
        for c in self.each(stage):
            c.start()

    def arrive(self, stage):
        for c in self.each(stage):
            c.wait_recv()

    def drain(self):
        for stage in self.stages():
            for c in self.each(stage):
                c.wait_send()


PLAIN, OWN, OTHERS = 0, 1, 2
SUMS = ("up", "down", "up2", "down2", "out", "query", "key", "value", "tail")
ROLES = (OWN, OWN, OTHERS, OTHERS, PLAIN, PLAIN, PLAIN, PLAIN, PLAIN)
FLAT = (1, 4, 5)
ORDERS = (FLAT, FLAT, FLAT, FLAT, (0, 1, 2), (0, 1, 2), (0, 1, 2), (0, 1, 2), (0, 3))


def sharing(i, rows, M, nz):
    if rows % (16 * 2 * nz * M) == 0 or (i == len(SUMS) - 1 and rows % (8 * 2 * nz * M) == 0):
        return ORDERS[i]
    return tuple(axis for axis in ORDERS[i] if axis != 0)


def kernel(static, names, *refs):
    ref = SimpleNamespace(**dict(zip(names, refs)))
    R, M, rows, D, F, S, near = static
    nz = R // 4
    G = rows // S
    W = 3 * G
    head = D // HEADS
    factor = 1.0 / math.sqrt(head)
    r, y = lax.axis_index("rows"), lax.axis_index("mlp")
    core, xi, z = lax.rem(r, 2), lax.rem(r // 2, 2), r // 4
    me = r * M + y
    devices = R * M
    pairs = M == 2
    up_row, down_row = lax.rem(r + 1, R), lax.rem(r + R - 1, R)
    after, before = lax.rem(me + 1, devices), lax.rem(me + devices - 1, devices)

    local = []
    lsem = ref.lsem
    for i, (src, dst) in enumerate(
        (
            (ref.x, ref.xb.at[1]),
            (ref.wq, ref.wqkv.at[:, 0:D]),
            (ref.wkv, ref.wqkv.at[:, D : 3 * D]),
            (ref.cot, ref.cotn),
            (ref.wo, ref.wob),
            (ref.wup, ref.wupb.at[y]),
            (ref.wdn, ref.wdnb.at[y]),
        )
    ):
        c = pltpu.make_async_copy(src, dst, lsem.at[i])
        c.start()
        local.append(c)

    barrier = pltpu.get_barrier_semaphore()
    others = [(r, lax.rem(y + t, M)) for t in range(1, M)]
    others.append((z * 4 + xi * 2 + 1 - core, y))
    for t in range(1, 2 * nz):
        to = lax.rem(xi * nz + z + t, 2 * nz)
        others.append((lax.rem(to, nz) * 4 + to // nz * 2 + core, y))
    if pairs:
        others += [(up_row, y), (down_row, y)]
    else:
        others += [(after // M, lax.rem(after, M)), (before // M, lax.rem(before, M))]
    for device in others:
        pl.semaphore_signal(barrier, inc=1, device_id=device, device_id_type=MESH)
    pl.semaphore_wait(barrier, len(others))

    def halo(source, at, sems):
        def first(k):
            if pairs:
                return [remote(source(k), at(2 * y, k), sems, (0, k), (r, 1 - y))]
            return [
                remote(source(k), at(0, k), sems, (0, k), (after // M, lax.rem(after, M))),
                remote(source(k), at(2, k), sems, (1, k), (before // M, lax.rem(before, M))),
            ]

        def second(k):
            if pairs:
                to = jnp.where(y == 0, up_row, down_row)
                return remote(at(2 * (1 - y), k), at(2 * y, k), sems, (1, k), (to, y))
            return first(k)[1]

        def send(k):
            for c in first(k):
                c.start()

        def pass_on(k):
            first(k)[0].wait_recv()
            if pairs:
                second(k).start()

        def arrive(k):
            second(k).wait_recv()

        def drain(k):
            first(k)[0].wait_send()
            second(k).wait_send()

        return send, pass_on, arrive, drain

    near_slot = 2 * (1 - y) if pairs else 0
    far_slot = 2 * y if pairs else 2
    xb = ref.xb
    quarter = rows // 4

    def part(k, n=quarter):
        return cut(k * n, n)

    x_send, x_pass, x_arrive, x_drain = halo(
        lambda k: ref.x.at[part(k)], lambda slot, k: xb.at[slot, part(k)], ref.xsem
    )
    loop(4, x_send)
    place_of = (r, y, M, core, xi, z, nz)
    spread = [
        Spread(source, parts, ref.spsem, i * (M - 1) * (nz + 2), place_of, i == 0)
        for i, (source, parts) in enumerate(((ref.wup, ref.wupb), (ref.wdn, ref.wdnb)))
    ]
    for part_of in spread:
        part_of.send(0)
    upb = ref.upb
    upb[y] = jnp.broadcast_to(ref.bup[...].astype(F32).reshape(1, F), (8, F))

    def bias_copy(t):
        return remote(upb.at[y], upb.at[y], ref.ubsem, t - 1, (r, lax.rem(y + t, M)))

    for t in range(1, M):
        bias_copy(t).start()

    def build(k):
        at = part(k)
        a, b = iota((quarter, rows), 0) + k * quarter, iota((quarter, rows), 1)
        ref.pm[at, :] = jnp.where(b == lax.rem(a, G) * S + a // G, 1.0, 0.0).astype(BF)
        ref.pt[at, :] = jnp.where(a == lax.rem(b, G) * S + b // G, 1.0, 0.0).astype(BF)

    loop(4, build)
    a, b = iota((quarter, quarter), 0), iota((quarter, quarter), 1)
    few = quarter // S
    ref.pq[...] = jnp.where(b == lax.rem(a, few) * S + a // few, 1.0, 0.0).astype(BF)
    pm, pt = ref.pm, ref.pt

    nodes = devices * G
    place = ref.nbr[...] // S - me * G + G
    place = jnp.where(place < 0, place + nodes, place)
    place = jnp.where(place >= nodes, place - nodes, place)
    place = place.astype(F32).astype(BF)
    lws = ref.lws
    lws[rows : rows + G, :] = jnp.zeros((G, near), F32)
    lws[0:rows, :] = dot(pm[...], place, NT)
    lwt = ref.lwt
    eye = jnp.where(iota((near, near), 0) == iota((near, near), 1), 1.0, 0.0).astype(BF)

    def turn(s):
        block = lws[pl.ds(pl.multiple_of(s * G, G), 2 * G), :].astype(BF)
        lwt[1, s] = dot(eye, block, NT).astype(BF)

    loop(S, turn)
    l_send, l_pass, l_arrive, l_drain = halo(
        lambda k: lwt.at[1], lambda slot, k: lwt.at[slot], ref.lwsem
    )
    l_send(0)

    modulation = dot(ref.nc[...], ref.adaw[...]) + ref.adab[...].astype(F32).reshape(1, 4 * D)
    ref.mod[...] = modulation
    mods = ref.mods
    for s in range(S):
        mods[s : s + 1, :] = ref.mod[pl.ds(ref.sid[s], 1), :]

    n1w, qkv = ref.n1w, ref.qkv
    wqkv = ref.wqkv

    turn16 = quarter // S

    def norm_block(slot, k):
        at = part(k)
        normed, _ = layer_norm(xb[slot, at, :].astype(F32))
        scaled = normed.reshape(turn16, S, D) * (1.0 + mods[:, 0:D])[None]
        scaled = scaled + mods[:, D : 2 * D][None]
        ordered = dot(ref.pq[...], scaled.reshape(quarter, D).astype(BF)).astype(BF)
        wide = dot(ordered, wqkv[...]).astype(BF).reshape(S, turn16, 3 * D)
        here = cut(slot * G + k * turn16, turn16)
        qkv[:, here, :] = wide
        n1w[:, here, :] = ordered.reshape(S, turn16, D)

    local[0].wait()
    local[1].wait()
    local[2].wait()

    loop(4, lambda k: norm_block(1, k))
    local[3].wait()
    xs, cotb = ref.xs, ref.cotb

    def order(k):
        xs[part(k), :] = dot(pm[part(k), :], xb[1]).astype(BF)
        cotb[part(k), :] = dot(pm[part(k), :], ref.cotn[...]).astype(BF)

    loop(4, order)

    cnt, cntt = ref.cnt, ref.cntt

    def count(s):
        block = lwt[1, s].astype(F32)
        block = jnp.where(iota((near, 2 * G), 1) < G, block, pltpu.roll(block, G, 1))
        key = iota((W, 2 * G), 0).astype(F32)
        total = jnp.zeros((W, 2 * G), F32)
        for j in range(near):
            total = total + jnp.where(block[j : j + 1, :] == key, 1.0, 0.0)
        cnt[s] = total

    loop(S, count)

    def near_norm(k):
        x_pass(k)
        norm_block(near_slot, k)

    loop(4, near_norm)


    def far_norm(k):
        x_arrive(k)
        norm_block(far_slot, k)

        @pl.when(k == 1)
        def _():
            spread[0].send(1)

    loop(4, far_norm)

    mixs, mixx, prob, stw = ref.mixs, ref.mixx, ref.prob, ref.stw
    ntb, mid = ref.ntb, ref.mid
    pair = 2 * head

    def apart(block):
        nothing = jnp.zeros((block.shape[0], head), block.dtype)
        left = jnp.concatenate([block[:, 0:head], nothing], axis=1)
        right = jnp.concatenate([nothing, block[:, head:pair]], axis=1)
        return jnp.concatenate([left, right], axis=0)

    def attend(k):
        for s2 in range(2):
            s = 2 * k + s2
            at = cut(s * G, G)
            times = cnt[s]
            logs = []
            for p in range(PAIRS):
                lo, hi = p * pair, (p + 1) * pair
                queries = apart(qkv[s, G : 2 * G, lo:hi])
                scores = dot(qkv[s, :, D + lo : D + hi], queries, NT) * factor
                scores = jnp.where(times > 0.0, scores, MASKED)
                top = jnp.max(scores, axis=0, keepdims=True)
                power = jnp.exp(scores - top)
                total = jnp.sum(power * times, axis=0, keepdims=True)
                probs = power * (1.0 / total)
                prob[s * PAIRS + p] = probs
                weight = (times * probs.astype(BF).astype(F32)).astype(BF)
                rest = (times * probs - weight.astype(F32)).astype(BF)
                both = jnp.concatenate([weight, rest], axis=1)
                mixed = dot(both, qkv[s, :, 2 * D + lo : 2 * D + hi], TN)
                one, two = mixed[0:G, 0:head], mixed[G : 2 * G, head:pair]
                mixs[at, lo : lo + head] = one.astype(BF)
                mixs[at, lo + head : hi] = two.astype(BF)
                mixx[at, lo : lo + head] = one + mixed[2 * G : 3 * G, 0:head]
                mixx[at, lo + head : hi] = two + mixed[3 * G : 4 * G, head:pair]
                logs.append(top + jnp.log(total))
            logs.append(jnp.zeros((8 - PAIRS, 2 * G), F32))
            stw[1, s] = jnp.concatenate(logs, axis=0)

    loop(4, attend)

    local[4].wait()
    wo = ref.wob
    half = rows // 2
    group = half // G

    def mix_out(c):
        at = part(c, half)
        middle = xs[at, :].astype(F32) + dot(mixs[at, :], wo[...])
        mid[at, :] = middle
        normed, _ = layer_norm(middle)
        for i in range(group):
            lo = i * G
            scale = mods[pl.ds(c * group + i, 1), 2 * D : 3 * D]
            shift = mods[pl.ds(c * group + i, 1), 3 * D : 4 * D]
            here = cut(c * half + lo, G)
            ntb[here, :] = (normed[lo : lo + G] * (1.0 + scale) + shift).astype(BF)

    loop(2, mix_out)

    local[5].wait()
    local[6].wait()
    spread[0].send(2)
    wup, wdn, actb, ghb = ref.wupb, ref.wdnb, ref.actb, ref.ghb
    bupg, g2o = ref.bupg, ref.g2o
    bupg[...] = jnp.zeros_like(bupg)
    g2o[...] = jnp.zeros_like(g2o)
    tile = 256

    def feed(p):
        def column(f):
            cols = part(f, tile)
            hidden = dot(ntb[...], wup[p, :, cols]) + upb[p, 0:1, cols]
            gate = jax.nn.sigmoid(hidden)
            active = hidden * gate
            actb[p, :, cols] = active.astype(BF)
            grad = dot(cotb[...], wdn[p, cols, :], NT)
            grad = (grad * (gate + active * (1.0 - gate))).astype(BF)
            ghb[p, :, cols] = grad
            bupg[p, 0:1, cols] += jnp.sum(grad.astype(F32), axis=0, keepdims=True)

        loop(F // tile, column)
        for q in range(D // tile):
            lo, hi = q * tile, (q + 1) * tile
            g2o[:, lo:hi] += dot(ghb[p], wup[p, lo:hi, :], NT)

    feed(y)

    base = 0
    sums = SimpleNamespace()
    written = []

    def write(source, result):
        c = pltpu.make_async_copy(source, result, ref.wsem.at[len(written)])
        c.start()
        written.append(c)

    for i, (name, bufs) in enumerate(zip(SUMS, ref.sums)):
        out, *bufs = bufs
        dtype = F32 if i == len(SUMS) - 1 else BF
        order = sharing(i, bufs[0].shape[0], M, nz)
        total = Sum(out, dtype, bufs, ref.sumsem, base, place_of, order, ROLES[i])
        base += Sum.slots(order, ROLES[i], nz, M)
        setattr(sums, name, total)
    sums.up.mate, sums.down.mate, sums.up2.mate, sums.down2.mate = (
        sums.up2,
        sums.down2,
        sums.up,
        sums.down,
    )

    def weight_grad(total, left, right):
        width = total.width
        for out, start, kind in (
            (total.cs, (1 - core) * width, BF),
            (total.part, core * width, F32),
        ):
            at = cut(start, width)
            out[...] = dot(left, right(at), TN).astype(kind)
            if kind == BF:
                total.core_send()

    def ffn_grad(total, count, which, rows_of, left, right):
        width = total.width
        many, block = min(rows_of, 512), rows_of // (2 * nz)
        for out, start, kind in (
            (total.cs, (1 - core) * width, BF),
            (total.part, core * width, F32),
        ):
            at = cut(start, width)

            def tile_row(i):
                u, f = i // (rows_of // many), lax.rem(i, rows_of // many)
                p = which(u)
                value = dot(left(p, part(f, many)), right(p, at), TN).astype(kind)
                if count == 1:
                    out[part(f, many), :] = value
                    return
                for v in range(many // block):
                    row = ((f * (many // block) + v) * count + u) * block
                    here = cut(row, block)
                    out[here, :] = value[v * block : (v + 1) * block]

            loop(count * rows_of // many, tile_row)
            if kind == BF:
                total.core_send()

    def up_grad(total, count, which):
        ffn_grad(total, count, which, D, lambda p, f: ntb[:, f], lambda p, at: ghb[p, :, at])

    def down_grad(total, count, which):
        ffn_grad(total, count, which, F, lambda p, f: actb[p, :, f], lambda p, at: cotb[:, at])

    up_grad(sums.up, 1, lambda u: y)
    down_grad(sums.down, 1, lambda u: y)
    sums.up.step()
    sums.down.step()
    l_pass(0)

    def feed_other(t):
        @pl.when(t == 0)
        def _():
            spread[0].send(3)
            spread[1].send(3)
            spread[0].arrive(3)
            spread[1].arrive(3)
            for u in range(1, M):
                bias_copy(u).wait_recv()

        feed(lax.rem(y + t + 1, M))

    loop(M - 1, feed_other)

    gmid, gmw, gatt, gmod = ref.gmid, ref.gmw, ref.cotn, ref.gmod
    row, lane = iota((8, D), 0), iota((8, D), 1) // head
    pick_one = jnp.where((row >= PAIRS) & (lane == 2 * (row - PAIRS)), 1.0, 0.0)
    pick_two = jnp.where((row >= PAIRS) & (lane == 2 * (row - PAIRS) + 1), 1.0, 0.0)
    m_send, m_pass, m_arrive, m_drain = halo(
        lambda k: gmw.at[pl.ds(2 * k, 2), pl.ds(G, G)],
        lambda slot, k: gmw.at[pl.ds(2 * k, 2), cut(slot * G, G)],
        ref.gmsem,
    )
    s_send, s_pass, s_arrive, s_drain = halo(
        lambda k: stw.at[1, pl.ds(2 * k, 2)],
        lambda slot, k: stw.at[slot, pl.ds(2 * k, 2)],
        ref.stsem,
    )

    def middle_back(c):
        at = part(c, half)
        grad = g2o[at, :]
        normed, inverse = layer_norm(mid[at, :])
        weighted = []
        for i in range(group):
            s = c * group + i
            lo, hi = i * G, (i + 1) * G
            scale = mods[pl.ds(s, 1), 2 * D : 3 * D]
            weighted.append(grad[lo:hi] * (1.0 + scale))
            gmod[pl.ds(s, 1), 2 * D : 3 * D] = jnp.sum(
                grad[lo:hi] * normed[lo:hi], axis=0, keepdims=True
            )
            gmod[pl.ds(s, 1), 3 * D : 4 * D] = jnp.sum(grad[lo:hi], axis=0, keepdims=True)
        weighted = jnp.concatenate(weighted, axis=0)
        middle = cotb[at, :].astype(F32) + norm_back(weighted, normed, inverse)
        gmid[at, :] = middle
        rounded = middle.astype(BF)
        gatt[at, :] = rounded
        mixture = dot(rounded, wo[...], NT).astype(BF)
        gmw[pl.ds(c * group, group), G : 2 * G, :] = mixture.reshape(group, G, D)
        product = mixture.astype(F32) * mixx[at, :]
        ones = dot(pick_one, product, NT, PRECISE)
        twos = dot(pick_two, product, NT, PRECISE)
        first_lanes = iota((8, 2 * G), 1) < G
        for g in range(group // 2):
            lo, hi = g * 2 * G, (g + 1) * 2 * G
            one, two = ones[:, lo:hi], twos[:, lo:hi]
            s = c * group + 2 * g
            stw[1, s] += jnp.where(first_lanes, one, pltpu.roll(two, G, 1))
            stw[1, s + 1] += jnp.where(first_lanes, pltpu.roll(one, G, 1), two)
        for k in range(2):
            m_send(2 * c + k)
            s_send(2 * c + k)

    def pass_on(k):
        m_pass(k)
        s_pass(k)

    def other_part(u):
        return lax.rem(y + u + 1, M)

    gqkv, gkvw = ref.gqkv, ref.gkvw

    def query_back(s):
        at = cut(s * G, G)
        times = cnt[s]
        for p in range(PAIRS):
            lo, hi = p * pair, (p + 1) * pair
            grads = apart(gmw[s, G : 2 * G, lo:hi])
            gprob = dot(qkv[s, :, 2 * D + lo : 2 * D + hi], grads, NT)
            gscore = prob[s * PAIRS + p] * (gprob - stw[1, s, PAIRS + p : PAIRS + p + 1, :])
            weight = (times * gscore.astype(BF).astype(F32)).astype(BF)
            gquery = dot(weight, qkv[s, :, D + lo : D + hi], TN) * factor
            gqkv[at, lo : lo + head] = gquery[0:G, 0:head].astype(BF)
            gqkv[at, lo + head : hi] = gquery[G : 2 * G, head:pair].astype(BF)
            queries = apart(qkv[s, G : 2 * G, lo:hi])
            gkvw[s, :, lo:hi] = (dot(weight, queries) * factor).astype(BF)
            weight = (times * prob[s * PAIRS + p].astype(BF).astype(F32)).astype(BF)
            gkvw[s, :, D + lo : D + hi] = dot(weight, grads).astype(BF)


    def count_back(s):
        shift = [2 * G, G, 0]
        block = jnp.concatenate(
            [lwt[b, s][:, 0:G].astype(F32) - float(shift[b]) for b in range(3)], axis=1
        ).astype(jnp.int32)
        key = iota((G, W), 0)
        total = jnp.zeros((G, W), F32)
        for j in range(near):
            total = total + jnp.where(block[j : j + 1, :] == key, 1.0, 0.0)
        cntt[s] = total

    def finish_out(k):
        at = part(k)
        value = mid[at, :] + ref.bdn[...].astype(F32).reshape(1, D)
        for p in range(M):
            value = value + dot(actb[p, at, :], wdn[p])
        ref.n1n[at, :] = value.astype(BF)


    def key_back(s):
        at = cut(s * G, G)
        times = cntt[s]
        stats = [
            jnp.concatenate([stw[b, s][:, i * G : (i + 1) * G] for b in range(3)], axis=1)
            for i in range(2)
        ]
        for p in range(PAIRS):
            lo, hi = p * pair, (p + 1) * pair
            queries, grads = qkv[s, :, lo:hi], gmw[s, :, lo:hi]
            scores = dot(apart(qkv[s, G : 2 * G, D + lo : D + hi]), queries, NT) * factor
            gprob = dot(apart(qkv[s, G : 2 * G, 2 * D + lo : 2 * D + hi]), grads, NT)
            gscores, weights = [], []
            for i in range(2):
                rows_of = slice(i * G, (i + 1) * G)
                log, delta = stats[i][p : p + 1], stats[i][PAIRS + p : PAIRS + p + 1]
                probs = jnp.exp(jnp.where(times > 0.0, scores[rows_of] - log, MASKED))
                gscore = probs * (gprob[rows_of] - delta)
                gscores.append((times * gscore.astype(BF).astype(F32)).astype(BF))
                weights.append((times * probs.astype(BF).astype(F32)).astype(BF))
            gkey = dot(jnp.concatenate(gscores, axis=0), queries) * factor
            gvalue = dot(jnp.concatenate(weights, axis=0), grads)
            for i in range(2):
                cols = pl.ds(D + lo + i * head, head)
                gqkv[at, cols] = gkey[i * G : (i + 1) * G, i * head : (i + 1) * head].astype(BF)
                cols = pl.ds(2 * D + lo + i * head, head)
                gqkv[at, cols] = gvalue[i * G : (i + 1) * G, i * head : (i + 1) * head].astype(BF)


    gdbs = ref.gdbs
    out_rows = ref.outr

    def first_back(c):
        at = part(c, half)
        grad = dot(gqkv[at, :], wqkv[...], NT)
        normed, inverse = layer_norm(xs[at, :].astype(F32))
        weighted = []
        for i in range(group):
            s = c * group + i
            lo, hi = i * G, (i + 1) * G
            here = cut(s * G, G)
            gmod[pl.ds(s, 1), 0:D] = jnp.sum(grad[lo:hi] * normed[lo:hi], axis=0, keepdims=True)
            gmod[pl.ds(s, 1), D : 2 * D] = jnp.sum(grad[lo:hi], axis=0, keepdims=True)
            gdbs[pl.ds(s, 1), :] = jnp.sum(cotb[here, :].astype(F32), axis=0, keepdims=True)
            weighted.append(grad[lo:hi] * (1.0 + mods[pl.ds(s, 1), 0:D]))
        weighted = jnp.concatenate(weighted, axis=0)
        g2o[at, :] = gmid[at, :] + norm_back(weighted, normed, inverse)

    tail = ref.tail
    base = 4 * D // tile * S
    base_up = base + D // tile * S

    def pack_tail():
        tail[...] = jnp.zeros_like(tail)
        for c in range(4 * D // tile):
            tail[c * S : (c + 1) * S, :] = gmod[:, c * tile : (c + 1) * tile]
        for c in range(D // tile):
            tail[base + c * S : base + (c + 1) * S, :] = gdbs[:, c * tile : (c + 1) * tile]
        for c in range(F // tile):
            for p in range(M):
                row = base_up + p * (F // tile) + c
                tail[row : row + 1, :] = bupg[p, 0:1, c * tile : (c + 1) * tile]
        sums.tail.cs[...] = tail[:, sums.tail.other]
        sums.tail.part[...] = tail[:, sums.tail.mine]
        sums.tail.core_send()

    def rows_back():
        for c in range(D // 128):
            lo, hi = c * 128, (c + 1) * 128
            for s in range(S):
                ref.turn[c, pl.ds(s, G, stride=S), :] = g2o[s * G : (s + 1) * G, lo:hi]
            out_rows[:, lo:hi] = ref.turn[c]
        write(out_rows, ref.o_rows)

    def order_back(k):
        ref.outl[part(k), :] = dot(pt[part(k), :], ref.n1n[...]).astype(BF)


    def drain():
        loop(4, x_drain)
        l_drain(0)
        loop(4, m_drain)
        loop(4, s_drain)
        for part_of in spread:
            part_of.drain()
        for t in range(1, M):
            bias_copy(t).wait_send()
        sums.up2.release()
        sums.down2.release()

    def release():
        for total in (sums.up, sums.down, sums.out, sums.query, sums.key, sums.value, sums.tail):
            total.release()

    def out_grad():
        weight_grad(sums.out, mixs[...], lambda at: gatt[:, at])

    def query_grad():
        weight_grad(sums.query, n1w[:, G : 2 * G, :].reshape(rows, D), lambda at: gqkv[:, at])

    def window_grad(total, shares):
        left = n1w[...].reshape(S * W, D)
        weight_grad(total, left, lambda at: shares[:, :, at].reshape(S * W, at.size))

    def key_grad():
        window_grad(sums.key, gkvw.at[:, :, 0:D])

    def value_grad():
        window_grad(sums.value, gkvw.at[:, :, D : 2 * D])

    def queries_of(k):
        query_back(2 * k)
        query_back(2 * k + 1)

    def keys_of(k):
        m_arrive(k)
        s_arrive(k)
        key_back(2 * k)
        key_back(2 * k + 1)

    def counts():
        l_arrive(0)
        loop(S, count_back)

    def layer_out():
        loop(4, finish_out)

    def layer_order():
        loop(4, order_back)
        write(ref.outl, ref.o_layer)

    sums.up.step()
    up_grad(sums.up2, M - 1, other_part)
    down_grad(sums.down2, M - 1, other_part)
    sums.up2.step()
    middle_back(0)
    sums.up.step()
    sums.down.step()
    sums.down2.step()
    middle_back(1)
    out_grad()
    sums.out.step()
    queries_of(0)
    sums.down.step()
    queries_of(1)
    sums.up2.step()
    queries_of(2)
    queries_of(3)
    pass_on(0)
    pass_on(1)
    query_grad()
    sums.query.step()
    sums.up2.step()
    key_grad()
    sums.key.step()
    pass_on(2)
    sums.down2.step()
    value_grad()
    sums.value.step()
    pass_on(3)
    counts()
    layer_out()
    sums.out.step()
    sums.up2.step()
    keys_of(0)
    sums.down2.step()
    keys_of(1)
    sums.query.step()
    keys_of(2)
    keys_of(3)
    sums.out.step()
    sums.key.step()
    first_back(0)
    sums.query.step()
    sums.down2.step()
    first_back(1)
    pack_tail()
    sums.up.step()
    sums.value.step()
    sums.up.step()
    rows_back()
    layer_order()
    sums.tail.step()
    sums.key.step()
    sums.out.step(2)
    sums.query.step(2)
    sums.value.step()
    sums.key.step(2)
    sums.tail.step()
    sums.down.step(2)
    sums.up.step()
    sums.out.step()
    sums.query.step()
    sums.tail.step()
    sums.value.step(2)
    sums.up.step()
    sums.key.step()
    sums.out.step()
    sums.tail.step()
    sums.query.step()
    sums.down.step()
    sums.value.step()
    sums.up.step()
    sums.key.step()
    sums.out.step()
    sums.value.step()
    sums.tail.step()
    sums.query.step()
    sums.down.step()
    release()
    sums.key.step()
    drain()
    sums.value.step()
    sums.tail.step()
    sums.down.step()
    late = (sums.up, sums.out, sums.query, sums.key, sums.value, sums.tail, sums.down)
    results = (ref.o_up, ref.o_out, ref.o_q, ref.o_k, ref.o_v, ref.o_tail, ref.o_dn)
    for total, result in zip(late, results):
        while total.todo:
            total.step()
        total.arrive()
        write(total.out, result)
    for total in late:
        total.finish()
    for c in written:
        c.wait()


WIDE = ("o_up", "o_dn", "o_out", "o_q", "o_k", "o_v")


def widen(static, names, *refs):
    ref = SimpleNamespace(**dict(zip(names, refs)))
    M, D, F, S = static
    tile = 256
    y = lax.axis_index("mlp")
    sources = (ref.o_up, ref.o_dn, ref.o_out, ref.o_q, ref.o_k, ref.o_v)
    targets = (
        ref.f_up,
        ref.f_dn,
        ref.f_out,
        ref.f_q,
        ref.f_kv.at[:, 0:D],
        ref.f_kv.at[:, D : 2 * D],
    )
    n = len(sources)
    straight = ((ref.o_rows, ref.rows, ref.f_rows), (ref.o_layer, ref.layer, ref.f_layer))
    passing = []
    for i, (source, middle, target) in enumerate(straight):
        load = pltpu.make_async_copy(source, middle, ref.isem.at[n + 1 + i])
        passing.append((load, pltpu.make_async_copy(middle, target, ref.osem.at[n + 1 + i])))
        load.start()
    loads = [
        pltpu.make_async_copy(source, ref.inb[i], ref.isem.at[i])
        for i, source in enumerate(sources)
    ]
    tail_in = pltpu.make_async_copy(ref.o_tail, ref.tail, ref.isem.at[n])
    loads[0].start()
    loads[1].start()
    tail_in.start()
    for load in loads[2:]:
        load.start()
    stores = []

    def store(copy):
        copy.start()
        stores.append(copy)

    for load, out in passing:
        load.wait()
        store(out)

    def convert(i):
        loads[i].wait()
        at_once = 128

        def part(k):
            at = cut(k * at_once, at_once)
            ref.outb[i][at, :] = ref.inb[i][at, :].astype(F32)
            pltpu.make_async_copy(ref.outb[i].at[at], targets[i].at[at], ref.osem.at[i]).start()

        loop(sources[i].shape[0] // at_once, part)
        stores.append(pltpu.make_async_copy(ref.outb[i], targets[i], ref.osem.at[i]))

    convert(0)
    convert(1)
    tail_in.wait()
    tail, gms = ref.tail, ref.gms
    pick = jnp.zeros((S, S), F32)
    for s in range(S):
        hit = (iota((S, S), 1) == s) & (iota((S, S), 0) == ref.sid[s])
        pick = pick + jnp.where(hit, 1.0, 0.0)
    for c in range(4 * D // tile):
        gms[:, c * tile : (c + 1) * tile] = dot(pick, tail[c * S : (c + 1) * S, :], NN, PRECISE)
    total = gms[...]
    ref.ada[...] = dot(ref.nc[...].astype(F32), total, TN, PRECISE)
    store(pltpu.make_async_copy(ref.ada, ref.f_ada, ref.osem.at[n]))
    for i in range(2, n):
        convert(i)
    ref.f_adab[...] = jnp.sum(total, axis=0)
    ref.f_cond[...] = dot(total, ref.adaw[...].astype(F32), NT, PRECISE)
    base = 4 * D // tile * S
    for c in range(D // tile):
        ref.f_downb[c * tile : (c + 1) * tile] = jnp.sum(
            tail[base + c * S : base + (c + 1) * S, :], axis=0
        )
    base += D // tile * S
    for c in range(F // tile):
        row = tail[pl.ds(base + y * (F // tile) + c, 1), :]
        ref.f_upb[c * tile : (c + 1) * tile] = row.reshape(tile)
    for c in stores:
        c.wait()


def shards(
    node_rows,
    noise_cond,
    sample_id,
    neighbours,
    ada_weight,
    ada_bias,
    query_weight,
    keyval_weight,
    out_weight,
    up_weight,
    up_bias,
    down_weight,
    down_bias,
    cotangent,
):
    rows, D = node_rows.shape
    F = up_weight.shape[1]
    S, cond = noise_cond.shape
    near = neighbours.shape[1]
    R, M = lax.axis_size("rows"), lax.axis_size("mlp")
    nz = R // 4
    G = rows // S
    W = 3 * G
    small = 16 * nz if 16 * nz > 88 else 128
    V, H = pltpu.VMEM, pl.ANY
    shape = jax.ShapeDtypeStruct
    arguments = dict(
        x=(node_rows, H),
        nc=(noise_cond, V),
        sid=(sample_id, pltpu.SMEM),
        nbr=(neighbours.T, V),
        adaw=(ada_weight, V),
        adab=(ada_bias, V),
        wq=(query_weight, H),
        wkv=(keyval_weight, H),
        wo=(out_weight, H),
        wup=(up_weight, H),
        bup=(up_bias, V),
        wdn=(down_weight, H),
        bdn=(down_bias, V),
        cot=(cotangent, H),
    )
    outputs = dict(
        o_layer=shape((rows, D), BF),
        o_rows=shape((rows, D), F32),
        o_q=shape((D, D), BF),
        o_k=shape((D, D), BF),
        o_v=shape((D, D), BF),
        o_out=shape((D, D), BF),
        o_up=shape((D, F), BF),
        o_dn=shape((F, D), BF),
        o_tail=shape((small, 256), F32),
    )
    scratch = dict(
        xb=V((3, rows, D), BF),
        cotn=V((rows, D), BF),
        wqkv=V((D, 3 * D), BF),
        wob=V((D, D), BF),
        wupb=V((M, D, F), BF),
        wdnb=V((M, F, D), BF),
        pm=V((rows, rows), BF),
        pt=V((rows, rows), BF),
        lws=V((rows + G, near), F32),
        lwt=V((3, S, near, 2 * G), BF),
        mod=V((S, 4 * D), F32),
        mods=V((S, 4 * D), F32),
        n1n=V((rows, D), BF),
        n1w=V((S, W, D), BF),
        gkvw=V((S, W, 2 * D), BF),
        pq=V((rows // 4, rows // 4), BF),
        xs=V((rows, D), BF),
        qkv=V((S, W, 3 * D), BF),
        cotb=V((rows, D), BF),
        cnt=V((S, W, 2 * G), F32),
        cntt=V((S, G, W), F32),
        mixs=V((rows, D), BF),
        mixx=V((rows, D), F32),
        prob=V((S * PAIRS, W, 2 * G), F32),
        ntb=V((rows, D), BF),
        mid=V((rows, D), F32),
        actb=V((M, rows, F), BF),
        ghb=V((M, rows, F), BF),
        bupg=V((M, 8, F), F32),
        upb=V((M, 8, F), F32),
        g2o=V((rows, D), F32),
        gmid=V((rows, D), F32),
        gmw=V((S, W, D), BF),
        stw=V((3, S, 8, 2 * G), F32),
        gmod=V((S, 4 * D), F32),
        gqkv=V((rows, 3 * D), BF),
        gdbs=V((S, D), F32),
        turn=V((D // 128, rows, 128), F32),
        tail=V((small, 256), F32),
        outr=V((rows, D), F32),
        outl=V((rows, D), BF),
    )
    sums = []
    wide = ((D, F), (F, D), (D, F), (F, D), *[(D, D)] * 4, (small, 256))
    count = 0
    for i, (n, c) in enumerate(wide):
        dtype = F32 if i == len(SUMS) - 1 else BF
        times = M - 1 if ROLES[i] == OTHERS else 1
        stage = (n * times, c // 2)
        count += Sum.slots(sharing(i, n * times, M, nz), ROLES[i], nz, M)
        out = V((8, 128) if ROLES[i] == OTHERS else (n, c), dtype)
        bufs = [out, V(stage, F32)] + [V(stage, dtype)] * 3
        if ROLES[i] == OWN:
            bufs.append(V((M - 1, n // (2 * nz), c // 2), dtype))
        elif ROLES[i] == PLAIN and 0 not in sharing(i, n, M, nz):
            bufs.append(V((M, n // (2 * nz), c // 2), dtype))
        sums.append(tuple(bufs))
    scratch.update(sums=tuple(sums))
    sem = pltpu.SemaphoreType.DMA
    for name, dims in dict(
        xsem=(2, 4),
        spsem=(2 * (M - 1) * (nz + 2),),
        ubsem=(M - 1,),
        lwsem=(2, 1),
        gmsem=(2, 4),
        stsem=(2, 4),
        sumsem=(count,),
    ).items():
        scratch[name] = (sem(dims), sem(dims))
    scratch.update(lsem=sem((7,)), wsem=sem((len(outputs),)))
    names = [*arguments, *outputs, *scratch]
    results = pl.pallas_call(
        functools.partial(kernel, (R, M, rows, D, F, S, near), names),
        out_shape=[*outputs.values()],
        in_specs=[pl.BlockSpec(memory_space=m) for _, m in arguments.values()],
        out_specs=[pl.BlockSpec(memory_space=H) for _ in outputs],
        scratch_shapes=[*scratch.values()],
        name="layer",
        compiler_params=pltpu.CompilerParams(
            collective_id=0, has_side_effects=True, vmem_limit_bytes=63 * 2**20
        ),
    )(*[a for a, _ in arguments.values()])
    got = dict(zip(outputs, results))
    inputs = dict(
        nc=(noise_cond, V),
        sid=(sample_id, pltpu.SMEM),
        adaw=(ada_weight, V),
        **{name: (value, H) for name, value in got.items()},
    )
    finals = dict(
        f_layer=shape((rows, D), BF),
        f_rows=shape((rows, D), F32),
        f_cond=shape((S, cond), F32),
        f_ada=shape((cond, 4 * D), F32),
        f_adab=shape((4 * D,), F32),
        f_q=shape((D, D), F32),
        f_kv=shape((D, 2 * D), F32),
        f_out=shape((D, D), F32),
        f_up=shape((D, F), F32),
        f_upb=shape((F,), F32),
        f_dn=shape((F, D), F32),
        f_downb=shape((D,), F32),
    )
    small_ones = ("f_cond", "f_adab", "f_upb", "f_downb")
    room = dict(
        inb=tuple(V(got[name].shape, BF) for name in WIDE),
        outb=tuple(V(got[name].shape, F32) for name in WIDE),
        tail=V((small, 256), F32),
        ada=V((cond, 4 * D), F32),
        layer=V((rows, D), BF),
        rows=V((rows, D), F32),
        gms=V((S, 4 * D), F32),
        isem=sem((len(WIDE) + 3,)),
        osem=sem((len(WIDE) + 3,)),
    )
    return pl.pallas_call(
        functools.partial(widen, (M, D, F, S), [*inputs, *finals, *room]),
        out_shape=[*finals.values()],
        in_specs=[pl.BlockSpec(memory_space=m) for _, m in inputs.values()],
        out_specs=[
            pl.BlockSpec(memory_space=V if name in small_ones else H) for name in finals
        ],
        scratch_shapes=[*room.values()],
        name="widen",
        compiler_params=pltpu.CompilerParams(vmem_limit_bytes=62 * 2**20),
    )(*[a for a, _ in inputs.values()])


def solution(mesh):
    both = P(("rows", "mlp"), None)
    placed = (
        both,
        P(),
        P(("rows", "mlp")),
        both,
        P(),
        P(),
        P(),
        P(),
        P(),
        P(None, "mlp"),
        P("mlp"),
        P("mlp", None),
        P(),
        both,
    )
    return jax.shard_map(
        shards,
        mesh=mesh,
        in_specs=placed,
        out_specs=(
            both,
            both,
            P(),
            P(),
            P(),
            P(),
            P(),
            P(),
            P(None, "mlp"),
            P("mlp"),
            P("mlp", None),
            P(),
        ),
        check_vma=False,
    )
```
